32 devices in a mesh: dp: 8 (over y, x, core), tensor: 4 (over z).
Axes of the slice: x: 2, y: 2, z: 4, core: 2. Of those that a mesh axis runs over, the one named last changes fastest.
Arguments:
- tokens: bfloat16 [16384, 1024], P(('dp', 'tensor')), may hold values from -6 to 6
- cotangent: bfloat16 [16384, 1024], P(('dp', 'tensor')), may hold values from -6 to 6
- lengths: int32 [8, 3], P('dp'), may hold values from 1 to 1024, 1920 in all within a row
- token_order: int32 [16384], P(('dp', 'tensor')), may hold values from 0 to 16383, as said below
- token_return: int32 [16384], P(('dp', 'tensor')), may hold values from 0 to 16383, as said below
- w_mix: float32 [1024, 8, 768], P('dp', 'tensor'), may hold values from -0.1875 to 0.1875
- w_ba: float32 [1024, 8, 2], P('dp', 'tensor'), may hold values from -0.1875 to 0.1875
- conv_w: float32 [512, 8, 4], P('dp', 'tensor'), may hold values from -3 to 3
- w_out: float32 [1024, 8, 256], P('dp', 'tensor'), may hold values from -0.1875 to 0.1875
- w_gate_up: float32 [1024, 2, 2816], P('dp', None, 'tensor'), may hold values from -0.1875 to 0.1875
- w_down: float32 [1024, 2816], P('dp', 'tensor'), may hold values from -0.15625 to 0.15625
- gain_attn: float32 [1024], replicated, may hold values from 0.25 to 1.75
- gain_ffn: float32 [1024], replicated, may hold values from 0.25 to 1.75
- gain_out: float32 [256], replicated, may hold values from 0.25 to 1.75
- decay_log: float32 [8], replicated, may hold values from -8 to -3.5
- decay_bias: float32 [8], replicated, may hold values from -1 to 1
Outputs:
- layer_out: bfloat16 [16384, 1024], P(('dp', 'tensor'))
- input_grad: bfloat16 [16384, 1024], P(('dp', 'tensor'))
- grad_w_mix: float32 [1024, 8, 768], P('dp', 'tensor')
- grad_w_ba: float32 [1024, 8, 2], P('dp', 'tensor')
- grad_conv_w: float32 [512, 8, 4], P('dp', 'tensor')
- grad_w_out: float32 [1024, 8, 256], P('dp', 'tensor')
- grad_w_gate_up: float32 [1024, 2, 2816], P('dp', None, 'tensor')
- grad_w_down: float32 [1024, 2816], P('dp', 'tensor')
- grad_gain_attn: float32 [1024], replicated
- grad_gain_ffn: float32 [1024], replicated
- grad_gain_out: float32 [256], replicated
- grad_decay_log: float32 [8], replicated
- grad_decay_bias: float32 [8], replicated
The draws below stay inside these ranges and needn't reach their ends.
Inputs may be any that keep to these rules, and one draw needn't show every extreme that they name: `lengths`: each row sums to 1920, and its largest entry is 1024. `token_order`: a permutation. Writing a row as 2048 * g + 512 * s + i with 0 <= i < 512, packed row and given row have the same s, and for every g and g' exactly 64 packed rows of group g' with a given s take given rows of group g. `token_return`: the inverse permutation of token_order.
All inputs are finite; a program needn't handle non-finite values.
Results may differ from the reference program's by a relative error of at most 0.015.
The reference program's roundings to bfloat16 on the way count: a program that leaves them out, or rounds other values in their place, can miss the bound.
Values may be sent and summed in bfloat16 or wider, within the bound.
No kernel may reach another device: no remote copies, remote signals or barrier semaphores. Data moves between devices by JAX's collectives and lax.ppermute only.
A program may use at most 256 MiB of HBM per device.

```python
import math
import jax
import jax.numpy as jnp
import numpy as np
from jax import lax

D = 1024
H = 8
DK = 128
DV = 256
FF = 2816
CONV = 4
SPAN = 64
SEQS = 3
TOK_DEV = 512
GROUP = 2048
GROUPS = 8
TOKENS = 16384
PAD = 128
MAXLEN = 1024
QKVH = 512
PROJH = 768


def token_maps(key):
    groups = TOKENS // GROUP
    splits = GROUP // TOK_DEV
    per_peer = TOK_DEV // groups
    pair_count = splits * groups
    source_keys = jax.random.split(jax.random.fold_in(key, 11), pair_count)
    target_keys = jax.random.split(jax.random.fold_in(key, 12), pair_count)
    source_perm = jax.vmap(lambda subkey: jax.random.permutation(subkey, TOK_DEV))(source_keys).astype(jnp.int32)
    target_perm = jax.vmap(lambda subkey: jax.random.permutation(subkey, TOK_DEV))(target_keys).astype(jnp.int32)
    grid_shape = (splits, groups, groups, per_peer)
    source_perm = source_perm.reshape(grid_shape)
    target_slot = jnp.transpose(target_perm.reshape(grid_shape), (0, 2, 1, 3))
    split_index = lax.broadcasted_iota(jnp.int32, grid_shape, 0)
    source_index = lax.broadcasted_iota(jnp.int32, grid_shape, 1)
    target_index = lax.broadcasted_iota(jnp.int32, grid_shape, 2)
    loader_row = ((source_index * splits + split_index) * TOK_DEV + source_perm).reshape(-1)
    packed_row = ((target_index * splits + split_index) * TOK_DEV + target_slot).reshape(-1)
    forward_map = jnp.zeros((TOKENS,), jnp.int32).at[packed_row].set(loader_row)
    inverse_map = jnp.zeros((TOKENS,), jnp.int32).at[loader_row].set(packed_row)
    return (forward_map, inverse_map)


def draw_token_order(key, part):
    return token_maps(key)[0]


def draw_token_return(key, part):
    return token_maps(key)[1]


def block_scale(own_key, extent, cuts, low, high):
    level, own = 1.0, jax.random.fold_in(own_key, 6)
    for axis_at, blocks in cuts:
        steps = jnp.exp(jax.random.uniform(jax.random.fold_in(own, axis_at), (blocks,), jnp.float32, low / len(cuts), high / len(cuts)))
        level = level * jnp.repeat(steps, extent[axis_at] // blocks).reshape([-1 if axis == axis_at else 1 for axis in range(len(extent))])
    return level


def split_up(count, total, most, skew):
    weights = [(1 << 20) // math.isqrt(standing ** skew) + 1 for standing in range(2, count + 1)]
    spare, holding = total - most - (count - 1), [1] * (count - 1)
    while spare > 0:
        free = [i for i in range(count - 1) if holding[i] < most]
        pool, budget = sum([weights[i] for i in free]), spare
        for i in free:
            more = min(most - holding[i], max(1, budget * weights[i] // pool), spare)
            holding[i] = holding[i] + more
            spare = spare - more
    return np.array([most] + holding)


def uneven_parts(stream_key, number_of, total, bound, skew):
    if number_of == 2:
        one = jax.random.randint(stream_key, (), max(1, total - bound), min(bound, total - 1) + 1)
        return jnp.stack([one, total - one])
    tallies = jnp.asarray(split_up(number_of, total, bound, skew), jnp.int32)
    couples = (number_of - 1) // 2
    giver, sink = tallies[1:1 + 2 * couples:2], tallies[2:2 + 2 * couples:2]
    room = jnp.minimum(giver - 1, bound - sink)
    moved = jax.random.randint(jax.random.fold_in(stream_key, 1), (couples,), 0, 1 << 20) % (room + 1)
    tallies = tallies.at[1:1 + 2 * couples:2].set(giver - moved).at[2:2 + 2 * couples:2].set(sink + moved)
    return tallies[jax.random.permutation(jax.random.fold_in(stream_key, 2), number_of)]


def noise(key, extent, width, limit, cuts=(), held_as=jnp.bfloat16):
    values = width * jax.random.normal(key, extent, jnp.float32)
    if cuts:
        values = values * block_scale(key, extent, cuts, -0.22, 0.18)
    return jnp.clip(values, -limit, limit).astype(held_as)


def setup_inputs(seed: int = 0) -> dict:
    streams_of = jax.random.split(jax.random.key(seed), 17)
    return {
        "tokens": noise(streams_of[0], (TOKENS, D), 1.0, 6.0, ((0, 32),)),
        "cotangent": noise(streams_of[1], (TOKENS, D), 1.0, 6.0, ((0, 32),)),
        "lengths": jax.vmap(lambda own: uneven_parts(own, SEQS, GROUP - PAD, MAXLEN, 2))(jax.random.split(streams_of[2], GROUPS)).reshape((GROUPS, SEQS)).astype(jnp.int32),
        "token_order": draw_token_order(jax.random.fold_in(streams_of[16], 71), 0),
        "token_return": draw_token_return(jax.random.fold_in(streams_of[16], 71), 0),
        "w_mix": noise(streams_of[5], (D, H, PROJH), D ** -0.5, 0.1875, ((0, 8), (1, 4)), jnp.float32),
        "w_ba": noise(streams_of[6], (D, H, 2), D ** -0.5, 0.1875, ((0, 8), (1, 4)), jnp.float32),
        "conv_w": noise(streams_of[7], (QKVH, H, CONV), CONV ** -0.5, 3.0, ((0, 8), (1, 4)), jnp.float32),
        "w_out": noise(streams_of[8], (D, H, DV), (H * DV // 2) ** -0.5, 0.1875, ((0, 8), (1, 4)), jnp.float32),
        "w_gate_up": noise(streams_of[9], (D, 2, FF), D ** -0.5, 0.1875, ((0, 8), (2, 4)), jnp.float32),
        "w_down": noise(streams_of[10], (D, FF), (FF // 2) ** -0.5, 0.15625, ((0, 8), (1, 4)), jnp.float32),
        "gain_attn": jnp.clip(1.0 + 0.15 * jax.random.normal(streams_of[11], (D,), jnp.float32), 0.25, 1.75),
        "gain_ffn": jnp.clip(1.0 + 0.15 * jax.random.normal(streams_of[12], (D,), jnp.float32), 0.25, 1.75),
        "gain_out": jnp.clip(1.0 + 0.15 * jax.random.normal(streams_of[13], (DV,), jnp.float32), 0.25, 1.75),
        "decay_log": jnp.clip(jax.random.uniform(streams_of[14], (H,), jnp.float32, -8.0, -3.5), -8.0, -3.5),
        "decay_bias": jnp.clip(jax.random.uniform(streams_of[15], (H,), jnp.float32, -1.0, 1.0), -1.0, 1.0),
    }


highest_precision = lax.Precision.HIGHEST
epsilon = 1e-06

@jax.custom_vjp
def low(v):
    return lax.optimization_barrier(v.astype(jnp.bfloat16)).astype(jnp.float32)

@jax.custom_vjp
def low_back(v):
    return v

def low_keep(v):
    return (low(v), None)

def low_pass(kept, grad):
    return (grad,)

def back_keep(v):
    return (v, None)

def back_low(kept, grad):
    return (low(grad),)
low.defvjp(low_keep, low_pass)
low_back.defvjp(back_keep, back_low)

def rms_scale(values):
    return lax.rsqrt(lax.optimization_barrier(jnp.mean(values * values, axis=-1, keepdims=True)) + epsilon)

def norm_rows(values, gain):
    return values * rms_scale(values) * gain

def segments(length_row, group_rows):
    seq_ends = jnp.cumsum(length_row).astype(jnp.int32)
    positions = jnp.arange(group_rows, dtype=jnp.int32)
    return lax.optimization_barrier(jnp.sum((positions[:, None] >= seq_ends[None, :]).astype(jnp.int32), axis=1)).astype(jnp.int32)

def short_conv(inputs, weights, segment_ids):
    row_count = inputs.shape[0]
    running = inputs * jnp.transpose(weights[:, :, 0])[None]
    for offset in range(1, weights.shape[2]):
        shifted = jnp.concatenate([jnp.zeros((offset,) + inputs.shape[1:], inputs.dtype), inputs[:row_count - offset]], axis=0)
        earlier = jnp.concatenate([jnp.full((offset,), -1, jnp.int32), segment_ids[:row_count - offset]])
        running = running + jnp.where((earlier == segment_ids)[:, None, None], shifted, 0.0) * jnp.transpose(weights[:, :, offset])[None]
    return running

def mixer_core(projected, small_proj, conv_weights, decay_rate, decay_shift, gain_norm, segment_ids, recurrence):
    conv_width = 2 * DK + DV
    active = jax.nn.silu(short_conv(projected[:, :, :conv_width], conv_weights, segment_ids))
    query_vec = active[:, :, :DK]
    key_vec = active[:, :, DK:2 * DK]
    value_vec = active[:, :, 2 * DK:]
    query_vec = query_vec * lax.rsqrt(lax.optimization_barrier(jnp.sum(query_vec * query_vec, axis=-1, keepdims=True)) + epsilon) * DK ** (-0.5)
    key_vec = key_vec * lax.rsqrt(lax.optimization_barrier(jnp.sum(key_vec * key_vec, axis=-1, keepdims=True)) + epsilon)
    beta_gate = jax.nn.sigmoid(small_proj[:, :, 0])
    log_decay = -jnp.exp(decay_rate)[None, :] * jax.nn.softplus(small_proj[:, :, 1] + decay_shift[None, :])
    result = recurrence(query_vec, key_vec, value_vec, beta_gate, log_decay, segment_ids)
    normed = result * rms_scale(result) * gain_norm
    gated_out = normed * jax.nn.silu(projected[:, :, conv_width:])
    return gated_out * (segment_ids < SEQS).astype(gated_out.dtype)[:, None, None]

def delta_steps(query_vec, key_vec, value_vec, beta_gate, log_decay, segment_ids):
    total_rows = query_vec.shape[0]
    starts = jnp.concatenate([jnp.ones((1,), dtype=bool), segment_ids[1:] != segment_ids[:-1]])
    keep_rate = jnp.where(starts[:, None], 0.0, jnp.exp(log_decay))

    def one_step(recurrent_matrix, pieces):
        single_query_row, single_key_row, value_row, beta_row, keep_row = pieces
        recurrent_matrix = keep_row[:, None, None] * recurrent_matrix
        predicted_values = jnp.einsum('pj,pjn->pn', single_key_row, recurrent_matrix, precision=highest_precision)
        recurrent_matrix = recurrent_matrix + beta_row[:, None, None] * single_key_row[:, :, None] * (value_row - predicted_values)[:, None, :]
        return (recurrent_matrix, jnp.einsum('pj,pjn->pn', single_query_row, recurrent_matrix, precision=highest_precision))

    def one_block(recurrent_matrix, pieces):
        return lax.scan(one_step, recurrent_matrix, pieces)

    def split_rows(array):
        return array.reshape((total_rows // SPAN, SPAN) + array.shape[1:])
    block_items = tuple((split_rows(member) for member in (query_vec, key_vec, value_vec, beta_gate, keep_rate)))
    initial = jnp.zeros((query_vec.shape[1], DK, DV), query_vec.dtype)
    outputs = lax.scan(jax.checkpoint(one_block), initial, block_items)[1]
    return outputs.reshape(total_rows, query_vec.shape[1], DV)

def reference(tokens, cotangent, lengths, token_order, token_return, w_mix, w_ba, conv_w, w_out, w_gate_up, w_down, gain_attn, gain_ffn, gain_out, decay_log, decay_bias):
    segment_all = jax.vmap(lambda length_row: segments(length_row, GROUP))(lengths)
    packed = tokens.astype(jnp.float32)[token_order].reshape(-1, GROUP, D)
    packed_grad = cotangent.astype(jnp.float32)[token_order].reshape(-1, GROUP, D)

    def forward(inputs, mix_w, small_w, conv_wt, out_w, ffn_w, down_w, norm_attn, norm_ffn, norm_out, decay_rate, decay_shift):
        mix_w = low(mix_w)
        small_w = low(small_w)
        conv_wt = low(conv_wt)
        out_w = low(out_w)
        ffn_w = low(ffn_w)
        down_w = low(down_w)

        def group_pass(pair_in):
            rows_in, seg_row = pair_in
            row_mask = (seg_row < SEQS).astype(jnp.float32)[:, None]
            normed_in = low(norm_rows(rows_in, norm_attn))
            projected = low_back(jnp.einsum('td,dhp->thp', normed_in, mix_w, precision=highest_precision))
            small_proj = low_back(jnp.einsum('td,dhc->thc', normed_in, small_w, precision=highest_precision))
            gated_out = low(mixer_core(projected, small_proj, conv_wt, decay_rate, decay_shift, norm_out, seg_row, delta_steps))
            mixed_rows = low_back(jnp.einsum('thv,dhv->td', gated_out, out_w, precision=highest_precision))
            middle = rows_in + mixed_rows
            normed_mid = low(norm_rows(middle, norm_ffn))
            gate_up = low_back(jnp.einsum('td,dcf->tcf', normed_mid, ffn_w, precision=highest_precision))
            hidden = low(jax.nn.silu(gate_up[:, 0]) * gate_up[:, 1] * row_mask)
            return middle + jnp.einsum('tf,df->td', hidden, down_w, precision=highest_precision)
        return lax.map(jax.checkpoint(group_pass), (inputs, segment_all))
    output, pullback = jax.vjp(forward, packed, w_mix, w_ba, conv_w, w_out, w_gate_up, w_down, gain_attn, gain_ffn, gain_out, decay_log, decay_bias)
    grads = pullback(packed_grad)
    layer_out = output.reshape(TOKENS, D)[token_return].astype(jnp.bfloat16)
    input_grad = grads[0].reshape(TOKENS, D)[token_return].astype(jnp.bfloat16)
    return (layer_out, input_grad, grads[1], grads[2], grads[3], grads[4], grads[5], grads[6], grads[7], grads[8], grads[9], grads[10], grads[11])
```

```python
import functools
import jax
import jax.numpy as jnp
from jax import lax
from jax.experimental import pallas as pl
from jax.experimental.pallas import tpu as pltpu
from jax.sharding import Mesh
from jax.sharding import PartitionSpec as P

DK = 128
DV = 256
SEQS = 3
CHUNK = 128
epsilon = 1e-06
f32 = jnp.float32
bf16 = jnp.bfloat16


def dot(a, b, ca=1, cb=0):
    return lax.dot_general(a, b, (((ca,), (cb,)), ((), ())), preferred_element_type=f32)


def halves(x):
    high = x.astype(bf16)
    return high, (x - high.astype(f32)).astype(bf16)


def dot1(a, b, ca=1, cb=0):
    return dot(a.astype(bf16), b.astype(bf16), ca, cb)


def dot3(a, b, ca=1, cb=0):
    ah, al = halves(a)
    bh, bl = halves(b)
    return dot(ah, bh, ca, cb) + (dot(ah, bl, ca, cb) + dot(al, bh, ca, cb))


def dot_exact(a, b, ca=1, cb=0):
    ah = a.astype(bf16)
    bh, bl = halves(b)
    bt = (b - bh.astype(f32) - bl.astype(f32)).astype(bf16)
    return dot(ah, bh, ca, cb) + (dot(ah, bl, ca, cb) + dot(ah, bt, ca, cb))


def sigmoid(x):
    return 1.0 / (1.0 + jnp.exp(-x))


def segment_of(position, ends):
    return sum((position >= e).astype(jnp.int32) for e in ends)


def iota(shape, axis):
    return lax.broadcasted_iota(jnp.int32, shape, axis)


def conv_masks(base, rows, ends, taps, sign):
    t = base + iota((rows, 1), 0)
    own = segment_of(t, ends)
    masks = []
    for j in range(1, taps):
        other = t - sign * j
        same = segment_of(other, ends) == own
        masks.append(jnp.where(same & (other >= 0), 1.0, 0.0))
    return masks


def chunk_terms(base, ends, g_col, g_row, q, k, beta):
    c = CHUNK
    ti = base + iota((c, 1), 0)
    tj = base + iota((1, c), 1)
    si = segment_of(ti, ends)
    sj = segment_of(tj, ends)
    ii = iota((c, c), 0)
    jj = iota((c, c), 1)
    decay = jnp.where((si == sj) & (ii >= jj), jnp.exp(jnp.minimum(g_col - g_row, 0.0)), 0.0)
    before = jnp.where(base > 0, segment_of(base - 1, ends), -1)
    last = segment_of(base + c - 1, ends)
    carry = jnp.where(si == before, jnp.exp(g_col), 0.0)
    g_last = g_col[c - 1 :, :]
    tail = jnp.where(si == last, jnp.exp(jnp.minimum(g_last - g_col, 0.0)), 0.0)
    return decay, carry, tail, ii, jj


def invert(lower, ii, jj, mul):
    first = ((ii ^ jj) == 1) & (ii > jj)
    eye = jnp.where(ii == jj, 1.0, 0.0)
    inv = [eye - jnp.where(first, a, 0.0) for a in lower]
    size = 2
    while size < CHUNK:
        joins = ((ii // (2 * size)) == (jj // (2 * size))) & ((ii & size) != 0) & ((jj & size) == 0)
        half = [mul(jnp.where(joins, a, 0.0), t) for a, t in zip(lower, inv)]
        inv = [t - mul(t, x) for t, x in zip(inv, half)]
        size *= 2
    return inv


def silu_parts(u):
    s = sigmoid(u)
    return u * s, s


def forward_kernel(
    ends_ref, proj_ref, taps_ref, rate_ref, shift_ref, gain_ref,
    gated_ref, o_ref, u_ref, s_ref, t_ref, qe_ref, m_ref,
    xs, state, *, heads, rows, taps,
):
    i = pl.program_id(0)
    wide = 2 * DK + DV
    full = wide + DV
    ends = [ends_ref[k] for k in range(SEQS)]
    base = i * rows
    c = CHUNK

    @pl.when(i == 0)
    def _():
        xs[0:8, :] = jnp.zeros((8, heads * wide), f32)
        state[...] = jnp.zeros_like(state)

    @pl.when(i > 0)
    def _():
        xs[0:8, :] = xs[rows : rows + 8, :]

    for h in range(heads):
        xs[8:, h * wide : (h + 1) * wide] = proj_ref[:, h * full : h * full + wide]
    small = proj_ref[:, heads * full :]
    beta_all = sigmoid(small)
    shifted = small + shift_ref[...]
    ld_all = -jnp.exp(rate_ref[...]) * (jnp.maximum(shifted, 0.0) + jnp.log1p(jnp.exp(-jnp.abs(shifted))))
    masks = conv_masks(base, rows, ends, taps, 1)
    qs, ks, vs = [], [], []
    for h in range(heads):
        sl = slice(h * wide, (h + 1) * wide)
        run = xs[8:, sl] * taps_ref[0:1, sl]
        for j in range(1, taps):
            run = run + (xs[8 - j : 8 - j + rows, sl] * masks[j - 1]) * taps_ref[j : j + 1, sl]
        act = run * sigmoid(run)
        q, k, v = act[:, :DK], act[:, DK : 2 * DK], act[:, 2 * DK :]
        qs.append(q * (lax.rsqrt(jnp.sum(q * q, axis=-1, keepdims=True) + epsilon) * DK ** (-0.5)))
        ks.append(k * lax.rsqrt(jnp.sum(k * k, axis=-1, keepdims=True) + epsilon))
        vs.append(v)
    lower_tri = jnp.where(iota((c, c), 0) >= iota((c, c), 1), 1.0, 0.0)
    n = rows // c
    probs = []
    for b in range(n):
        rs = slice(b * c, (b + 1) * c)
        g_all = dot_exact(lower_tri, ld_all[rs])
        g_t = g_all.T
        for h in range(heads):
            q, k, v = qs[h][rs], ks[h][rs], vs[h][rs]
            beta = beta_all[rs, 2 * h : 2 * h + 1]
            g_col = g_all[:, 2 * h + 1 : 2 * h + 2]
            g_row = g_t[2 * h + 1 : 2 * h + 2, :]
            decay, carry, tail, ii, jj = chunk_terms(base + b * c, ends, g_col, g_row, q, k, beta)
            qkk = DOT_QK(jnp.concatenate([q, k], axis=0), k, 1, 1)
            p = qkk[:c] * decay
            a = jnp.where(ii > jj, qkk[c:] * decay, 0.0) * beta
            probs.append(dict(b=b, h=h, q=q, k=k, v=v, beta=beta, carry=carry, tail=tail, p=p, a=a))
    inv = invert([x["a"] for x in probs], ii, jj, DOT_INV)
    for x, t in zip(probs, inv):
        x["t"] = t
        rhs = jnp.concatenate([(x["beta"] * x["carry"]) * x["k"], x["beta"] * x["v"]], axis=1)
        x["wv"] = DOT_WV(t, rhs)
    for x in probs:
        pwv = DOT_P(x["p"], x["wv"])
        x["qe"] = x["carry"] * x["q"] - pwv[:, :DK]
        x["pv"] = pwv[:, DK:]
        kwv = DOT_K(x["tail"] * x["k"], x["wv"], 0, 0)
        c_last = x["carry"][c - 1 :, :]
        x["m"] = jnp.where(ii == jj, c_last, 0.0) - kwv[:, :DK]
        x["bf"] = kwv[:, DK:]
    for x in probs:
        b, h = x["b"], x["h"]
        s = state[h]
        s_ref[b, h] = s
        t_ref[b, h] = x["t"]
        qe_ref[b, h] = x["qe"]
        m_ref[b, h] = x["m"]
        w = x["wv"][:, :DK]
        state[h] = x["bf"] + DOT_S(x["m"], s)
        wq = DOT_O(jnp.concatenate([w, x["qe"]], axis=0), s)
        u_ref[b * c : (b + 1) * c, h * DV : (h + 1) * DV] = x["wv"][:, DK:] - wq[:c]
        o_ref[b * c : (b + 1) * c, h * DV : (h + 1) * DV] = x["pv"] + wq[c:]
    live = jnp.where(segment_of(base + iota((rows, 1), 0), ends) < SEQS, 1.0, 0.0)
    for h in range(heads):
        o = o_ref[:, h * DV : (h + 1) * DV]
        z = proj_ref[:, h * full + wide : (h + 1) * full]
        r = lax.rsqrt(jnp.mean(o * o, axis=-1, keepdims=True) + epsilon)
        gated_ref[:, h * DV : (h + 1) * DV] = (o * (r * live) * gain_ref[...] * (z * sigmoid(z))).astype(bf16)


def backward_kernel(
    ends_ref, proj_ref, halo_ref, taps_ref, rate_ref, shift_ref, gain_ref,
    dgated_ref, o_ref, u_ref, s_ref, t_ref, qe_ref, m_ref,
    dproj_ref, dtaps_ref, dgain_ref, ddecay_ref,
    xs, ds, dstate, *, heads, rows, taps, blocks,
):
    step = pl.program_id(0)
    i = blocks - 1 - step
    wide = 2 * DK + DV
    full = wide + DV
    ends = [ends_ref[k] for k in range(SEQS)]
    base = i * rows
    c = CHUNK

    @pl.when(step == 0)
    def _():
        ds[...] = jnp.zeros_like(ds)
        dstate[...] = jnp.zeros_like(dstate)
        dtaps_ref[...] = jnp.zeros_like(dtaps_ref)
        dgain_ref[...] = jnp.zeros_like(dgain_ref)
        ddecay_ref[...] = jnp.zeros_like(ddecay_ref)

    @pl.when(step > 0)
    def _():
        ds[rows : rows + 8, :] = ds[0:8, :]

    for h in range(heads):
        xs[0:8, h * wide : (h + 1) * wide] = halo_ref[:, h * full : h * full + wide]
        xs[8:, h * wide : (h + 1) * wide] = proj_ref[:, h * full : h * full + wide]
    small = proj_ref[:, heads * full :]
    beta_all = sigmoid(small)
    shifted = small + shift_ref[...]
    rate = -jnp.exp(rate_ref[...])
    ld_all = rate * (jnp.maximum(shifted, 0.0) + jnp.log1p(jnp.exp(-jnp.abs(shifted))))
    masks = conv_masks(base, rows, ends, taps, 1)
    live = jnp.where(segment_of(base + iota((rows, 1), 0), ends) < SEQS, 1.0, 0.0)
    acts = []
    dos = []
    for h in range(heads):
        sl = slice(h * wide, (h + 1) * wide)
        run = xs[8:, sl] * taps_ref[0:1, sl]
        for j in range(1, taps):
            run = run + (xs[8 - j : 8 - j + rows, sl] * masks[j - 1]) * taps_ref[j : j + 1, sl]
        sg = sigmoid(run)
        act = run * sg
        dact = sg * (1.0 + run * (1.0 - sg))
        q, k, v = act[:, :DK], act[:, DK : 2 * DK], act[:, 2 * DK :]
        rq = lax.rsqrt(jnp.sum(q * q, axis=-1, keepdims=True) + epsilon)
        rk = lax.rsqrt(jnp.sum(k * k, axis=-1, keepdims=True) + epsilon)
        acts.append((q * rq, k * rk, v, dact, rq, rk))
        o = o_ref[:, h * DV : (h + 1) * DV]
        z = proj_ref[:, h * full + wide : (h + 1) * full]
        dg = dgated_ref[:, h * DV : (h + 1) * DV] * live
        r = lax.rsqrt(jnp.mean(o * o, axis=-1, keepdims=True) + epsilon)
        nrm = o * r
        sz = sigmoid(z)
        dz = dg * nrm * gain_ref[...] * (sz * (1.0 + z * (1.0 - sz)))
        dng = dg * (z * sz)
        dgain_ref[...] += jnp.sum((dng * nrm).reshape(rows // 8, 8, DV), axis=0)
        dn = dng * gain_ref[...]
        dos.append(r * (dn - nrm * jnp.mean(dn * nrm, axis=-1, keepdims=True)))
        dproj_ref[:, h * full + wide : (h + 1) * full] = dz.astype(bf16)
    low_i = iota((c, c), 0)
    low_j = iota((c, c), 1)
    lower_tri = jnp.where(low_i >= low_j, 1.0, 0.0)
    upper_tri = jnp.where(low_i <= low_j, 1.0, 0.0)
    strict_low = jnp.where(low_i > low_j, 1.0, 0.0)
    n = rows // c
    probs = []
    for b in reversed(range(n)):
        rs = slice(b * c, (b + 1) * c)
        g_all = dot_exact(lower_tri, ld_all[rs])
        g_t = g_all.T
        for h in range(heads):
            q, k, v = acts[h][0][rs] * DK ** (-0.5), acts[h][1][rs], acts[h][2][rs]
            beta = beta_all[rs, 2 * h : 2 * h + 1]
            g_col = g_all[:, 2 * h + 1 : 2 * h + 2]
            g_row = g_t[2 * h + 1 : 2 * h + 2, :]
            decay, carry, tail, ii, jj = chunk_terms(base + b * c, ends, g_col, g_row, q, k, beta)
            qkk = DOT_QK(jnp.concatenate([q, k], axis=0), k, 1, 1)
            p = qkk[:c] * decay
            dkk = jnp.where(ii > jj, qkk[c:] * decay, 0.0)
            do = dos[h][rs]
            u = u_ref[rs, h * DV : (h + 1) * DV]
            dp = DOT_B(do, u, 1, 1)
            pdo = DOT_B(p, do, 0, 0)
            qdo = DOT_B(qe_ref[b, h], do, 0, 0)
            f = DOT_B(do, s_ref[b, h], 1, 1)
            probs.append(dict(b=b, h=h, q=q, k=k, v=v, beta=beta, carry=carry, tail=tail, decay=decay, p=p, dkk=dkk,
                              do=do, u=u, dp=dp, pdo=pdo, qdo=qdo, f=f))
    for x in probs:
        b, h = x["b"], x["h"]
        dnext = dstate[h]
        x["dnext"] = dnext
        dstate[h] = DOT_S(m_ref[b, h], dnext, 0, 0) + x["qdo"]
    for x in probs:
        du = x["pdo"] + DOT_B(x["tail"] * x["k"], x["dnext"])
        x["dr"] = DOT_B(t_ref[x["b"], x["h"]], du, 0, 0)
        x["j"] = DOT_B(x["u"], x["dnext"], 1, 1)
    dq_all = [[None] * n for _ in range(heads)]
    dk_all = [[None] * n for _ in range(heads)]
    dv_all = [[None] * n for _ in range(heads)]
    dsmall = [[None] * heads for _ in range(n)]
    lane = iota((c, DK), 1)
    for x in probs:
        b, h, q, k, beta, carry = x["b"], x["h"], x["q"], x["k"], x["beta"], x["carry"]
        dr = x["dr"]
        s = s_ref[b, h]
        neg = DOT_B(dr, x["u"], 1, 1)
        hh = DOT_B(dr, s, 1, 1)
        neg = jnp.where(ii > jj, neg, 0.0)
        adk = neg * x["dkk"]
        dbeta = (
            jnp.sum(dr * x["v"], axis=-1, keepdims=True)
            - carry * jnp.sum(k * hh, axis=-1, keepdims=True)
            - jnp.sum(adk, axis=-1, keepdims=True)
        )
        dcarry = jnp.sum(q * x["f"], axis=-1, keepdims=True) - beta * jnp.sum(k * hh, axis=-1, keepdims=True)
        e = x["dp"] * x["p"] - beta * adk
        dqk = x["dp"] * x["decay"]
        dkk = -(neg * beta) * jnp.where(ii > jj, x["decay"], 0.0)
        dtail = x["tail"] * jnp.sum(k * x["j"], axis=-1, keepdims=True)
        dcl = carry[c - 1 :, :] * jnp.sum(x["dnext"] * s, keepdims=True)
        col = carry * dcarry + jnp.where(iota((c, 1), 0) == c - 1, dcl, 0.0)
        straddle = jnp.where(ii > jj, dot_exact(upper_tri, e), 0.0)
        both = dot_exact(upper_tri, jnp.where(lane == 0, col, 0.0)) + dot_exact(
            strict_low, jnp.where(lane == 0, dtail, 0.0)
        )
        dld = jnp.sum(straddle, axis=-1, keepdims=True) + both[:, 0:1]
        dq_all[h][b] = carry * x["f"] + DOT_B(dqk, k)
        dk_all[h][b] = (
            x["tail"] * x["j"] - (carry * beta) * hh + DOT_B(dqk, q, 0, 0) + DOT_B(dkk, k) + DOT_B(dkk, k, 0, 0)
        )
        dv_all[h][b] = beta * dr
        dsmall[b][h] = (dbeta, dld)
    for b in range(n):
        rs = slice(b * c, (b + 1) * c)
        tile = jnp.zeros((c, DK), f32)
        for h in range(heads):
            dbeta, dld = dsmall[b][h]
            tile = jnp.where(lane == 2 * h, dbeta, jnp.where(lane == 2 * h + 1, dld, tile))
        bet = beta_all[rs]
        dshift = rate * tile * sigmoid(shifted[rs])
        even = (lane & 1) == 0
        inside = lane < 2 * heads
        ddecay_ref[0:8, :] += jnp.sum(jnp.where(even, 0.0, tile * ld_all[rs]).reshape(c // 8, 8, DK), axis=0)
        ddecay_ref[8:16, :] += jnp.sum(jnp.where(even, 0.0, dshift).reshape(c // 8, 8, DK), axis=0)
        dproj_ref[rs, heads * full :] = jnp.where(
            inside, jnp.where(even, tile * (bet * (1.0 - bet)), dshift), 0.0
        ).astype(bf16)
    for h in range(heads):
        qn, kn, v, dact, rq, rk = acts[h]
        dq = jnp.concatenate(dq_all[h], axis=0) * DK ** (-0.5)
        dk = jnp.concatenate(dk_all[h], axis=0)
        dq = rq * (dq - qn * jnp.sum(dq * qn, axis=-1, keepdims=True))
        dk = rk * (dk - kn * jnp.sum(dk * kn, axis=-1, keepdims=True))
        dv = jnp.concatenate(dv_all[h], axis=0)
        o = h * wide
        ds[0:rows, o : o + DK] = dq * dact[:, :DK]
        ds[0:rows, o + DK : o + 2 * DK] = dk * dact[:, DK : 2 * DK]
        ds[0:rows, o + 2 * DK : o + wide] = dv * dact[:, 2 * DK :]
    ahead = conv_masks(base, rows, ends, taps, -1)
    for h in range(heads):
        sl = slice(h * wide, (h + 1) * wide)
        own = ds[0:rows, sl]
        total = own * taps_ref[0:1, sl]
        dtaps_ref[0:8, sl] += jnp.sum((own * xs[8:, sl]).reshape(rows // 8, 8, wide), axis=0)
        for j in range(1, taps):
            total = total + (ds[j : j + rows, sl] * ahead[j - 1]) * taps_ref[j : j + 1, sl]
            dtaps_ref[8 * j : 8 * j + 8, sl] += jnp.sum(
                (own * (xs[8 - j : 8 - j + rows, sl] * masks[j - 1])).reshape(rows // 8, 8, wide), axis=0
            )
        dproj_ref[:, h * full : h * full + wide] = total.astype(bf16)


DOT_QK = dot3
DOT_INV = dot3
DOT_WV = dot3
DOT_P = dot3
DOT_K = dot3
DOT_S = dot3
DOT_O = dot3
DOT_B = dot3


def mixer_forward(ends, proj, taps, rate, shift, gain, *, heads, rows):
    total, width = proj.shape
    blocks = total // rows
    n = rows // CHUNK
    row = lambda i, e: (i, 0)
    same = lambda i, e: (0, 0)
    quad = lambda i, e: (i, 0, 0, 0)
    wide = 2 * DK + DV
    chunks = total // CHUNK
    kernel = functools.partial(forward_kernel, heads=heads, rows=rows, taps=taps.shape[0])
    return pl.pallas_call(
        kernel,
        grid_spec=pltpu.PrefetchScalarGridSpec(
            num_scalar_prefetch=1,
            grid=(blocks,),
            in_specs=[
                pl.BlockSpec((rows, width), row),
                pl.BlockSpec(taps.shape, same),
                pl.BlockSpec(rate.shape, same),
                pl.BlockSpec(shift.shape, same),
                pl.BlockSpec(gain.shape, same),
            ],
            out_specs=[
                pl.BlockSpec((rows, heads * DV), row),
                pl.BlockSpec((rows, heads * DV), row),
                pl.BlockSpec((rows, heads * DV), row),
                pl.BlockSpec((n, heads, DK, DV), quad),
                pl.BlockSpec((n, heads, CHUNK, CHUNK), quad),
                pl.BlockSpec((n, heads, CHUNK, DK), quad),
                pl.BlockSpec((n, heads, DK, DK), quad),
            ],
            scratch_shapes=[
                pltpu.VMEM((rows + 8, heads * wide), f32),
                pltpu.VMEM((heads, DK, DV), f32),
            ],
        ),
        out_shape=[
            jax.ShapeDtypeStruct((total, heads * DV), bf16),
            jax.ShapeDtypeStruct((total, heads * DV), f32),
            jax.ShapeDtypeStruct((total, heads * DV), f32),
            jax.ShapeDtypeStruct((chunks, heads, DK, DV), f32),
            jax.ShapeDtypeStruct((chunks, heads, CHUNK, CHUNK), f32),
            jax.ShapeDtypeStruct((chunks, heads, CHUNK, DK), f32),
            jax.ShapeDtypeStruct((chunks, heads, DK, DK), f32),
        ],
        compiler_params=pltpu.CompilerParams(
            dimension_semantics=("arbitrary",), vmem_limit_bytes=56 * 1024 * 1024
        ),
        name="mixer_forward",
    )(ends, proj, taps, rate, shift, gain)


def mixer_backward(ends, proj, taps, rate, shift, gain, dgated, saved, *, heads, rows):
    total, width = proj.shape
    blocks = total // rows
    n = rows // CHUNK
    row = lambda s, e: (blocks - 1 - s, 0)
    halo = lambda s, e: (jnp.maximum((blocks - 1 - s) * (rows // 8) - 1, 0), 0)
    same = lambda s, e: (0, 0)
    quad = lambda s, e: (blocks - 1 - s, 0, 0, 0)
    wide = 2 * DK + DV
    kernel = functools.partial(backward_kernel, heads=heads, rows=rows, taps=taps.shape[0], blocks=blocks)
    return pl.pallas_call(
        kernel,
        grid_spec=pltpu.PrefetchScalarGridSpec(
            num_scalar_prefetch=1,
            grid=(blocks,),
            in_specs=[
                pl.BlockSpec((rows, width), row),
                pl.BlockSpec((8, width), halo),
                pl.BlockSpec(taps.shape, same),
                pl.BlockSpec(rate.shape, same),
                pl.BlockSpec(shift.shape, same),
                pl.BlockSpec(gain.shape, same),
                pl.BlockSpec((rows, heads * DV), row),
                pl.BlockSpec((rows, heads * DV), row),
                pl.BlockSpec((rows, heads * DV), row),
                pl.BlockSpec((n, heads, DK, DV), quad),
                pl.BlockSpec((n, heads, CHUNK, CHUNK), quad),
                pl.BlockSpec((n, heads, CHUNK, DK), quad),
                pl.BlockSpec((n, heads, DK, DK), quad),
            ],
            out_specs=[
                pl.BlockSpec((rows, width), row),
                pl.BlockSpec((32, heads * wide), same),
                pl.BlockSpec((8, DV), same),
                pl.BlockSpec((16, 128), same),
            ],
            scratch_shapes=[
                pltpu.VMEM((rows + 8, heads * wide), f32),
                pltpu.VMEM((rows + 8, heads * wide), f32),
                pltpu.VMEM((heads, DK, DV), f32),
            ],
        ),
        out_shape=[
            jax.ShapeDtypeStruct((total, width), bf16),
            jax.ShapeDtypeStruct((32, heads * wide), f32),
            jax.ShapeDtypeStruct((8, DV), f32),
            jax.ShapeDtypeStruct((16, 128), f32),
        ],
        compiler_params=pltpu.CompilerParams(
            dimension_semantics=("arbitrary",), vmem_limit_bytes=56 * 1024 * 1024
        ),
        name="mixer_backward",
    )(ends, proj, proj, taps, rate, shift, gain, dgated, *saved)


BLOCK_ROWS = 256


def rms_scale(values):
    return lax.rsqrt(jnp.mean(values * values, axis=-1, keepdims=True) + epsilon)


def norm_back(values, scale, gain, grad):
    u = gain * grad
    back = scale * u - values * (scale * scale * scale) * jnp.mean(values * u, axis=-1, keepdims=True)
    return back, jnp.sum(grad * (values * scale), axis=0)


def swap(x, axis, bit):
    size = lax.axis_size(axis)
    return lax.ppermute(x, axis, [(i, i ^ bit) for i in range(size)])


def exchange_roles(x):
    n = lax.axis_size("lo")
    return lax.ppermute(x, ("lo", "tensor"), [(a * n + b, b * n + a) for a in range(n) for b in range(n)])


def bits(size):
    return [1 << k for k in range(size.bit_length() - 1)]


def gather_rows(x):
    pieces = {0: x}
    for bit in reversed(bits(lax.axis_size("lo"))):
        pieces.update({k ^ bit: swap(p, "lo", bit) for k, p in list(pieces.items())})
    return jnp.concatenate([pieces[k] for k in sorted(pieces)], axis=0)


def scatter_sum(x):
    n = lax.axis_size("lo")
    rows = x.shape[0] // n
    held = {k: x[k * rows : (k + 1) * rows] for k in range(n)}
    for bit in bits(n):
        sent = [k for k in held if k & bit]
        sums = {}
        for k in sent:
            got = swap(held[k].astype(x.dtype), "lo", bit)
            sums[k ^ bit] = held[k ^ bit].astype(f32) + got.astype(f32)
        held = sums
    return held[0]


def sum_everywhere(x):
    for axis in ("lo", "tensor", "hi"):
        for bit in bits(lax.axis_size(axis)):
            x = x + swap(x, axis, bit)
    return x


def rank_of(key):
    return jnp.sum((key[..., None, :] < key[..., :, None]).astype(jnp.int32), axis=-1)


def after(x, *first):
    return lax.optimization_barrier((x, first))[0]


def widen(columns):
    return lax.all_gather(exchange_roles(columns), ("hi", "tensor"), axis=0, tiled=True)


def narrow(columns):
    return exchange_roles(
        lax.psum_scatter(columns.astype(bf16), ("hi", "tensor"), scatter_dimension=0, tiled=True)
    ).astype(f32)


def product(a, b, ca=1, cb=0, dtype=f32):
    return lax.dot_general(a, b, (((ca,), (cb,)), ((), ())), preferred_element_type=f32).astype(dtype)


def body(
    tokens,
    cotangent,
    lengths,
    token_order,
    token_return,
    w_mix,
    w_ba,
    conv_w,
    w_out,
    w_gate_up,
    w_down,
    gain_attn,
    gain_ffn,
    gain_out,
    decay_log,
    decay_bias,
):
    splits = lax.axis_size("lo")
    groups = lax.axis_size("hi") * splits
    me = lax.axis_index("lo")
    local_rows, model_width = tokens.shape
    group_rows = local_rows * splits
    per_peer = local_rows // groups
    weight_rows, heads, head_width = w_mix.shape
    units = w_down.shape[1]
    taps = conv_w.shape[2]
    conv_width = head_width - DV
    proj_width = heads * head_width

    spread = ("hi", "tensor")
    width = lax.axis_size("hi")
    span = jnp.arange(local_rows, dtype=jnp.int32)

    send_rank = rank_of(token_return // group_rows * local_rows + token_return % local_rows)
    send_hot = (span[:, None] == send_rank[None, :]).astype(bf16)

    def across(rows):
        moved = lax.all_to_all(
            rows.reshape(groups, per_peer, model_width), spread, split_axis=0, concat_axis=0, tiled=True
        )
        return moved.reshape(local_rows, model_width)

    def pack(rows):
        return across(product(send_hot, rows, dtype=bf16))

    def unpack(rows):
        return product(send_hot, across(rows), 0, 0, bf16)

    orders = gather_rows(exchange_roles(token_order)).reshape(splits, local_rows)
    orders = jnp.take(orders, jnp.arange(splits, dtype=jnp.int32) ^ me, axis=0)
    given = orders // group_rows
    place_of = rank_of(given * local_rows + span[None, :]) % per_peer
    held_at = (((given % splits) ^ me) * width + given // splits) * per_peer + place_of
    order_hot = (held_at[:, :, None] == span[None, None, :]).astype(bf16)

    def to_sequence(rows):
        parts = rows.reshape(splits * width, splits, per_peer, -1)
        parts = jnp.transpose(parts, (1, 0, 2, 3)).reshape(splits, local_rows, -1)
        return lax.dot_general(
            order_hot, parts, (((2,), (1,)), ((0,), (0,))), preferred_element_type=f32
        ).astype(bf16).reshape(group_rows, -1)

    def from_sequence(rows):
        parts = lax.dot_general(
            order_hot, rows.reshape(splits, local_rows, -1), (((1,), (1,)), ((0,), (0,))), preferred_element_type=f32
        ).astype(bf16).reshape(splits, splits * width, per_peer, -1)
        return jnp.transpose(parts, (1, 0, 2, 3)).reshape(group_rows, -1)

    own_lengths = exchange_roles(lengths)
    ends = jnp.sum(jnp.where(jnp.tri(SEQS, dtype=bool), own_lengths, 0), axis=1).astype(jnp.int32)
    spare = 128 - heads * w_ba.shape[2] - taps
    mix_all = widen(
        jnp.concatenate(
            [
                w_mix.reshape(weight_rows, proj_width).astype(bf16),
                w_ba.reshape(weight_rows, -1).astype(bf16),
                conv_w.reshape(weight_rows, taps).astype(bf16),
                jnp.zeros((weight_rows, spare), bf16),
            ],
            axis=1,
        )
    )
    packed_in = pack(tokens)
    out_all = widen(after(w_out.reshape(weight_rows, heads * DV).astype(bf16), packed_in))
    ffn_all = widen(
        after(
            jnp.concatenate(
                [w_gate_up.reshape(weight_rows, 2 * units).astype(bf16), w_down.astype(bf16)], axis=1
            ),
            packed_in,
        )
    )

    input_f32 = packed_in.astype(f32)
    input_scale = rms_scale(input_f32)
    gathered = gather_rows((input_f32 * input_scale * gain_attn).astype(bf16))
    packed_grad = pack(after(cotangent, gathered))
    normed_seq = to_sequence(gathered)

    small_at = proj_width
    conv_at = small_at + heads * w_ba.shape[2]
    conv_all = mix_all[:, conv_at : conv_at + taps].reshape(-1, heads, taps).astype(f32)
    tap_rows = jnp.transpose(conv_all, (2, 1, 0)).reshape(taps, heads * conv_width)
    projected = product(normed_seq, mix_all)
    head_start = me * heads
    lanes = jnp.zeros((1, 128), f32)
    rate_row = lanes.at[0, 1 : 2 * heads : 2].set(lax.dynamic_slice_in_dim(decay_log, head_start, heads))
    shift_row = lanes.at[0, 1 : 2 * heads : 2].set(lax.dynamic_slice_in_dim(decay_bias, head_start, heads))
    gain_row = gain_out[None]
    saved = mixer_forward(
        ends, projected, tap_rows, rate_row, shift_row, gain_row, heads=heads, rows=BLOCK_ROWS
    )
    grad_all = gather_rows(packed_grad)
    gated = saved[0]
    middle = input_f32 + scatter_sum(product(from_sequence(gated), out_all, 1, 1))
    mid_scale = rms_scale(middle)
    normed_mid_all = gather_rows((middle * mid_scale * gain_ffn).astype(bf16))

    in_sequence = jnp.arange(group_rows, dtype=jnp.int32).reshape(splits, local_rows, 1) < ends[SEQS - 1]
    live = from_sequence(jnp.broadcast_to(in_sequence, (splits, local_rows, 128)).astype(bf16))[:, :1].astype(f32)
    w_pair = ffn_all[:, : 2 * units]
    w_last = ffn_all[:, 2 * units :]
    grad_hidden = product(grad_all, w_last) * live
    gate_up = product(normed_mid_all, w_pair)
    gate, up = gate_up[:, :units], gate_up[:, units:]
    s = sigmoid(gate)
    hidden = (gate * s * up * live).astype(bf16)
    grad_pair = jnp.concatenate(
        [grad_hidden * up * (s * (1.0 + gate * (1.0 - s))), grad_hidden * (gate * s)], axis=1
    ).astype(bf16)
    grad_norm_terms = product(grad_pair, w_pair, 1, 1, bf16)
    grad_norm_mid = scatter_sum(grad_norm_terms)
    hidden, grad_pair = after((hidden, grad_pair), grad_norm_terms)
    grad_ffn = jnp.concatenate(
        [product(normed_mid_all, grad_pair, 0, 0, bf16), product(grad_all, hidden, 0, 0, bf16)], axis=1
    )
    layer_terms = product(hidden, w_last, 1, 1, bf16)
    grad_mid_norm, grad_gain_ffn = norm_back(middle, mid_scale, gain_ffn, grad_norm_mid)
    grad_middle = packed_grad.astype(f32) + grad_mid_norm
    grad_middle_all = gather_rows(after(grad_middle.astype(bf16), grad_ffn, layer_terms))
    grad_ffn = narrow(grad_ffn)

    grad_middle_seq = to_sequence(grad_middle_all)
    grad_gated = product(grad_middle_seq, out_all)
    grad_out_w = product(grad_middle_seq, gated, 0, 0, bf16)
    grad_gated, layer_terms = after((grad_gated, layer_terms), grad_out_w)
    grad_out_w = narrow(grad_out_w)
    layer_out = unpack((middle + scatter_sum(layer_terms)).astype(bf16))
    grad_proj, grad_taps, grad_gain_out, grad_decay = mixer_backward(
        ends, projected, tap_rows, rate_row, shift_row, gain_row, grad_gated, saved[1:],
        heads=heads, rows=BLOCK_ROWS,
    )
    grad_conv = jnp.sum(grad_taps.reshape(taps, 8, heads, conv_width), axis=1)
    grad_conv = jnp.transpose(grad_conv, (2, 1, 0)).reshape(-1, taps).astype(bf16)
    grad_mix = product(normed_seq, grad_proj, 0, 0, bf16)
    grad_mix = jnp.concatenate([grad_mix[:, :conv_at], grad_conv, grad_mix[:, conv_at + taps :]], axis=1)
    grad_normed = scatter_sum(from_sequence(product(after(grad_proj, grad_mix), mix_all, 1, 1, bf16)))
    grad_mix = narrow(grad_mix)
    grad_input_norm, grad_gain_attn = norm_back(input_f32, input_scale, gain_attn, grad_normed)
    input_grad = unpack((grad_middle + grad_input_norm).astype(bf16))

    head_total = decay_log.shape[0]
    decay_sums = jnp.sum(grad_decay.reshape(2, 8, 128), axis=1)[:, 1 : 2 * heads : 2]
    decay_full = lax.dynamic_update_slice(jnp.zeros((2, head_total), f32), decay_sums, (0, head_start))
    flat = jnp.concatenate(
        [grad_gain_attn, grad_gain_ffn, jnp.sum(grad_gain_out, axis=0), decay_full.reshape(-1)]
    )
    flat = sum_everywhere(jnp.pad(flat, (0, -flat.shape[0] % 1024)).reshape(8, -1)).reshape(-1)
    at = 0
    sums = []
    for size in (model_width, model_width, gain_out.shape[0], head_total, head_total):
        sums.append(flat[at : at + size])
        at += size
    return (
        layer_out,
        input_grad,
        grad_mix[:, :small_at].reshape(w_mix.shape),
        grad_mix[:, small_at:conv_at].reshape(w_ba.shape),
        grad_mix[:, conv_at : conv_at + taps].reshape(conv_w.shape),
        grad_out_w.reshape(w_out.shape),
        grad_ffn[:, : 2 * units].reshape(w_gate_up.shape),
        grad_ffn[:, 2 * units :],
        *sums,
    )


def solution(mesh):
    dp, splits = mesh.shape["dp"], mesh.shape["tensor"]
    roles = Mesh(mesh.devices.reshape(dp // splits, splits, splits), ("hi", "lo", "tensor"))
    group = ("hi", "lo")
    rows = P((*group, "tensor"))
    by_head = P(group, "tensor", None)
    by_unit = (P(group, None, "tensor"), P(group, "tensor"))
    return jax.shard_map(
        body,
        mesh=roles,
        in_specs=(rows, rows, P(group), rows, rows, by_head, by_head, by_head, by_head, *by_unit)
        + (P(),) * 5,
        out_specs=(rows, rows, by_head, by_head, by_head, by_head, *by_unit) + (P(),) * 5,
        check_vma=False,
    )
```

```python
import functools
import jax
import jax.numpy as jnp
from jax import lax
from jax.experimental import pallas as pl
from jax.experimental.pallas import tpu as pltpu
from jax.sharding import Mesh
from jax.sharding import PartitionSpec as P

DK = 128
DV = 256
SEQS = 3
CHUNK = 128
epsilon = 1e-06
f32 = jnp.float32
bf16 = jnp.bfloat16


def dot(a, b, ca=1, cb=0):
    return lax.dot_general(a, b, (((ca,), (cb,)), ((), ())), preferred_element_type=f32)


def halves(x):
    high = x.astype(bf16)
    return high, (x - high.astype(f32)).astype(bf16)


def dot1(a, b, ca=1, cb=0):
    return dot(a.astype(bf16), b.astype(bf16), ca, cb)


def dot3(a, b, ca=1, cb=0):
    ah, al = halves(a)
    bh, bl = halves(b)
    return dot(ah, bh, ca, cb) + (dot(ah, bl, ca, cb) + dot(al, bh, ca, cb))


def dot_exact(a, b, ca=1, cb=0):
    ah = a.astype(bf16)
    bh, bl = halves(b)
    bt = (b - bh.astype(f32) - bl.astype(f32)).astype(bf16)
    return dot(ah, bh, ca, cb) + (dot(ah, bl, ca, cb) + dot(ah, bt, ca, cb))


def sigmoid(x):
    return 1.0 / (1.0 + jnp.exp(-x))


def segment_of(position, ends):
    return sum((position >= e).astype(jnp.int32) for e in ends)


def iota(shape, axis):
    return lax.broadcasted_iota(jnp.int32, shape, axis)


def conv_masks(base, rows, ends, taps, sign):
    t = base + iota((rows, 1), 0)
    own = segment_of(t, ends)
    masks = []
    for j in range(1, taps):
        other = t - sign * j
        same = segment_of(other, ends) == own
        masks.append(jnp.where(same & (other >= 0), 1.0, 0.0))
    return masks


def chunk_terms(base, ends, g_col, g_row, q, k, beta):
    c = CHUNK
    ti = base + iota((c, 1), 0)
    tj = base + iota((1, c), 1)
    si = segment_of(ti, ends)
    sj = segment_of(tj, ends)
    ii = iota((c, c), 0)
    jj = iota((c, c), 1)
    decay = jnp.where((si == sj) & (ii >= jj), jnp.exp(jnp.minimum(g_col - g_row, 0.0)), 0.0)
    before = jnp.where(base > 0, segment_of(base - 1, ends), -1)
    last = segment_of(base + c - 1, ends)
    carry = jnp.where(si == before, jnp.exp(g_col), 0.0)
    g_last = g_col[c - 1 :, :]
    tail = jnp.where(si == last, jnp.exp(jnp.minimum(g_last - g_col, 0.0)), 0.0)
    return decay, carry, tail, ii, jj


def invert(lower, ii, jj, mul):
    first = ((ii ^ jj) == 1) & (ii > jj)
    eye = jnp.where(ii == jj, 1.0, 0.0)
    inv = [eye - jnp.where(first, a, 0.0) for a in lower]
    size = 2
    while size < CHUNK:
        joins = ((ii // (2 * size)) == (jj // (2 * size))) & ((ii & size) != 0) & ((jj & size) == 0)
        half = [mul(jnp.where(joins, a, 0.0), t) for a, t in zip(lower, inv)]
        inv = [t - mul(t, x) for t, x in zip(inv, half)]
        size *= 2
    return inv


def silu_parts(u):
    s = sigmoid(u)
    return u * s, s


def forward_kernel(
    ends_ref, proj_ref, before_ref, taps_ref, rate_ref, shift_ref, gain_ref, enter_ref,
    gated_ref, o_ref, u_ref, s_ref, t_ref, qe_ref, m_ref, state,
    xs, *, heads, rows, taps, start,
):
    i = pl.program_id(0)
    wide = 2 * DK + DV
    full = wide + DV
    ends = [ends_ref[k] for k in range(SEQS)]
    base = start + i * rows
    c = CHUNK

    @pl.when(i == 0)
    def _():
        for h in range(heads):
            xs[0:8, h * wide : (h + 1) * wide] = before_ref[:, h * full : h * full + wide]
        state[...] = enter_ref[...]

    @pl.when(i > 0)
    def _():
        xs[0:8, :] = xs[rows : rows + 8, :]

    for h in range(heads):
        xs[8:, h * wide : (h + 1) * wide] = proj_ref[:, h * full : h * full + wide]
    small = proj_ref[:, heads * full :]
    beta_all = sigmoid(small)
    shifted = small + shift_ref[...]
    ld_all = -jnp.exp(rate_ref[...]) * (jnp.maximum(shifted, 0.0) + jnp.log1p(jnp.exp(-jnp.abs(shifted))))
    masks = conv_masks(base, rows, ends, taps, 1)
    qs, ks, vs = [], [], []
    for h in range(heads):
        sl = slice(h * wide, (h + 1) * wide)
        run = xs[8:, sl] * taps_ref[0:1, sl]
        for j in range(1, taps):
            run = run + (xs[8 - j : 8 - j + rows, sl] * masks[j - 1]) * taps_ref[j : j + 1, sl]
        act = run * sigmoid(run)
        q, k, v = act[:, :DK], act[:, DK : 2 * DK], act[:, 2 * DK :]
        qs.append(q * (lax.rsqrt(jnp.sum(q * q, axis=-1, keepdims=True) + epsilon) * DK ** (-0.5)))
        ks.append(k * lax.rsqrt(jnp.sum(k * k, axis=-1, keepdims=True) + epsilon))
        vs.append(v)
    lower_tri = jnp.where(iota((c, c), 0) >= iota((c, c), 1), 1.0, 0.0)
    n = rows // c
    probs = []
    for b in range(n):
        rs = slice(b * c, (b + 1) * c)
        g_all = dot_exact(lower_tri, ld_all[rs])
        g_t = g_all.T
        for h in range(heads):
            q, k, v = qs[h][rs], ks[h][rs], vs[h][rs]
            beta = beta_all[rs, 2 * h : 2 * h + 1]
            g_col = g_all[:, 2 * h + 1 : 2 * h + 2]
            g_row = g_t[2 * h + 1 : 2 * h + 2, :]
            decay, carry, tail, ii, jj = chunk_terms(base + b * c, ends, g_col, g_row, q, k, beta)
            qkk = DOT_QK(jnp.concatenate([q, k], axis=0), k, 1, 1)
            p = qkk[:c] * decay
            a = jnp.where(ii > jj, qkk[c:] * decay, 0.0) * beta
            probs.append(dict(b=b, h=h, q=q, k=k, v=v, beta=beta, carry=carry, tail=tail, p=p, a=a))
    inv = invert([x["a"] for x in probs], ii, jj, DOT_INV)
    for x, t in zip(probs, inv):
        x["t"] = t
        rhs = jnp.concatenate([(x["beta"] * x["carry"]) * x["k"], x["beta"] * x["v"]], axis=1)
        x["wv"] = DOT_WV(t, rhs)
    for x in probs:
        pwv = DOT_P(x["p"], x["wv"])
        x["qe"] = x["carry"] * x["q"] - pwv[:, :DK]
        x["pv"] = pwv[:, DK:]
        kwv = DOT_K(x["tail"] * x["k"], x["wv"], 0, 0)
        c_last = x["carry"][c - 1 :, :]
        x["m"] = jnp.where(ii == jj, c_last, 0.0) - kwv[:, :DK]
        x["bf"] = kwv[:, DK:]
    for x in probs:
        b, h = x["b"], x["h"]
        s = state[h]
        s_ref[b, h] = s
        t_ref[b, h] = x["t"]
        qe_ref[b, h] = x["qe"]
        m_ref[b, h] = x["m"]
        w = x["wv"][:, :DK]
        state[h] = x["bf"] + DOT_S(x["m"], s)
        wq = DOT_O(jnp.concatenate([w, x["qe"]], axis=0), s)
        u_ref[b * c : (b + 1) * c, h * DV : (h + 1) * DV] = x["wv"][:, DK:] - wq[:c]
        o_ref[b * c : (b + 1) * c, h * DV : (h + 1) * DV] = x["pv"] + wq[c:]
    live = jnp.where(segment_of(base + iota((rows, 1), 0), ends) < SEQS, 1.0, 0.0)
    for h in range(heads):
        o = o_ref[:, h * DV : (h + 1) * DV]
        z = proj_ref[:, h * full + wide : (h + 1) * full]
        r = lax.rsqrt(jnp.mean(o * o, axis=-1, keepdims=True) + epsilon)
        gated_ref[:, h * DV : (h + 1) * DV] = (o * (r * live) * gain_ref[...] * (z * sigmoid(z))).astype(bf16)


def backward_kernel(
    ends_ref, proj_ref, halo_ref, before_ref, taps_ref, rate_ref, shift_ref, gain_ref,
    dgated_ref, o_ref, u_ref, s_ref, t_ref, qe_ref, m_ref, leave_ref, later_ref,
    dproj_ref, dtaps_ref, dgain_ref, ddecay_ref, dstate, first_ref,
    xs, ds, *, heads, rows, taps, blocks, start,
):
    step = pl.program_id(0)
    i = blocks - 1 - step
    wide = 2 * DK + DV
    full = wide + DV
    ends = [ends_ref[k] for k in range(SEQS)]
    base = start + i * rows
    c = CHUNK

    @pl.when(step == 0)
    def _():
        ds[rows : rows + 8, :] = later_ref[...]
        dstate[...] = leave_ref[...]
        dtaps_ref[...] = jnp.zeros_like(dtaps_ref)
        dgain_ref[...] = jnp.zeros_like(dgain_ref)
        ddecay_ref[...] = jnp.zeros_like(ddecay_ref)

    @pl.when(step > 0)
    def _():
        ds[rows : rows + 8, :] = ds[0:8, :]

    for h in range(heads):
        cols = slice(h * full, h * full + wide)
        xs[0:8, h * wide : (h + 1) * wide] = jnp.where(i == 0, before_ref[:, cols], halo_ref[:, cols])
        xs[8:, h * wide : (h + 1) * wide] = proj_ref[:, h * full : h * full + wide]
    small = proj_ref[:, heads * full :]
    beta_all = sigmoid(small)
    shifted = small + shift_ref[...]
    rate = -jnp.exp(rate_ref[...])
    ld_all = rate * (jnp.maximum(shifted, 0.0) + jnp.log1p(jnp.exp(-jnp.abs(shifted))))
    masks = conv_masks(base, rows, ends, taps, 1)
    live = jnp.where(segment_of(base + iota((rows, 1), 0), ends) < SEQS, 1.0, 0.0)
    acts = []
    dos = []
    for h in range(heads):
        sl = slice(h * wide, (h + 1) * wide)
        run = xs[8:, sl] * taps_ref[0:1, sl]
        for j in range(1, taps):
            run = run + (xs[8 - j : 8 - j + rows, sl] * masks[j - 1]) * taps_ref[j : j + 1, sl]
        sg = sigmoid(run)
        act = run * sg
        dact = sg * (1.0 + run * (1.0 - sg))
        q, k, v = act[:, :DK], act[:, DK : 2 * DK], act[:, 2 * DK :]
        rq = lax.rsqrt(jnp.sum(q * q, axis=-1, keepdims=True) + epsilon)
        rk = lax.rsqrt(jnp.sum(k * k, axis=-1, keepdims=True) + epsilon)
        acts.append((q * rq, k * rk, v, dact, rq, rk))
        o = o_ref[:, h * DV : (h + 1) * DV]
        z = proj_ref[:, h * full + wide : (h + 1) * full]
        dg = dgated_ref[:, h * DV : (h + 1) * DV] * live
        r = lax.rsqrt(jnp.mean(o * o, axis=-1, keepdims=True) + epsilon)
        nrm = o * r
        sz = sigmoid(z)
        dz = dg * nrm * gain_ref[...] * (sz * (1.0 + z * (1.0 - sz)))
        dng = dg * (z * sz)
        dgain_ref[...] += jnp.sum((dng * nrm).reshape(rows // 8, 8, DV), axis=0)
        dn = dng * gain_ref[...]
        dos.append(r * (dn - nrm * jnp.mean(dn * nrm, axis=-1, keepdims=True)))
        dproj_ref[:, h * full + wide : (h + 1) * full] = dz.astype(bf16)
    low_i = iota((c, c), 0)
    low_j = iota((c, c), 1)
    lower_tri = jnp.where(low_i >= low_j, 1.0, 0.0)
    upper_tri = jnp.where(low_i <= low_j, 1.0, 0.0)
    strict_low = jnp.where(low_i > low_j, 1.0, 0.0)
    n = rows // c
    probs = []
    for b in reversed(range(n)):
        rs = slice(b * c, (b + 1) * c)
        g_all = dot_exact(lower_tri, ld_all[rs])
        g_t = g_all.T
        for h in range(heads):
            q, k, v = acts[h][0][rs] * DK ** (-0.5), acts[h][1][rs], acts[h][2][rs]
            beta = beta_all[rs, 2 * h : 2 * h + 1]
            g_col = g_all[:, 2 * h + 1 : 2 * h + 2]
            g_row = g_t[2 * h + 1 : 2 * h + 2, :]
            decay, carry, tail, ii, jj = chunk_terms(base + b * c, ends, g_col, g_row, q, k, beta)
            qkk = DOT_QK(jnp.concatenate([q, k], axis=0), k, 1, 1)
            p = qkk[:c] * decay
            dkk = jnp.where(ii > jj, qkk[c:] * decay, 0.0)
            do = dos[h][rs]
            u = u_ref[rs, h * DV : (h + 1) * DV]
            dp = DOT_B(do, u, 1, 1)
            pdo = DOT_B(p, do, 0, 0)
            qdo = DOT_B(qe_ref[b, h], do, 0, 0)
            f = DOT_B(do, s_ref[b, h], 1, 1)
            probs.append(dict(b=b, h=h, q=q, k=k, v=v, beta=beta, carry=carry, tail=tail, decay=decay, p=p, dkk=dkk,
                              do=do, u=u, dp=dp, pdo=pdo, qdo=qdo, f=f))
    for x in probs:
        b, h = x["b"], x["h"]
        dnext = dstate[h]
        x["dnext"] = dnext
        dstate[h] = DOT_S(m_ref[b, h], dnext, 0, 0) + x["qdo"]
    for x in probs:
        du = x["pdo"] + DOT_B(x["tail"] * x["k"], x["dnext"])
        x["dr"] = DOT_B(t_ref[x["b"], x["h"]], du, 0, 0)
        x["j"] = DOT_B(x["u"], x["dnext"], 1, 1)
    dq_all = [[None] * n for _ in range(heads)]
    dk_all = [[None] * n for _ in range(heads)]
    dv_all = [[None] * n for _ in range(heads)]
    dsmall = [[None] * heads for _ in range(n)]
    lane = iota((c, DK), 1)
    for x in probs:
        b, h, q, k, beta, carry = x["b"], x["h"], x["q"], x["k"], x["beta"], x["carry"]
        dr = x["dr"]
        s = s_ref[b, h]
        neg = DOT_B(dr, x["u"], 1, 1)
        hh = DOT_B(dr, s, 1, 1)
        neg = jnp.where(ii > jj, neg, 0.0)
        adk = neg * x["dkk"]
        dbeta = (
            jnp.sum(dr * x["v"], axis=-1, keepdims=True)
            - carry * jnp.sum(k * hh, axis=-1, keepdims=True)
            - jnp.sum(adk, axis=-1, keepdims=True)
        )
        dcarry = jnp.sum(q * x["f"], axis=-1, keepdims=True) - beta * jnp.sum(k * hh, axis=-1, keepdims=True)
        e = x["dp"] * x["p"] - beta * adk
        dqk = x["dp"] * x["decay"]
        dkk = -(neg * beta) * jnp.where(ii > jj, x["decay"], 0.0)
        dtail = x["tail"] * jnp.sum(k * x["j"], axis=-1, keepdims=True)
        dcl = carry[c - 1 :, :] * jnp.sum(x["dnext"] * s, keepdims=True)
        col = carry * dcarry + jnp.where(iota((c, 1), 0) == c - 1, dcl, 0.0)
        straddle = jnp.where(ii > jj, dot_exact(upper_tri, e), 0.0)
        both = dot_exact(upper_tri, jnp.where(lane == 0, col, 0.0)) + dot_exact(
            strict_low, jnp.where(lane == 0, dtail, 0.0)
        )
        dld = jnp.sum(straddle, axis=-1, keepdims=True) + both[:, 0:1]
        dq_all[h][b] = carry * x["f"] + DOT_G(dqk, k)
        dk_all[h][b] = (
            x["tail"] * x["j"] - (carry * beta) * hh + DOT_G(dqk, q, 0, 0) + DOT_G(dkk, k) + DOT_G(dkk, k, 0, 0)
        )
        dv_all[h][b] = beta * dr
        dsmall[b][h] = (dbeta, dld)
    for b in range(n):
        rs = slice(b * c, (b + 1) * c)
        tile = jnp.zeros((c, DK), f32)
        for h in range(heads):
            dbeta, dld = dsmall[b][h]
            tile = jnp.where(lane == 2 * h, dbeta, jnp.where(lane == 2 * h + 1, dld, tile))
        bet = beta_all[rs]
        dshift = rate * tile * sigmoid(shifted[rs])
        even = (lane & 1) == 0
        inside = lane < 2 * heads
        ddecay_ref[0:8, :] += jnp.sum(jnp.where(even, 0.0, tile * ld_all[rs]).reshape(c // 8, 8, DK), axis=0)
        ddecay_ref[8:16, :] += jnp.sum(jnp.where(even, 0.0, dshift).reshape(c // 8, 8, DK), axis=0)
        dproj_ref[rs, heads * full :] = jnp.where(
            inside, jnp.where(even, tile * (bet * (1.0 - bet)), dshift), 0.0
        ).astype(bf16)
    for h in range(heads):
        qn, kn, v, dact, rq, rk = acts[h]
        dq = jnp.concatenate(dq_all[h], axis=0) * DK ** (-0.5)
        dk = jnp.concatenate(dk_all[h], axis=0)
        dq = rq * (dq - qn * jnp.sum(dq * qn, axis=-1, keepdims=True))
        dk = rk * (dk - kn * jnp.sum(dk * kn, axis=-1, keepdims=True))
        dv = jnp.concatenate(dv_all[h], axis=0)
        o = h * wide
        ds[0:rows, o : o + DK] = dq * dact[:, :DK]
        ds[0:rows, o + DK : o + 2 * DK] = dk * dact[:, DK : 2 * DK]
        ds[0:rows, o + 2 * DK : o + wide] = dv * dact[:, 2 * DK :]
    ahead = conv_masks(base, rows, ends, taps, -1)
    for h in range(heads):
        sl = slice(h * wide, (h + 1) * wide)
        own = ds[0:rows, sl]
        total = own * taps_ref[0:1, sl]
        dtaps_ref[0:8, sl] += jnp.sum((own * xs[8:, sl]).reshape(rows // 8, 8, wide), axis=0)
        for j in range(1, taps):
            total = total + (ds[j : j + rows, sl] * ahead[j - 1]) * taps_ref[j : j + 1, sl]
            dtaps_ref[8 * j : 8 * j + 8, sl] += jnp.sum(
                (own * (xs[8 - j : 8 - j + rows, sl] * masks[j - 1])).reshape(rows // 8, 8, wide), axis=0
            )
        dproj_ref[:, h * full : h * full + wide] = total.astype(bf16)
    first_ref[...] = ds[0:8, :]


DOT_QK = dot3
DOT_INV = dot3
DOT_WV = dot3
DOT_P = dot3
DOT_K = dot3
DOT_S = dot3
DOT_O = dot3
DOT_B = dot3
DOT_G = dot1


def mixer_forward(ends, proj, before, before_at, taps, rate, shift, gain, enter, *, heads, rows, start):
    total, width = proj.shape
    blocks = total // rows
    n = rows // CHUNK
    row = lambda i, e: (i, 0)
    same = lambda i, e: (0, 0)
    quad = lambda i, e: (i, 0, 0, 0)
    wide = 2 * DK + DV
    chunks = total // CHUNK
    kernel = functools.partial(forward_kernel, heads=heads, rows=rows, taps=taps.shape[0], start=start)
    wide_rows = pl.BlockSpec((rows, heads * DV), row)
    return pl.pallas_call(
        kernel,
        grid_spec=pltpu.PrefetchScalarGridSpec(
            num_scalar_prefetch=1,
            grid=(blocks,),
            in_specs=[
                pl.BlockSpec((rows, width), row),
                pl.BlockSpec((8, width), lambda i, e: (before_at, 0)),
                pl.BlockSpec(taps.shape, same),
                pl.BlockSpec(rate.shape, same),
                pl.BlockSpec(shift.shape, same),
                pl.BlockSpec(gain.shape, same),
                pl.BlockSpec(enter.shape, lambda i, e: (0, 0, 0)),
            ],
            out_specs=[
                wide_rows,
                wide_rows,
                wide_rows,
                pl.BlockSpec((n, heads, DK, DV), quad),
                pl.BlockSpec((n, heads, CHUNK, CHUNK), quad),
                pl.BlockSpec((n, heads, CHUNK, DK), quad),
                pl.BlockSpec((n, heads, DK, DK), quad),
                pl.BlockSpec(enter.shape, lambda i, e: (0, 0, 0)),
            ],
            scratch_shapes=[pltpu.VMEM((rows + 8, heads * wide), f32)],
        ),
        out_shape=[
            jax.ShapeDtypeStruct((total, heads * DV), bf16),
            jax.ShapeDtypeStruct((total, heads * DV), f32),
            jax.ShapeDtypeStruct((total, heads * DV), f32),
            jax.ShapeDtypeStruct((chunks, heads, DK, DV), f32),
            jax.ShapeDtypeStruct((chunks, heads, CHUNK, CHUNK), f32),
            jax.ShapeDtypeStruct((chunks, heads, CHUNK, DK), f32),
            jax.ShapeDtypeStruct((chunks, heads, DK, DK), f32),
            jax.ShapeDtypeStruct(enter.shape, f32),
        ],
        compiler_params=pltpu.CompilerParams(
            dimension_semantics=("arbitrary",), vmem_limit_bytes=56 * 1024 * 1024
        ),
        cost_estimate=pl.CostEstimate(
            flops=total * heads * 6_000_000, bytes_accessed=total * heads * 9_000, transcendentals=total * heads * 2_000
        ),
        name="mixer_forward",
    )(ends, proj, before, taps, rate, shift, gain, enter)


def mixer_backward(
    ends, proj, before, before_at, taps, rate, shift, gain, dgated, saved, leave, later, *, heads, rows, start
):
    total, width = proj.shape
    blocks = total // rows
    n = rows // CHUNK
    row = lambda s, e: (blocks - 1 - s, 0)
    halo = lambda s, e: (jnp.maximum((blocks - 1 - s) * (rows // 8) - 1, 0), 0)
    same = lambda s, e: (0, 0)
    quad = lambda s, e: (blocks - 1 - s, 0, 0, 0)
    wide = 2 * DK + DV
    kernel = functools.partial(
        backward_kernel, heads=heads, rows=rows, taps=taps.shape[0], blocks=blocks, start=start
    )
    wide_rows = pl.BlockSpec((rows, heads * DV), row)
    return pl.pallas_call(
        kernel,
        grid_spec=pltpu.PrefetchScalarGridSpec(
            num_scalar_prefetch=1,
            grid=(blocks,),
            in_specs=[
                pl.BlockSpec((rows, width), row),
                pl.BlockSpec((8, width), halo),
                pl.BlockSpec((8, width), lambda s, e: (before_at, 0)),
                pl.BlockSpec(taps.shape, same),
                pl.BlockSpec(rate.shape, same),
                pl.BlockSpec(shift.shape, same),
                pl.BlockSpec(gain.shape, same),
                wide_rows,
                wide_rows,
                wide_rows,
                pl.BlockSpec((n, heads, DK, DV), quad),
                pl.BlockSpec((n, heads, CHUNK, CHUNK), quad),
                pl.BlockSpec((n, heads, CHUNK, DK), quad),
                pl.BlockSpec((n, heads, DK, DK), quad),
                pl.BlockSpec(leave.shape, lambda s, e: (0, 0, 0)),
                pl.BlockSpec(later.shape, same),
            ],
            out_specs=[
                pl.BlockSpec((rows, width), row),
                pl.BlockSpec((8 * taps.shape[0], heads * wide), same),
                pl.BlockSpec((8, DV), same),
                pl.BlockSpec((16, 128), same),
                pl.BlockSpec(leave.shape, lambda s, e: (0, 0, 0)),
                pl.BlockSpec(later.shape, same),
            ],
            scratch_shapes=[
                pltpu.VMEM((rows + 8, heads * wide), f32),
                pltpu.VMEM((rows + 8, heads * wide), f32),
            ],
        ),
        out_shape=[
            jax.ShapeDtypeStruct((total, width), bf16),
            jax.ShapeDtypeStruct((8 * taps.shape[0], heads * wide), f32),
            jax.ShapeDtypeStruct((8, DV), f32),
            jax.ShapeDtypeStruct((16, 128), f32),
            jax.ShapeDtypeStruct(leave.shape, f32),
            jax.ShapeDtypeStruct(later.shape, f32),
        ],
        compiler_params=pltpu.CompilerParams(
            dimension_semantics=("arbitrary",), vmem_limit_bytes=56 * 1024 * 1024
        ),
        cost_estimate=pl.CostEstimate(
            flops=total * heads * 1_000_000, bytes_accessed=total * heads * 9_000, transcendentals=total * heads * 2_000
        ),
        name="mixer_backward",
    )(ends, proj, proj, before, taps, rate, shift, gain, dgated, *saved, leave, later)


BLOCK_ROWS = 256
RUNS = 2


def rms_scale(values):
    return lax.rsqrt(jnp.mean(values * values, axis=-1, keepdims=True) + epsilon)


def norm_back(values, scale, gain, grad):
    u = gain * grad
    back = scale * u - values * (scale * scale * scale) * jnp.mean(values * u, axis=-1, keepdims=True)
    return back, jnp.sum(grad * (values * scale), axis=0)


def swap(x, axis, bit):
    size = lax.axis_size(axis)
    return lax.ppermute(x, axis, [(i, i ^ bit) for i in range(size)])


def exchange_roles(x):
    n = lax.axis_size("lo")
    return lax.ppermute(x, ("lo", "tensor"), [(a * n + b, b * n + a) for a in range(n) for b in range(n)])


def bits(size):
    return [1 << k for k in range(size.bit_length() - 1)]


def reversed_bits(n):
    order = [0]
    for bit in reversed(bits(n)):
        order = order + [k ^ bit for k in order]
    return order


def gather_first(x):
    return jnp.concatenate([x, swap(x, "lo", bits(lax.axis_size("lo"))[-1])], axis=0)


def gather_last(x):
    for bit in reversed(bits(lax.axis_size("lo"))[:-1]):
        x = jnp.concatenate([x, swap(x, "lo", bit)], axis=0)
    return x


def gather_rows(x):
    return gather_last(gather_first(x))


def halve(x, bit, kind):
    half = x.shape[0] // 2
    return x[:half].astype(f32) + swap(x[half:].astype(kind), "lo", bit).astype(f32)


def scatter_first(x):
    kind = x.dtype
    for bit in bits(lax.axis_size("lo"))[:-1]:
        x = halve(x, bit, kind)
    half = x.shape[0] // 2
    return x[:half], x[half:].astype(kind)


def scatter_last(kept, sent):
    return kept + swap(sent, "lo", bits(lax.axis_size("lo"))[-1]).astype(f32)


def sum_everywhere(x):
    for axis in ("lo", "tensor", "hi"):
        for bit in bits(lax.axis_size(axis)):
            x = x + swap(x, axis, bit)
    return x


def rank_of(key):
    return jnp.sum((key[..., None, :] < key[..., :, None]).astype(jnp.int32), axis=-1)


def after(x, *first):
    return lax.optimization_barrier((x, first))[0]


def widen(columns):
    return lax.all_gather(columns, ("hi", "tensor"), axis=0, tiled=True)


def narrow(columns):
    return exchange_roles(
        lax.psum_scatter(columns.astype(bf16), ("hi", "tensor"), scatter_dimension=0, tiled=True)
    ).astype(f32)


def product(a, b, ca=1, cb=0, dtype=f32):
    return lax.dot_general(a, b, (((ca,), (cb,)), ((), ())), preferred_element_type=f32).astype(dtype)


def body(
    tokens,
    cotangent,
    lengths,
    token_order,
    token_return,
    w_mix,
    w_ba,
    conv_w,
    w_out,
    w_gate_up,
    w_down,
    gain_attn,
    gain_ffn,
    gain_out,
    decay_log,
    decay_bias,
):
    splits = lax.axis_size("lo")
    groups = lax.axis_size("hi") * splits
    me = lax.axis_index("lo")
    local_rows, model_width = tokens.shape
    group_rows = local_rows * splits
    per_peer = local_rows // groups
    weight_rows, heads, head_width = w_mix.shape
    units = w_down.shape[1]
    taps = conv_w.shape[2]
    conv_width = head_width - DV
    proj_width = heads * head_width

    spread = ("hi", "tensor")
    width = lax.axis_size("hi")
    span = jnp.arange(local_rows, dtype=jnp.int32)
    part_rows = width * per_peer

    send_rank = rank_of(token_return // group_rows * local_rows + token_return % local_rows)
    send_hot = (span[:, None] == send_rank[None, :]).astype(bf16)

    def across(rows):
        return lax.all_to_all(rows, spread, split_axis=0, concat_axis=0, tiled=True)

    def pack(rows):
        return across(product(send_hot, rows, dtype=bf16).reshape(groups, per_peer, model_width))

    def by_part(rows):
        rows = jnp.transpose(rows.reshape(width, splits, per_peer, model_width), (1, 0, 2, 3))
        return rows.reshape(local_rows, model_width)

    def send_back(rows):
        rows = jnp.transpose(rows.reshape(splits, width, per_peer, model_width), (1, 0, 2, 3))
        return across(rows.reshape(groups, per_peer, model_width))

    def unpack(got):
        return product(send_hot, got.reshape(local_rows, model_width), 0, 0, bf16)

    pieces = jnp.array(reversed_bits(splits), jnp.int32)
    orders = gather_rows(exchange_roles(token_order)).reshape(splits, local_rows)
    parts = jnp.arange(splits, dtype=jnp.int32)
    stand = jnp.sum(jnp.where(pieces[None, :] == (parts ^ me)[:, None], parts[None, :], 0), axis=1)
    orders = jnp.sum(jnp.where((stand[:, None] == parts[None, :])[:, :, None], orders[None], 0), axis=1)
    given = orders // group_rows
    place_of = rank_of(given * local_rows + span[None, :]) % per_peer
    piece_of = jnp.sum(jnp.where((given % splits)[..., None] == parts, stand, 0), axis=-1)
    held_at = (piece_of * width + given // splits) * per_peer + place_of
    order_hot = (held_at[:, :, None] == span[None, None, :]).astype(bf16)
    run_parts = splits // RUNS
    run_rows = run_parts * local_rows

    def order_of(run):
        return order_hot[run * run_parts : (run + 1) * run_parts]

    def to_sequence(run, rows):
        rows = rows.reshape(splits, run_parts, part_rows, -1)
        rows = jnp.transpose(rows, (1, 0, 2, 3)).reshape(run_parts, local_rows, -1)
        return lax.dot_general(
            order_of(run), rows, (((2,), (1,)), ((0,), (0,))), preferred_element_type=f32
        ).astype(bf16).reshape(run_rows, -1)

    def from_sequence(run, rows):
        rows = lax.dot_general(
            order_of(run), rows.reshape(run_parts, local_rows, -1), (((1,), (1,)), ((0,), (0,))),
            preferred_element_type=f32,
        ).astype(bf16).reshape(run_parts, splits, part_rows, -1)
        return jnp.transpose(rows, (1, 0, 2, 3)).reshape(run_rows, -1)

    own_lengths = exchange_roles(lengths)
    ends = jnp.sum(jnp.where(jnp.tri(SEQS, dtype=bool), own_lengths, 0), axis=1).astype(jnp.int32)
    small_at = proj_width
    conv_at = small_at + heads * w_ba.shape[2]
    spare = 128 - heads * w_ba.shape[2] - taps
    mix_all = widen(
        exchange_roles(jnp.concatenate(
            [
                w_mix.reshape(weight_rows, proj_width).astype(bf16),
                w_ba.reshape(weight_rows, -1).astype(bf16),
                conv_w.reshape(weight_rows, taps).astype(bf16),
                jnp.zeros((weight_rows, spare), bf16),
                w_out.reshape(weight_rows, heads * DV).astype(bf16),
            ],
            axis=1,
        ))
    )
    packed_in = by_part(pack(tokens))
    runs = range(RUNS)
    own_rows = local_rows // RUNS

    def split(rows):
        return [rows[r * own_rows : (r + 1) * own_rows] for r in runs]

    input_f32 = packed_in.astype(f32)
    input_scale = rms_scale(input_f32)
    input_runs = split(input_f32)
    gathered = [gather_rows(x) for x in split((input_f32 * input_scale * gain_attn).astype(bf16))]
    cotangent, w_down, w_gate_up = after((cotangent, w_down, w_gate_up), *gathered)
    packed_grad = pack(cotangent)
    ffn_own = exchange_roles(
        jnp.concatenate([w_gate_up.reshape(weight_rows, 2 * units).astype(bf16), w_down.astype(bf16)], axis=1)
    )
    ffn_all = widen(ffn_own)
    w_pair, w_last = ffn_all[:, : 2 * units], ffn_all[:, 2 * units :]
    out_all = mix_all[:, small_at + 128 :]
    mix_all = mix_all[:, : small_at + 128]

    conv_all = mix_all[:, conv_at : conv_at + taps].reshape(-1, heads, taps).astype(f32)
    tap_rows = jnp.transpose(conv_all, (2, 1, 0)).reshape(taps, heads * conv_width)
    head_start = me * heads
    lanes = jnp.zeros((1, 128), f32)
    rate_row = lanes.at[0, 1 : 2 * heads : 2].set(lax.dynamic_slice_in_dim(decay_log, head_start, heads))
    shift_row = lanes.at[0, 1 : 2 * heads : 2].set(lax.dynamic_slice_in_dim(decay_bias, head_start, heads))
    gain_row = gain_out[None]
    constants = (tap_rows, rate_row, shift_row, gain_row)

    state = jnp.zeros((heads, DK, DV), f32)

    def ahead(r):
        return (projected[r - 1], run_rows // 8 - 1) if r else (projected[r], 0)

    def mix_forward(r, state):
        return mixer_forward(
            ends, projected[r], *ahead(r), *constants, state, heads=heads, rows=BLOCK_ROWS, start=r * run_rows
        )

    def feed_forward(r, normed_mid):
        place = (r * run_parts + jnp.arange(run_parts, dtype=jnp.int32))[:, None, None] * local_rows
        alive = (place + span[None, :, None] < ends[SEQS - 1]).astype(bf16)
        live = from_sequence(r, jnp.broadcast_to(alive, (run_parts, local_rows, 128)))[:, :1].astype(f32)
        grad_hidden = product(grad_all[r], w_last) * live
        gate_up = product(normed_mid, w_pair)
        gate, up = gate_up[:, :units], gate_up[:, units:]
        s = sigmoid(gate)
        hidden = (gate * s * up * live).astype(bf16)
        grad_pair = jnp.concatenate(
            [grad_hidden * up * (s * (1.0 + gate * (1.0 - s))), grad_hidden * (gate * s)], axis=1
        ).astype(bf16)
        return hidden, grad_pair, product(grad_pair, w_pair, 1, 1, bf16)

    def normed_of(middle):
        scale = rms_scale(middle)
        return scale, (middle * scale * gain_ffn).astype(bf16)

    constants = (tap_rows, rate_row, shift_row, gain_row)
    seq_0 = to_sequence(0, gathered[0])
    projected = [after(product(seq_0, mix_all), ffn_own)]
    *saved_0, state = mix_forward(0, state)
    terms_0 = product(from_sequence(0, saved_0[0]), out_all, 1, 1)
    seq_1 = to_sequence(1, after(gathered[1], terms_0))
    projected.append(product(seq_1, mix_all))
    grad_runs = split(by_part(after(packed_grad, terms_0)))
    kept_0, sent_0 = scatter_first(terms_0)
    grad_first = [gather_first(x) for x in grad_runs]
    projected[1], kept_0, sent_0, grad_first = lax.optimization_barrier((projected[1], kept_0, sent_0, grad_first))
    grad_all = [gather_last(x) for x in grad_first]
    *saved_1, state = mix_forward(1, state)
    middle_0 = input_runs[0] + after(scatter_last(kept_0, sent_0), saved_1[0])
    scale_0, normed_mid_0 = normed_of(middle_0)
    terms_1 = product(from_sequence(1, saved_1[0]), out_all, 1, 1)
    first_0 = gather_first(normed_mid_0)
    kept_1, sent_1 = scatter_first(terms_1)
    kept_1, sent_1, first_0 = lax.optimization_barrier((kept_1, sent_1, first_0))
    normed_mid_0 = gather_last(first_0)

    hidden_0, pair_0, grad_terms_0 = feed_forward(0, normed_mid_0)
    middle_1 = input_runs[1] + after(scatter_last(kept_1, sent_1), grad_terms_0)
    scale_1, normed_mid_1 = normed_of(middle_1)
    first_1 = gather_first(normed_mid_1)
    grad_kept_0, grad_sent_0 = scatter_first(grad_terms_0)
    grad_kept_0, grad_sent_0, first_1 = lax.optimization_barrier((grad_kept_0, grad_sent_0, first_1))
    normed_mid_1 = gather_last(first_1)
    hidden_1, pair_1, grad_terms_1 = feed_forward(1, normed_mid_1)
    grad_kept_1, grad_sent_1 = scatter_first(grad_terms_1)
    grad_kept_1, grad_sent_1, grad_terms_0_sum = lax.optimization_barrier(
        (grad_kept_1, grad_sent_1, scatter_last(grad_kept_0, grad_sent_0))
    )
    hidden_0, pair_0, hidden_1, pair_1 = after((hidden_0, pair_0, hidden_1, pair_1), grad_sent_1)
    grad_pairs = product(normed_mid_0, pair_0, 0, 0) + product(normed_mid_1, pair_1, 0, 0)
    grad_terms_1_sum = after(scatter_last(grad_kept_1, grad_sent_1), grad_pairs)
    back_1, gain_1 = norm_back(middle_1, scale_1, gain_ffn, grad_terms_1_sum)
    grad_middle_1 = grad_runs[1].astype(f32) + back_1
    first_1 = gather_first(grad_middle_1.astype(bf16))
    hidden_0, hidden_1 = after((hidden_0, hidden_1), grad_middle_1)
    grad_last = product(grad_all[0], hidden_0, 0, 0) + product(grad_all[1], hidden_1, 0, 0)
    layer_terms = [product(h, w_last, 1, 1, bf16) for h in (hidden_0, hidden_1)]
    back_0, gain_0 = norm_back(middle_0, scale_0, gain_ffn, after(grad_terms_0_sum, grad_middle_1))
    grad_gain_ffn = gain_0 + gain_1
    grad_middle_0 = grad_runs[0].astype(f32) + back_0
    first_1, grad_last, layer_terms, grad_low_0 = lax.optimization_barrier(
        (first_1, grad_last, layer_terms, grad_middle_0.astype(bf16))
    )
    grad_mid_seq_1 = to_sequence(1, gather_last(first_1))
    grad_ffn = narrow(jnp.concatenate([grad_pairs.astype(bf16), grad_last.astype(bf16)], axis=1))

    def mix_backward(r, grad_gated, saved, leave, later):
        return mixer_backward(
            ends, projected[r], *ahead(r), *constants, grad_gated, saved[1:], leave, later,
            heads=heads, rows=BLOCK_ROWS, start=r * run_rows,
        )

    leave = jnp.zeros((heads, DK, DV), f32)
    later = jnp.zeros((8, heads * conv_width), f32)
    first_0 = gather_first(grad_low_0)
    layer_parts = [scatter_first(x) for x in layer_terms]
    grad_gated_1 = product(grad_mid_seq_1, out_all)
    grad_proj_1, *sums_1, leave, later = mix_backward(
        1, after(grad_gated_1, grad_low_0, layer_parts), saved_1, leave, later
    )
    grad_mid_seq_0 = to_sequence(0, gather_last(after(first_0, grad_proj_1)))
    grad_gated_0 = product(grad_mid_seq_0, out_all)
    grad_out_w = product(grad_mid_seq_0, saved_0[0], 0, 0) + product(grad_mid_seq_1, saved_1[0], 0, 0)
    normed_kept_1, normed_sent_1 = scatter_first(from_sequence(1, product(grad_proj_1, mix_all, 1, 1, bf16)))
    layer_sums = [scatter_last(*x) for x in layer_parts]
    layer_rows = [(m + x).astype(bf16) for m, x in zip((middle_0, middle_1), layer_sums)]
    grad_out_w = grad_out_w.astype(bf16)
    grad_gated_0, normed_kept_1, normed_sent_1, layer_rows, grad_out_w, grad_ffn = lax.optimization_barrier(
        (grad_gated_0, normed_kept_1, normed_sent_1, layer_rows, grad_out_w, grad_ffn)
    )
    layer_back = send_back(jnp.concatenate(layer_rows, axis=0))
    grad_proj_0, *sums_0, leave, later = mix_backward(0, grad_gated_0, saved_0, leave, later)
    grad_proj_0, layer_back = lax.optimization_barrier((grad_proj_0, layer_back))
    grad_taps, grad_gain_out, grad_decay = [a + b for a, b in zip(sums_0, sums_1)]
    grad_conv = jnp.sum(grad_taps.reshape(taps, 8, heads, conv_width), axis=1)
    grad_conv = jnp.transpose(grad_conv, (2, 1, 0)).reshape(-1, taps)
    grad_mix = product(seq_0, grad_proj_0, 0, 0) + product(seq_1, grad_proj_1, 0, 0)
    grad_mix = (grad_mix + jnp.pad(grad_conv, ((0, 0), (conv_at, spare)))).astype(bf16)
    grad_mix = jnp.concatenate([grad_mix, grad_out_w], axis=1)
    normed_terms_0 = from_sequence(0, product(after(grad_proj_0, grad_mix), mix_all, 1, 1, bf16))
    grad_mix = narrow(grad_mix)
    normed_sum_1 = scatter_last(normed_kept_1, normed_sent_1)
    grad_normed = jnp.concatenate([scatter_last(*scatter_first(normed_terms_0)), normed_sum_1], axis=0)
    grad_input_norm, grad_gain_attn = norm_back(input_f32, input_scale, gain_attn, grad_normed)
    grad_middle = jnp.concatenate([grad_middle_0, grad_middle_1], axis=0)
    input_grad = unpack(send_back((grad_middle + grad_input_norm).astype(bf16)))
    layer_out = unpack(layer_back)

    head_total = decay_log.shape[0]
    decay_sums = jnp.sum(grad_decay.reshape(2, 8, 128), axis=1)[:, 1 : 2 * heads : 2]
    decay_full = lax.dynamic_update_slice(jnp.zeros((2, head_total), f32), decay_sums, (0, head_start))
    flat = jnp.concatenate(
        [grad_gain_attn, grad_gain_ffn, jnp.sum(grad_gain_out, axis=0), decay_full.reshape(-1)]
    )
    flat = sum_everywhere(jnp.pad(flat, (0, -flat.shape[0] % 1024)).reshape(8, -1)).reshape(-1)
    at = 0
    sums = []
    for size in (model_width, model_width, gain_out.shape[0], head_total, head_total):
        sums.append(flat[at : at + size])
        at += size
    return (
        layer_out,
        input_grad,
        grad_mix[:, :small_at].reshape(w_mix.shape),
        grad_mix[:, small_at:conv_at].reshape(w_ba.shape),
        grad_mix[:, conv_at : conv_at + taps].reshape(conv_w.shape),
        grad_mix[:, small_at + 128 :].reshape(w_out.shape),
        grad_ffn[:, : 2 * units].reshape(w_gate_up.shape),
        grad_ffn[:, 2 * units :],
        *sums,
    )


def solution(mesh):
    dp, splits = mesh.shape["dp"], mesh.shape["tensor"]
    roles = Mesh(mesh.devices.reshape(dp // splits, splits, splits), ("hi", "lo", "tensor"))
    group = ("hi", "lo")
    rows = P((*group, "tensor"))
    by_head = P(group, "tensor", None)
    by_unit = (P(group, None, "tensor"), P(group, "tensor"))
    return jax.shard_map(
        body,
        mesh=roles,
        in_specs=(rows, rows, P(group), rows, rows, by_head, by_head, by_head, by_head, *by_unit)
        + (P(),) * 5,
        out_specs=(rows, rows, by_head, by_head, by_head, by_head, *by_unit) + (P(),) * 5,
        check_vma=False,
    )
```

```python
import functools
import jax
import jax.numpy as jnp
from jax import lax
from jax.experimental import pallas as pl
from jax.experimental.pallas import tpu as pltpu
from jax.sharding import Mesh
from jax.sharding import PartitionSpec as P

DK = 128
DV = 256
SEQS = 3
CHUNK = 128
epsilon = 1e-06
f32 = jnp.float32
bf16 = jnp.bfloat16


def dot(a, b, ca=1, cb=0):
    return lax.dot_general(a, b, (((ca,), (cb,)), ((), ())), preferred_element_type=f32)


def halves(x):
    high = x.astype(bf16)
    return high, (x - high.astype(f32)).astype(bf16)


def dot1(a, b, ca=1, cb=0):
    return dot(a.astype(bf16), b.astype(bf16), ca, cb)


def dot3(a, b, ca=1, cb=0):
    ah, al = halves(a)
    bh, bl = halves(b)
    return dot(jnp.concatenate([ah, al, ah], axis=ca), jnp.concatenate([bh, bh, bl], axis=cb), ca, cb)


def dot_exact(a, b, ca=1, cb=0):
    ah = a.astype(bf16)
    bh, bl = halves(b)
    bt = (b - bh.astype(f32) - bl.astype(f32)).astype(bf16)
    return dot(ah, bh, ca, cb) + (dot(ah, bl, ca, cb) + dot(ah, bt, ca, cb))


def sigmoid(x):
    return 1.0 / (1.0 + jnp.exp(-x))


def segment_of(position, ends):
    return sum((position >= e).astype(jnp.int32) for e in ends)


def iota(shape, axis):
    return lax.broadcasted_iota(jnp.int32, shape, axis)


def conv_masks(base, rows, ends, taps, sign):
    t = base + iota((rows, 1), 0)
    own = segment_of(t, ends)
    masks = []
    for j in range(1, taps):
        other = t - sign * j
        same = segment_of(other, ends) == own
        masks.append(jnp.where(same & (other >= 0), 1.0, 0.0))
    return masks


def chunk_terms(base, ends, g_col, g_row, q, k, beta):
    c = CHUNK
    ti = base + iota((c, 1), 0)
    tj = base + iota((1, c), 1)
    si = segment_of(ti, ends)
    sj = segment_of(tj, ends)
    ii = iota((c, c), 0)
    jj = iota((c, c), 1)
    decay = jnp.where((si == sj) & (ii >= jj), jnp.exp(jnp.minimum(g_col - g_row, 0.0)), 0.0)
    before = jnp.where(base > 0, segment_of(base - 1, ends), -1)
    last = segment_of(base + c - 1, ends)
    carry = jnp.where(si == before, jnp.exp(g_col), 0.0)
    g_last = g_col[c - 1 :, :]
    tail = jnp.where(si == last, jnp.exp(jnp.minimum(g_last - g_col, 0.0)), 0.0)
    return decay, carry, tail, ii, jj


def invert(lower, ii, jj, mul):
    first = ((ii ^ jj) == 1) & (ii > jj)
    eye = jnp.where(ii == jj, 1.0, 0.0)
    inv = [eye - jnp.where(first, a, 0.0) for a in lower]
    size = 2
    while size < CHUNK:
        joins = ((ii // (2 * size)) == (jj // (2 * size))) & ((ii & size) != 0) & ((jj & size) == 0)
        half = [mul(jnp.where(joins, a, 0.0), t) for a, t in zip(lower, inv)]
        inv = [t - mul(t, x) for t, x in zip(inv, half)]
        size *= 2
    return inv


def silu_parts(u):
    s = sigmoid(u)
    return u * s, s


def forward_kernel(
    ends_ref, proj_ref, before_ref, taps_ref, rate_ref, shift_ref, gain_ref, enter_ref,
    gated_ref, o_ref, u_ref, s_ref, t_ref, qe_ref, m_ref, state,
    xs, *, heads, rows, taps, start,
):
    i = pl.program_id(0)
    wide = 2 * DK + DV
    full = wide + DV
    ends = [ends_ref[k] for k in range(SEQS)]
    base = start + i * rows
    c = CHUNK

    @pl.when(i == 0)
    def _():
        for h in range(heads):
            xs[0:8, h * wide : (h + 1) * wide] = before_ref[:, h * full : h * full + wide]
        state[...] = enter_ref[...]

    @pl.when(i > 0)
    def _():
        xs[0:8, :] = xs[rows : rows + 8, :]

    for h in range(heads):
        xs[8:, h * wide : (h + 1) * wide] = proj_ref[:, h * full : h * full + wide]
    small = proj_ref[:, heads * full :]
    beta_all = sigmoid(small)
    shifted = small + shift_ref[...]
    ld_all = -jnp.exp(rate_ref[...]) * (jnp.maximum(shifted, 0.0) + jnp.log1p(jnp.exp(-jnp.abs(shifted))))
    masks = conv_masks(base, rows, ends, taps, 1)
    qs, ks, vs = [], [], []
    for h in range(heads):
        sl = slice(h * wide, (h + 1) * wide)
        run = xs[8:, sl] * taps_ref[0:1, sl]
        for j in range(1, taps):
            run = run + (xs[8 - j : 8 - j + rows, sl] * masks[j - 1]) * taps_ref[j : j + 1, sl]
        act = run * sigmoid(run)
        q, k, v = act[:, :DK], act[:, DK : 2 * DK], act[:, 2 * DK :]
        qs.append(q * (lax.rsqrt(jnp.sum(q * q, axis=-1, keepdims=True) + epsilon) * DK ** (-0.5)))
        ks.append(k * lax.rsqrt(jnp.sum(k * k, axis=-1, keepdims=True) + epsilon))
        vs.append(v)
    lower_tri = jnp.where(iota((c, c), 0) >= iota((c, c), 1), 1.0, 0.0)
    n = rows // c
    probs = []
    for b in range(n):
        rs = slice(b * c, (b + 1) * c)
        g_all = dot_exact(lower_tri, ld_all[rs])
        g_t = g_all.T
        for h in range(heads):
            q, k, v = qs[h][rs], ks[h][rs], vs[h][rs]
            beta = beta_all[rs, 2 * h : 2 * h + 1]
            g_col = g_all[:, 2 * h + 1 : 2 * h + 2]
            g_row = g_t[2 * h + 1 : 2 * h + 2, :]
            decay, carry, tail, ii, jj = chunk_terms(base + b * c, ends, g_col, g_row, q, k, beta)
            qkk = DOT_QK(jnp.concatenate([q, k], axis=0), k, 1, 1)
            p = qkk[:c] * decay
            a = jnp.where(ii > jj, qkk[c:] * decay, 0.0) * beta
            probs.append(dict(b=b, h=h, q=q, k=k, v=v, beta=beta, carry=carry, tail=tail, p=p, a=a))
    inv = invert([x["a"] for x in probs], ii, jj, DOT_INV)
    for x, t in zip(probs, inv):
        x["t"] = t
        rhs = jnp.concatenate([(x["beta"] * x["carry"]) * x["k"], x["beta"] * x["v"]], axis=1)
        x["wv"] = DOT_WV(t, rhs)
    for x in probs:
        pwv = DOT_P(x["p"], x["wv"])
        x["qe"] = x["carry"] * x["q"] - pwv[:, :DK]
        x["pv"] = pwv[:, DK:]
        kwv = DOT_K(x["tail"] * x["k"], x["wv"], 0, 0)
        c_last = x["carry"][c - 1 :, :]
        x["m"] = jnp.where(ii == jj, c_last, 0.0) - kwv[:, :DK]
        x["bf"] = kwv[:, DK:]
    for x in probs:
        b, h = x["b"], x["h"]
        s = state[h]
        s_ref[b, h] = s
        t_ref[b, h] = x["t"]
        qe_ref[b, h] = x["qe"]
        m_ref[b, h] = x["m"]
        w = x["wv"][:, :DK]
        state[h] = x["bf"] + DOT_S(x["m"], s)
        wq = DOT_O(jnp.concatenate([w, x["qe"]], axis=0), s)
        u_ref[b * c : (b + 1) * c, h * DV : (h + 1) * DV] = x["wv"][:, DK:] - wq[:c]
        o_ref[b * c : (b + 1) * c, h * DV : (h + 1) * DV] = x["pv"] + wq[c:]
    live = jnp.where(segment_of(base + iota((rows, 1), 0), ends) < SEQS, 1.0, 0.0)
    for h in range(heads):
        o = o_ref[:, h * DV : (h + 1) * DV]
        z = proj_ref[:, h * full + wide : (h + 1) * full]
        r = lax.rsqrt(jnp.mean(o * o, axis=-1, keepdims=True) + epsilon)
        gated_ref[:, h * DV : (h + 1) * DV] = (o * (r * live) * gain_ref[...] * (z * sigmoid(z))).astype(bf16)


def backward_kernel(
    ends_ref, proj_ref, halo_ref, before_ref, taps_ref, rate_ref, shift_ref, gain_ref,
    dgated_ref, o_ref, u_ref, s_ref, t_ref, qe_ref, m_ref, leave_ref, later_ref,
    dproj_ref, dtaps_ref, dgain_ref, ddecay_ref, dstate, first_ref,
    xs, ds, *, heads, rows, taps, blocks, start,
):
    step = pl.program_id(0)
    i = blocks - 1 - step
    wide = 2 * DK + DV
    full = wide + DV
    ends = [ends_ref[k] for k in range(SEQS)]
    base = start + i * rows
    c = CHUNK

    @pl.when(step == 0)
    def _():
        ds[rows : rows + 8, :] = later_ref[...]
        dstate[...] = leave_ref[...]
        dtaps_ref[...] = jnp.zeros_like(dtaps_ref)
        dgain_ref[...] = jnp.zeros_like(dgain_ref)
        ddecay_ref[...] = jnp.zeros_like(ddecay_ref)

    @pl.when(step > 0)
    def _():
        ds[rows : rows + 8, :] = ds[0:8, :]

    for h in range(heads):
        cols = slice(h * full, h * full + wide)
        xs[0:8, h * wide : (h + 1) * wide] = jnp.where(i == 0, before_ref[:, cols], halo_ref[:, cols])
        xs[8:, h * wide : (h + 1) * wide] = proj_ref[:, h * full : h * full + wide]
    small = proj_ref[:, heads * full :]
    beta_all = sigmoid(small)
    shifted = small + shift_ref[...]
    rate = -jnp.exp(rate_ref[...])
    ld_all = rate * (jnp.maximum(shifted, 0.0) + jnp.log1p(jnp.exp(-jnp.abs(shifted))))
    masks = conv_masks(base, rows, ends, taps, 1)
    live = jnp.where(segment_of(base + iota((rows, 1), 0), ends) < SEQS, 1.0, 0.0)
    acts = []
    dos = []
    for h in range(heads):
        sl = slice(h * wide, (h + 1) * wide)
        run = xs[8:, sl] * taps_ref[0:1, sl]
        for j in range(1, taps):
            run = run + (xs[8 - j : 8 - j + rows, sl] * masks[j - 1]) * taps_ref[j : j + 1, sl]
        sg = sigmoid(run)
        act = run * sg
        dact = sg * (1.0 + run * (1.0 - sg))
        q, k, v = act[:, :DK], act[:, DK : 2 * DK], act[:, 2 * DK :]
        rq = lax.rsqrt(jnp.sum(q * q, axis=-1, keepdims=True) + epsilon)
        rk = lax.rsqrt(jnp.sum(k * k, axis=-1, keepdims=True) + epsilon)
        acts.append((q * rq, k * rk, v, dact, rq, rk))
        o = o_ref[:, h * DV : (h + 1) * DV]
        z = proj_ref[:, h * full + wide : (h + 1) * full]
        dg = dgated_ref[:, h * DV : (h + 1) * DV] * live
        r = lax.rsqrt(jnp.mean(o * o, axis=-1, keepdims=True) + epsilon)
        nrm = o * r
        sz = sigmoid(z)
        dz = dg * nrm * gain_ref[...] * (sz * (1.0 + z * (1.0 - sz)))
        dng = dg * (z * sz)
        dgain_ref[...] += jnp.sum((dng * nrm).reshape(rows // 8, 8, DV), axis=0)
        dn = dng * gain_ref[...]
        dos.append(r * (dn - nrm * jnp.mean(dn * nrm, axis=-1, keepdims=True)))
        dproj_ref[:, h * full + wide : (h + 1) * full] = dz.astype(bf16)
    low_i = iota((c, c), 0)
    low_j = iota((c, c), 1)
    lower_tri = jnp.where(low_i >= low_j, 1.0, 0.0)
    upper_tri = jnp.where(low_i <= low_j, 1.0, 0.0)
    strict_low = jnp.where(low_i > low_j, 1.0, 0.0)
    n = rows // c
    probs = []
    for b in reversed(range(n)):
        rs = slice(b * c, (b + 1) * c)
        g_all = dot_exact(lower_tri, ld_all[rs])
        g_t = g_all.T
        for h in range(heads):
            q, k, v = acts[h][0][rs] * DK ** (-0.5), acts[h][1][rs], acts[h][2][rs]
            beta = beta_all[rs, 2 * h : 2 * h + 1]
            g_col = g_all[:, 2 * h + 1 : 2 * h + 2]
            g_row = g_t[2 * h + 1 : 2 * h + 2, :]
            decay, carry, tail, ii, jj = chunk_terms(base + b * c, ends, g_col, g_row, q, k, beta)
            qkk = DOT_QK(jnp.concatenate([q, k], axis=0), k, 1, 1)
            p = qkk[:c] * decay
            dkk = jnp.where(ii > jj, qkk[c:] * decay, 0.0)
            do = dos[h][rs]
            u = u_ref[rs, h * DV : (h + 1) * DV]
            dp = DOT_B(do, u, 1, 1)
            pdo = DOT_B(p, do, 0, 0)
            qdo = DOT_B(qe_ref[b, h], do, 0, 0)
            f = DOT_B(do, s_ref[b, h], 1, 1)
            probs.append(dict(b=b, h=h, q=q, k=k, v=v, beta=beta, carry=carry, tail=tail, decay=decay, p=p, dkk=dkk,
                              do=do, u=u, dp=dp, pdo=pdo, qdo=qdo, f=f))
    for x in probs:
        b, h = x["b"], x["h"]
        dnext = dstate[h]
        x["dnext"] = dnext
        dstate[h] = DOT_S(m_ref[b, h], dnext, 0, 0) + x["qdo"]
    for x in probs:
        du = x["pdo"] + DOT_B(x["tail"] * x["k"], x["dnext"])
        x["dr"] = DOT_B(t_ref[x["b"], x["h"]], du, 0, 0)
        x["j"] = DOT_B(x["u"], x["dnext"], 1, 1)
    dq_all = [[None] * n for _ in range(heads)]
    dk_all = [[None] * n for _ in range(heads)]
    dv_all = [[None] * n for _ in range(heads)]
    dsmall = [[None] * heads for _ in range(n)]
    lane = iota((c, DK), 1)
    for x in probs:
        b, h, q, k, beta, carry = x["b"], x["h"], x["q"], x["k"], x["beta"], x["carry"]
        dr = x["dr"]
        s = s_ref[b, h]
        neg = DOT_B(dr, x["u"], 1, 1)
        hh = DOT_B(dr, s, 1, 1)
        neg = jnp.where(ii > jj, neg, 0.0)
        adk = neg * x["dkk"]
        dbeta = (
            jnp.sum(dr * x["v"], axis=-1, keepdims=True)
            - carry * jnp.sum(k * hh, axis=-1, keepdims=True)
            - jnp.sum(adk, axis=-1, keepdims=True)
        )
        dcarry = jnp.sum(q * x["f"], axis=-1, keepdims=True) - beta * jnp.sum(k * hh, axis=-1, keepdims=True)
        e = x["dp"] * x["p"] - beta * adk
        dqk = x["dp"] * x["decay"]
        dkk = -(neg * beta) * jnp.where(ii > jj, x["decay"], 0.0)
        dtail = x["tail"] * jnp.sum(k * x["j"], axis=-1, keepdims=True)
        dcl = carry[c - 1 :, :] * jnp.sum(x["dnext"] * s, keepdims=True)
        col = carry * dcarry + jnp.where(iota((c, 1), 0) == c - 1, dcl, 0.0)
        straddle = jnp.where(ii > jj, dot_exact(upper_tri, e), 0.0)
        both = dot_exact(upper_tri, jnp.where(lane == 0, col, 0.0)) + dot_exact(
            strict_low, jnp.where(lane == 0, dtail, 0.0)
        )
        dld = jnp.sum(straddle, axis=-1, keepdims=True) + both[:, 0:1]
        dq_all[h][b] = carry * x["f"] + DOT_G(dqk, k)
        dk_all[h][b] = (
            x["tail"] * x["j"] - (carry * beta) * hh + DOT_G(dqk, q, 0, 0) + DOT_G(dkk, k) + DOT_G(dkk, k, 0, 0)
        )
        dv_all[h][b] = beta * dr
        dsmall[b][h] = (dbeta, dld)
    for b in range(n):
        rs = slice(b * c, (b + 1) * c)
        tile = jnp.zeros((c, DK), f32)
        for h in range(heads):
            dbeta, dld = dsmall[b][h]
            tile = jnp.where(lane == 2 * h, dbeta, jnp.where(lane == 2 * h + 1, dld, tile))
        bet = beta_all[rs]
        dshift = rate * tile * sigmoid(shifted[rs])
        even = (lane & 1) == 0
        inside = lane < 2 * heads
        ddecay_ref[0:8, :] += jnp.sum(jnp.where(even, 0.0, tile * ld_all[rs]).reshape(c // 8, 8, DK), axis=0)
        ddecay_ref[8:16, :] += jnp.sum(jnp.where(even, 0.0, dshift).reshape(c // 8, 8, DK), axis=0)
        dproj_ref[rs, heads * full :] = jnp.where(
            inside, jnp.where(even, tile * (bet * (1.0 - bet)), dshift), 0.0
        ).astype(bf16)
    for h in range(heads):
        qn, kn, v, dact, rq, rk = acts[h]
        dq = jnp.concatenate(dq_all[h], axis=0) * DK ** (-0.5)
        dk = jnp.concatenate(dk_all[h], axis=0)
        dq = rq * (dq - qn * jnp.sum(dq * qn, axis=-1, keepdims=True))
        dk = rk * (dk - kn * jnp.sum(dk * kn, axis=-1, keepdims=True))
        dv = jnp.concatenate(dv_all[h], axis=0)
        o = h * wide
        ds[0:rows, o : o + DK] = dq * dact[:, :DK]
        ds[0:rows, o + DK : o + 2 * DK] = dk * dact[:, DK : 2 * DK]
        ds[0:rows, o + 2 * DK : o + wide] = dv * dact[:, 2 * DK :]
    ahead = conv_masks(base, rows, ends, taps, -1)
    for h in range(heads):
        sl = slice(h * wide, (h + 1) * wide)
        own = ds[0:rows, sl]
        total = own * taps_ref[0:1, sl]
        dtaps_ref[0:8, sl] += jnp.sum((own * xs[8:, sl]).reshape(rows // 8, 8, wide), axis=0)
        for j in range(1, taps):
            total = total + (ds[j : j + rows, sl] * ahead[j - 1]) * taps_ref[j : j + 1, sl]
            dtaps_ref[8 * j : 8 * j + 8, sl] += jnp.sum(
                (own * (xs[8 - j : 8 - j + rows, sl] * masks[j - 1])).reshape(rows // 8, 8, wide), axis=0
            )
        dproj_ref[:, h * full : h * full + wide] = total.astype(bf16)
    first_ref[...] = ds[0:8, :]


DOT_QK = dot3
DOT_INV = dot3
DOT_WV = dot3
DOT_P = dot3
DOT_K = dot3
DOT_S = dot3
DOT_O = dot3
DOT_B = dot3
DOT_G = dot1


def mixer_forward(ends, proj, before, before_at, taps, rate, shift, gain, enter, *, heads, rows, start):
    total, width = proj.shape
    blocks = total // rows
    n = rows // CHUNK
    row = lambda i, e: (i, 0)
    same = lambda i, e: (0, 0)
    quad = lambda i, e: (i, 0, 0, 0)
    wide = 2 * DK + DV
    chunks = total // CHUNK
    kernel = functools.partial(forward_kernel, heads=heads, rows=rows, taps=taps.shape[0], start=start)
    wide_rows = pl.BlockSpec((rows, heads * DV), row)
    return pl.pallas_call(
        kernel,
        grid_spec=pltpu.PrefetchScalarGridSpec(
            num_scalar_prefetch=1,
            grid=(blocks,),
            in_specs=[
                pl.BlockSpec((rows, width), row),
                pl.BlockSpec((8, width), lambda i, e: (before_at, 0)),
                pl.BlockSpec(taps.shape, same),
                pl.BlockSpec(rate.shape, same),
                pl.BlockSpec(shift.shape, same),
                pl.BlockSpec(gain.shape, same),
                pl.BlockSpec(enter.shape, lambda i, e: (0, 0, 0)),
            ],
            out_specs=[
                wide_rows,
                wide_rows,
                wide_rows,
                pl.BlockSpec((n, heads, DK, DV), quad),
                pl.BlockSpec((n, heads, CHUNK, CHUNK), quad),
                pl.BlockSpec((n, heads, CHUNK, DK), quad),
                pl.BlockSpec((n, heads, DK, DK), quad),
                pl.BlockSpec(enter.shape, lambda i, e: (0, 0, 0)),
            ],
            scratch_shapes=[pltpu.VMEM((rows + 8, heads * wide), f32)],
        ),
        out_shape=[
            jax.ShapeDtypeStruct((total, heads * DV), bf16),
            jax.ShapeDtypeStruct((total, heads * DV), f32),
            jax.ShapeDtypeStruct((total, heads * DV), f32),
            jax.ShapeDtypeStruct((chunks, heads, DK, DV), f32),
            jax.ShapeDtypeStruct((chunks, heads, CHUNK, CHUNK), f32),
            jax.ShapeDtypeStruct((chunks, heads, CHUNK, DK), f32),
            jax.ShapeDtypeStruct((chunks, heads, DK, DK), f32),
            jax.ShapeDtypeStruct(enter.shape, f32),
        ],
        compiler_params=pltpu.CompilerParams(
            dimension_semantics=("arbitrary",), vmem_limit_bytes=56 * 1024 * 1024
        ),
        cost_estimate=pl.CostEstimate(
            flops=total * heads * 1_000_000, bytes_accessed=total * heads * 9_000, transcendentals=total * heads * 2_000
        ),
        name="mixer_forward",
    )(ends, proj, before, taps, rate, shift, gain, enter)


def mixer_backward(
    ends, proj, before, before_at, taps, rate, shift, gain, dgated, saved, leave, later, *, heads, rows, start
):
    total, width = proj.shape
    blocks = total // rows
    n = rows // CHUNK
    row = lambda s, e: (blocks - 1 - s, 0)
    halo = lambda s, e: (jnp.maximum((blocks - 1 - s) * (rows // 8) - 1, 0), 0)
    same = lambda s, e: (0, 0)
    quad = lambda s, e: (blocks - 1 - s, 0, 0, 0)
    wide = 2 * DK + DV
    kernel = functools.partial(
        backward_kernel, heads=heads, rows=rows, taps=taps.shape[0], blocks=blocks, start=start
    )
    wide_rows = pl.BlockSpec((rows, heads * DV), row)
    return pl.pallas_call(
        kernel,
        grid_spec=pltpu.PrefetchScalarGridSpec(
            num_scalar_prefetch=1,
            grid=(blocks,),
            in_specs=[
                pl.BlockSpec((rows, width), row),
                pl.BlockSpec((8, width), halo),
                pl.BlockSpec((8, width), lambda s, e: (before_at, 0)),
                pl.BlockSpec(taps.shape, same),
                pl.BlockSpec(rate.shape, same),
                pl.BlockSpec(shift.shape, same),
                pl.BlockSpec(gain.shape, same),
                wide_rows,
                wide_rows,
                wide_rows,
                pl.BlockSpec((n, heads, DK, DV), quad),
                pl.BlockSpec((n, heads, CHUNK, CHUNK), quad),
                pl.BlockSpec((n, heads, CHUNK, DK), quad),
                pl.BlockSpec((n, heads, DK, DK), quad),
                pl.BlockSpec(leave.shape, lambda s, e: (0, 0, 0)),
                pl.BlockSpec(later.shape, same),
            ],
            out_specs=[
                pl.BlockSpec((rows, width), row),
                pl.BlockSpec((8 * taps.shape[0], heads * wide), same),
                pl.BlockSpec((8, DV), same),
                pl.BlockSpec((16, 128), same),
                pl.BlockSpec(leave.shape, lambda s, e: (0, 0, 0)),
                pl.BlockSpec(later.shape, same),
            ],
            scratch_shapes=[
                pltpu.VMEM((rows + 8, heads * wide), f32),
                pltpu.VMEM((rows + 8, heads * wide), f32),
            ],
        ),
        out_shape=[
            jax.ShapeDtypeStruct((total, width), bf16),
            jax.ShapeDtypeStruct((8 * taps.shape[0], heads * wide), f32),
            jax.ShapeDtypeStruct((8, DV), f32),
            jax.ShapeDtypeStruct((16, 128), f32),
            jax.ShapeDtypeStruct(leave.shape, f32),
            jax.ShapeDtypeStruct(later.shape, f32),
        ],
        compiler_params=pltpu.CompilerParams(
            dimension_semantics=("arbitrary",), vmem_limit_bytes=56 * 1024 * 1024
        ),
        cost_estimate=pl.CostEstimate(
            flops=total * heads * 1_000_000, bytes_accessed=total * heads * 9_000, transcendentals=total * heads * 2_000
        ),
        name="mixer_backward",
    )(ends, proj, proj, before, taps, rate, shift, gain, dgated, *saved, leave, later)


FORWARD_ROWS = 512
BACKWARD_ROWS = 256
RUNS = 2


def rms_scale(values):
    return lax.rsqrt(jnp.mean(values * values, axis=-1, keepdims=True) + epsilon)


def norm_back(values, scale, gain, grad):
    u = gain * grad
    back = scale * u - values * (scale * scale * scale) * jnp.mean(values * u, axis=-1, keepdims=True)
    return back, jnp.sum(grad * (values * scale), axis=0)


def swap(x, axis, bit):
    size = lax.axis_size(axis)
    return lax.ppermute(x, axis, [(i, i ^ bit) for i in range(size)])


def exchange_roles(x):
    n = lax.axis_size("lo")
    return lax.ppermute(x, ("lo", "tensor"), [(a * n + b, b * n + a) for a in range(n) for b in range(n)])


def bits(size):
    return [1 << k for k in range(size.bit_length() - 1)]


def reversed_bits(n):
    order = [0]
    for bit in reversed(bits(n)):
        order = order + [k ^ bit for k in order]
    return order


def gather_first(x):
    return jnp.concatenate([x, swap(x, "lo", bits(lax.axis_size("lo"))[-1])], axis=0)


def gather_last(x):
    for bit in reversed(bits(lax.axis_size("lo"))[:-1]):
        x = jnp.concatenate([x, swap(x, "lo", bit)], axis=0)
    return x


def gather_rows(x):
    return gather_last(gather_first(x))


def halve(x, bit, kind):
    half = x.shape[0] // 2
    return x[:half].astype(f32) + swap(x[half:].astype(kind), "lo", bit).astype(f32)


def scatter_first(x):
    kind = x.dtype
    for bit in bits(lax.axis_size("lo"))[:-1]:
        x = halve(x, bit, kind)
    half = x.shape[0] // 2
    return x[:half], x[half:].astype(kind)


def scatter_last(kept, sent):
    return kept + swap(sent, "lo", bits(lax.axis_size("lo"))[-1]).astype(f32)


def sum_everywhere(x):
    for axis in ("lo", "tensor", "hi"):
        for bit in bits(lax.axis_size(axis)):
            x = x + swap(x, axis, bit)
    return x


def rank_of(key):
    return jnp.sum((key[..., None, :] < key[..., :, None]).astype(jnp.int32), axis=-1)


def after(x, *first):
    return lax.optimization_barrier((x, first))[0]


def widen(columns):
    return lax.all_gather(columns, ("hi", "tensor"), axis=0, tiled=True)


def narrow(columns):
    return lax.psum_scatter(columns.astype(bf16), ("hi", "tensor"), scatter_dimension=0, tiled=True)


def product(a, b, ca=1, cb=0, dtype=f32):
    return lax.dot_general(a, b, (((ca,), (cb,)), ((), ())), preferred_element_type=f32).astype(dtype)


def body(
    tokens,
    cotangent,
    lengths,
    token_order,
    token_return,
    w_mix,
    w_ba,
    conv_w,
    w_out,
    w_gate_up,
    w_down,
    gain_attn,
    gain_ffn,
    gain_out,
    decay_log,
    decay_bias,
):
    splits = lax.axis_size("lo")
    groups = lax.axis_size("hi") * splits
    me = lax.axis_index("lo")
    local_rows, model_width = tokens.shape
    group_rows = local_rows * splits
    per_peer = local_rows // groups
    weight_rows, heads, head_width = w_mix.shape
    units = w_down.shape[1]
    taps = conv_w.shape[2]
    conv_width = head_width - DV
    proj_width = heads * head_width

    spread = ("hi", "tensor")
    width = lax.axis_size("hi")
    span = jnp.arange(local_rows, dtype=jnp.int32)
    part_rows = width * per_peer

    send_rank = rank_of(token_return // group_rows * local_rows + token_return % local_rows)
    send_hot = (span[:, None] == send_rank[None, :]).astype(bf16)

    def across(rows):
        return lax.all_to_all(rows, spread, split_axis=0, concat_axis=0, tiled=True)

    def pack(rows):
        return product(send_hot, rows, dtype=bf16).reshape(groups, per_peer, -1)

    def by_part(rows):
        rows = jnp.transpose(rows.reshape(width, splits, per_peer, -1), (1, 0, 2, 3))
        return rows.reshape(local_rows, -1)

    def from_part(rows):
        rows = jnp.transpose(rows.reshape(splits, width, per_peer, model_width), (1, 0, 2, 3))
        return rows.reshape(groups, per_peer, model_width)

    def unpack(rows):
        return product(send_hot, rows.reshape(local_rows, model_width), 0, 0, bf16)

    place = token_return % local_rows
    lane = jnp.arange(128, dtype=jnp.int32)[None, :]
    digits = jnp.where(lane == 0, (place // 16)[:, None], jnp.where(lane == 1, (place % 16)[:, None], 0))
    tagged = jnp.concatenate([tokens, digits.astype(bf16)], axis=1)
    arrived = across(pack(tagged))
    packed_grad = across(pack(after(cotangent, arrived)))
    run_parts = splits // RUNS
    run_rows = run_parts * local_rows

    def in_parts(rows):
        rows = rows.reshape(splits, run_parts, part_rows, -1)
        return jnp.transpose(rows, (1, 0, 2, 3)).reshape(run_parts, local_rows, -1)

    def order_of(tags):
        tags = in_parts(tags)[:, :, :2].astype(jnp.int32)
        at = tags[:, :, 0] * 16 + tags[:, :, 1]
        return (at[:, None, :] == span[None, :, None]).astype(bf16)

    def to_sequence(order, rows):
        return lax.dot_general(
            order, in_parts(rows), (((2,), (1,)), ((0,), (0,))), preferred_element_type=f32
        ).astype(bf16).reshape(run_rows, -1)

    def from_sequence(order, rows):
        rows = lax.dot_general(
            order, rows.reshape(run_parts, local_rows, -1), (((1,), (1,)), ((0,), (0,))),
            preferred_element_type=f32,
        ).astype(bf16).reshape(run_parts, splits, part_rows, -1)
        return jnp.transpose(rows, (1, 0, 2, 3)).reshape(run_rows, -1)

    head_start = me * heads
    lanes = jnp.zeros((1, 128), f32)
    rate_row = lanes.at[0, 1 : 2 * heads : 2].set(lax.dynamic_slice_in_dim(decay_log, head_start, heads))
    shift_row = lanes.at[0, 1 : 2 * heads : 2].set(lax.dynamic_slice_in_dim(decay_bias, head_start, heads))
    own_lengths = exchange_roles(lengths)
    ends = jnp.sum(jnp.where(jnp.tri(SEQS, dtype=bool), own_lengths, 0), axis=1).astype(jnp.int32)
    small_at = proj_width
    conv_at = small_at + heads * w_ba.shape[2]
    spare = 128 - heads * w_ba.shape[2] - taps
    mix_own = exchange_roles(
        jnp.concatenate(
            [
                w_mix.reshape(weight_rows, proj_width).astype(bf16),
                w_ba.reshape(weight_rows, -1).astype(bf16),
                conv_w.reshape(weight_rows, taps).astype(bf16),
                jnp.zeros((weight_rows, spare), bf16),
                w_out.reshape(weight_rows, heads * DV).astype(bf16),
            ],
            axis=1,
        )
    )
    mix_all = widen(mix_own)
    arrived = by_part(after(arrived, ends, rate_row, shift_row))
    packed_in, tags = arrived[:, :model_width], arrived[:, model_width:]
    runs = range(RUNS)
    own_rows = local_rows // RUNS

    def split(rows):
        return [rows[r * own_rows : (r + 1) * own_rows] for r in runs]

    input_f32 = packed_in.astype(f32)
    input_scale = rms_scale(input_f32)
    input_runs = split(input_f32)
    normed_runs = split(jnp.concatenate([(input_f32 * input_scale * gain_attn).astype(bf16), tags], axis=1))
    gathered_0 = gather_rows(normed_runs[0])
    ffn_sent = jnp.concatenate(
        [w_gate_up.reshape(weight_rows, 2 * units).astype(bf16), w_down.astype(bf16)], axis=1
    )
    out_all = mix_all[:, small_at + 128 :]
    mix_all = mix_all[:, : small_at + 128]

    conv_all = mix_all[:, conv_at : conv_at + taps].reshape(-1, heads, taps).astype(f32)
    tap_rows = jnp.transpose(conv_all, (2, 1, 0)).reshape(taps, heads * conv_width)
    gain_row = gain_out[None]
    constants = (tap_rows, rate_row, shift_row, gain_row)

    state = jnp.zeros((heads, DK, DV), f32)

    def ahead(r):
        return (projected[r - 1], run_rows // 8 - 1) if r else (projected[r], 0)

    def mix_forward(r, state):
        return mixer_forward(
            ends, projected[r], *ahead(r), *constants, state, heads=heads, rows=FORWARD_ROWS, start=r * run_rows
        )

    def feed_forward(r, normed_mid):
        place = (r * run_parts + jnp.arange(run_parts, dtype=jnp.int32))[:, None, None] * local_rows
        alive = (place + span[None, :, None] < ends[SEQS - 1]).astype(bf16)
        live = from_sequence(orders[r], jnp.broadcast_to(alive, (run_parts, local_rows, 128)))[:, :1].astype(f32)
        grad_hidden = product(grad_all[r], w_last) * live
        gate_up = product(normed_mid, w_pair)
        gate, up = gate_up[:, :units], gate_up[:, units:]
        s = sigmoid(gate)
        hidden = (gate * s * up * live).astype(bf16)
        grad_pair = jnp.concatenate(
            [grad_hidden * up * (s * (1.0 + gate * (1.0 - s))), grad_hidden * (gate * s)], axis=1
        ).astype(bf16)
        return hidden, grad_pair, product(grad_pair, w_pair, 1, 1, bf16)

    def normed_of(middle):
        scale = rms_scale(middle)
        return scale, (middle * scale * gain_ffn).astype(bf16)

    constants = (tap_rows, rate_row, shift_row, gain_row)
    orders = [order_of(gathered_0[:, model_width:])]
    seq_0 = to_sequence(orders[0], gathered_0[:, :model_width])
    projected = [product(seq_0, mix_all)]
    packed_grad = by_part(packed_grad)
    projected[0], normed_runs, ffn_sent, packed_grad = lax.optimization_barrier(
        (projected[0], normed_runs, ffn_sent, packed_grad)
    )
    *saved_0, state = mix_forward(0, state)
    crossed = swap(packed_grad, "lo", bits(splits)[-1])
    saved_0, first_1, ffn_own = lax.optimization_barrier(
        (saved_0, gather_first(normed_runs[1]), exchange_roles(ffn_sent))
    )
    ffn_all = widen(ffn_own)
    grad_runs = split(packed_grad)
    gathered_1 = gather_last(first_1)
    terms_0 = product(from_sequence(orders[0], saved_0[0]), out_all, 1, 1)
    gathered_1 = after(gathered_1, terms_0)
    orders.append(order_of(gathered_1[:, model_width:]))
    seq_1 = to_sequence(orders[1], gathered_1[:, :model_width])
    projected.append(product(seq_1, mix_all))
    kept_0, sent_0 = scatter_first(terms_0)
    projected[1], kept_0, sent_0, crossed = lax.optimization_barrier((projected[1], kept_0, sent_0, crossed))
    grad_all = [gather_last(jnp.concatenate(x, axis=0)) for x in zip(grad_runs, split(crossed))]
    *saved_1, state = mix_forward(1, state)
    middle_0 = input_runs[0] + after(scatter_last(kept_0, sent_0), saved_1[0])
    scale_0, normed_mid_0 = normed_of(middle_0)
    terms_1 = product(from_sequence(orders[1], saved_1[0]), out_all, 1, 1)
    first_0 = gather_first(normed_mid_0)
    kept_1, sent_1 = scatter_first(terms_1)
    kept_1, sent_1, first_0, ffn_all = lax.optimization_barrier((kept_1, sent_1, first_0, ffn_all))
    w_pair, w_last = ffn_all[:, : 2 * units], ffn_all[:, 2 * units :]
    normed_mid_0 = gather_last(first_0)

    hidden_0, pair_0, grad_terms_0 = feed_forward(0, normed_mid_0)
    middle_1 = input_runs[1] + after(scatter_last(kept_1, sent_1), grad_terms_0)
    scale_1, normed_mid_1 = normed_of(middle_1)
    first_1 = gather_first(normed_mid_1)
    grad_kept_0, grad_sent_0 = scatter_first(grad_terms_0)
    grad_kept_0, grad_sent_0, first_1 = lax.optimization_barrier((grad_kept_0, grad_sent_0, first_1))
    normed_mid_1 = gather_last(first_1)
    hidden_1, pair_1, grad_terms_1 = feed_forward(1, normed_mid_1)
    grad_kept_1, grad_sent_1 = scatter_first(grad_terms_1)
    grad_kept_1, grad_sent_1, grad_terms_0_sum = lax.optimization_barrier(
        (grad_kept_1, grad_sent_1, scatter_last(grad_kept_0, grad_sent_0))
    )
    hidden_0, pair_0, hidden_1, pair_1 = after((hidden_0, pair_0, hidden_1, pair_1), grad_sent_1)
    grad_pairs = product(normed_mid_0, pair_0, 0, 0) + product(normed_mid_1, pair_1, 0, 0)
    grad_terms_1_sum = after(scatter_last(grad_kept_1, grad_sent_1), grad_pairs)
    back_1, gain_1 = norm_back(middle_1, scale_1, gain_ffn, grad_terms_1_sum)
    grad_middle_1 = grad_runs[1].astype(f32) + back_1
    first_1 = gather_first(grad_middle_1.astype(bf16))
    hidden_0, hidden_1 = after((hidden_0, hidden_1), grad_middle_1)
    grad_last = product(grad_all[0], hidden_0, 0, 0) + product(grad_all[1], hidden_1, 0, 0)
    layer_terms = [product(h, w_last, 1, 1, bf16) for h in (hidden_0, hidden_1)]
    back_0, gain_0 = norm_back(middle_0, scale_0, gain_ffn, after(grad_terms_0_sum, grad_middle_1))
    grad_gain_ffn = gain_0 + gain_1
    grad_middle_0 = grad_runs[0].astype(f32) + back_0
    first_1, grad_last, layer_terms, grad_low_0 = lax.optimization_barrier(
        (first_1, grad_last, layer_terms, grad_middle_0.astype(bf16))
    )
    grad_mid_seq_1 = to_sequence(orders[1], gather_last(first_1))
    grad_ffn = narrow(jnp.concatenate([grad_pairs.astype(bf16), grad_last.astype(bf16)], axis=1))

    def mix_backward(r, grad_gated, saved, leave, later):
        return mixer_backward(
            ends, projected[r], *ahead(r), *constants, grad_gated, saved[1:], leave, later,
            heads=heads, rows=BACKWARD_ROWS, start=r * run_rows,
        )

    leave = jnp.zeros((heads, DK, DV), f32)
    later = jnp.zeros((8, heads * conv_width), f32)
    layer_parts = [scatter_first(x) for x in layer_terms]
    grad_gated_1 = product(grad_mid_seq_1, out_all)
    grad_gated_1, grad_low_0, layer_parts = lax.optimization_barrier((grad_gated_1, grad_low_0, layer_parts))
    grad_proj_1, *sums_1, leave, later = mix_backward(1, grad_gated_1, saved_1, leave, later)
    grad_proj_1, first_0 = lax.optimization_barrier((grad_proj_1, gather_first(grad_low_0)))
    grad_mid_seq_0 = to_sequence(orders[0], gather_last(first_0))
    grad_gated_0 = product(grad_mid_seq_0, out_all)
    grad_gated_0, layer_parts = lax.optimization_barrier((grad_gated_0, layer_parts))
    grad_proj_0, *sums_0, leave, later = mix_backward(0, grad_gated_0, saved_0, leave, later)
    layer_sums = [scatter_last(*x) for x in layer_parts]
    grad_proj_0, grad_ffn, layer_sums = lax.optimization_barrier((grad_proj_0, grad_ffn, layer_sums))
    grad_taps, grad_gain_out, grad_decay = [a + b for a, b in zip(sums_0, sums_1)]
    grad_conv = jnp.sum(grad_taps.reshape(taps, 8, heads, conv_width), axis=1)
    grad_conv = jnp.transpose(grad_conv, (2, 1, 0)).reshape(-1, taps)
    grad_mix = product(seq_0, grad_proj_0, 0, 0) + product(seq_1, grad_proj_1, 0, 0)
    grad_mix = (grad_mix + jnp.pad(grad_conv, ((0, 0), (conv_at, spare)))).astype(bf16)
    grad_out_w = product(grad_mid_seq_0, saved_0[0], 0, 0) + product(grad_mid_seq_1, saved_1[0], 0, 0)
    grad_mix = jnp.concatenate([grad_mix, grad_out_w.astype(bf16)], axis=1)
    layer_rows = jnp.concatenate([m + x for m, x in zip((middle_0, middle_1), layer_sums)], axis=0)
    layer_back = across(from_part(layer_rows.astype(bf16)))
    grad_mix, layer_back, grad_ffn = lax.optimization_barrier((grad_mix, layer_back, exchange_roles(grad_ffn)))
    proj_parts = after((grad_proj_0, grad_proj_1), grad_mix)
    normed_terms = [from_sequence(orders[r], product(proj_parts[r], mix_all, 1, 1, bf16)) for r in runs]
    grad_mix = exchange_roles(narrow(grad_mix)).astype(f32)
    grad_ffn = grad_ffn.astype(f32)
    normed_terms = [x.reshape(splits, own_rows, model_width) for x in normed_terms]
    normed_terms = jnp.concatenate(normed_terms, axis=1).reshape(group_rows, model_width)
    grad_normed = scatter_last(*scatter_first(normed_terms))
    grad_input_norm, grad_gain_attn = norm_back(input_f32, input_scale, gain_attn, grad_normed)
    grad_middle = jnp.concatenate([grad_middle_0, grad_middle_1], axis=0)
    input_grad = unpack(across(from_part((grad_middle + grad_input_norm).astype(bf16))))
    layer_out = unpack(layer_back)

    head_total = decay_log.shape[0]
    decay_sums = jnp.sum(grad_decay.reshape(2, 8, 128), axis=1)[:, 1 : 2 * heads : 2]
    decay_full = lax.dynamic_update_slice(jnp.zeros((2, head_total), f32), decay_sums, (0, head_start))
    flat = jnp.concatenate(
        [grad_gain_attn, grad_gain_ffn, jnp.sum(grad_gain_out, axis=0), decay_full.reshape(-1)]
    )
    flat = sum_everywhere(jnp.pad(flat, (0, -flat.shape[0] % 1024)).reshape(8, -1)).reshape(-1)
    at = 0
    sums = []
    for size in (model_width, model_width, gain_out.shape[0], head_total, head_total):
        sums.append(flat[at : at + size])
        at += size
    return (
        layer_out,
        input_grad,
        grad_mix[:, :small_at].reshape(w_mix.shape),
        grad_mix[:, small_at:conv_at].reshape(w_ba.shape),
        grad_mix[:, conv_at : conv_at + taps].reshape(conv_w.shape),
        grad_mix[:, small_at + 128 :].reshape(w_out.shape),
        grad_ffn[:, : 2 * units].reshape(w_gate_up.shape),
        grad_ffn[:, 2 * units :],
        *sums,
    )


def solution(mesh):
    dp, splits = mesh.shape["dp"], mesh.shape["tensor"]
    roles = Mesh(mesh.devices.reshape(dp // splits, splits, splits), ("hi", "lo", "tensor"))
    group = ("hi", "lo")
    rows = P((*group, "tensor"))
    by_head = P(group, "tensor", None)
    by_unit = (P(group, None, "tensor"), P(group, "tensor"))
    return jax.shard_map(
        body,
        mesh=roles,
        in_specs=(rows, rows, P(group), rows, rows, by_head, by_head, by_head, by_head, *by_unit)
        + (P(),) * 5,
        out_specs=(rows, rows, by_head, by_head, by_head, by_head, *by_unit) + (P(),) * 5,
        check_vma=False,
    )
```

```python
import functools
import jax
import jax.numpy as jnp
from jax import lax
from jax.experimental import pallas as pl
from jax.experimental.pallas import tpu as pltpu
from jax.sharding import Mesh
from jax.sharding import PartitionSpec as P

DK = 128
DV = 256
SEQS = 3
CHUNK = 128
epsilon = 1e-06
f32 = jnp.float32
bf16 = jnp.bfloat16


def dot(a, b, ca=1, cb=0):
    return lax.dot_general(a, b, (((ca,), (cb,)), ((), ())), preferred_element_type=f32)


def halves(x):
    high = x.astype(bf16)
    return high, (x - high.astype(f32)).astype(bf16)


def dot1(a, b, ca=1, cb=0):
    return dot(a.astype(bf16), b.astype(bf16), ca, cb)


def dot3(a, b, ca=1, cb=0):
    ah, al = halves(a)
    bh, bl = halves(b)
    return dot(jnp.concatenate([ah, al, ah], axis=ca), jnp.concatenate([bh, bh, bl], axis=cb), ca, cb)


def dot_exact(a, b, ca=1, cb=0):
    ah = a.astype(bf16)
    bh, bl = halves(b)
    bt = (b - bh.astype(f32) - bl.astype(f32)).astype(bf16)
    return dot(ah, bh, ca, cb) + (dot(ah, bl, ca, cb) + dot(ah, bt, ca, cb))


def sigmoid(x):
    return 1.0 / (1.0 + jnp.exp(-x))


def segment_of(position, ends):
    return sum((position >= e).astype(jnp.int32) for e in ends)


def iota(shape, axis):
    return lax.broadcasted_iota(jnp.int32, shape, axis)


def conv_masks(base, rows, ends, taps, sign):
    t = base + iota((rows, 1), 0)
    own = segment_of(t, ends)
    masks = []
    for j in range(1, taps):
        other = t - sign * j
        same = segment_of(other, ends) == own
        masks.append(jnp.where(same & (other >= 0), 1.0, 0.0))
    return masks


def chunk_terms(base, ends, g_col, g_row, q, k, beta):
    c = CHUNK
    ti = base + iota((c, 1), 0)
    tj = base + iota((1, c), 1)
    si = segment_of(ti, ends)
    sj = segment_of(tj, ends)
    ii = iota((c, c), 0)
    jj = iota((c, c), 1)
    decay = jnp.where((si == sj) & (ii >= jj), jnp.exp(jnp.minimum(g_col - g_row, 0.0)), 0.0)
    before = jnp.where(base > 0, segment_of(base - 1, ends), -1)
    last = segment_of(base + c - 1, ends)
    carry = jnp.where(si == before, jnp.exp(g_col), 0.0)
    g_last = g_col[c - 1 :, :]
    tail = jnp.where(si == last, jnp.exp(jnp.minimum(g_last - g_col, 0.0)), 0.0)
    return decay, carry, tail, ii, jj


def invert(lower, ii, jj, mul):
    first = ((ii ^ jj) == 1) & (ii > jj)
    eye = jnp.where(ii == jj, 1.0, 0.0)
    inv = [eye - jnp.where(first, a, 0.0) for a in lower]
    size = 2
    while size < CHUNK:
        joins = ((ii // (2 * size)) == (jj // (2 * size))) & ((ii & size) != 0) & ((jj & size) == 0)
        half = [mul(jnp.where(joins, a, 0.0), t) for a, t in zip(lower, inv)]
        inv = [t - mul(t, x) for t, x in zip(inv, half)]
        size *= 2
    return inv


def silu_parts(u):
    s = sigmoid(u)
    return u * s, s


def forward_kernel(
    ends_ref, proj_ref, before_ref, taps_ref, rate_ref, shift_ref, gain_ref, enter_ref,
    gated_ref, o_ref, u_ref, s_ref, t_ref, qe_ref, m_ref, state,
    xs, *, heads, rows, taps, start,
):
    i = pl.program_id(0)
    wide = 2 * DK + DV
    full = wide + DV
    ends = [ends_ref[k] for k in range(SEQS)]
    base = start + i * rows
    c = CHUNK

    @pl.when(i == 0)
    def _():
        for h in range(heads):
            xs[0:8, h * wide : (h + 1) * wide] = before_ref[:, h * full : h * full + wide]
        state[...] = enter_ref[...]

    @pl.when(i > 0)
    def _():
        xs[0:8, :] = xs[rows : rows + 8, :]

    for h in range(heads):
        xs[8:, h * wide : (h + 1) * wide] = proj_ref[:, h * full : h * full + wide]
    small = proj_ref[:, heads * full :]
    beta_all = sigmoid(small)
    shifted = small + shift_ref[...]
    ld_all = -jnp.exp(rate_ref[...]) * (jnp.maximum(shifted, 0.0) + jnp.log1p(jnp.exp(-jnp.abs(shifted))))
    masks = conv_masks(base, rows, ends, taps, 1)
    qs, ks, vs = [], [], []
    for h in range(heads):
        sl = slice(h * wide, (h + 1) * wide)
        run = xs[8:, sl] * taps_ref[0:1, sl]
        for j in range(1, taps):
            run = run + (xs[8 - j : 8 - j + rows, sl] * masks[j - 1]) * taps_ref[j : j + 1, sl]
        act = run * sigmoid(run)
        q, k, v = act[:, :DK], act[:, DK : 2 * DK], act[:, 2 * DK :]
        qs.append(q * (lax.rsqrt(jnp.sum(q * q, axis=-1, keepdims=True) + epsilon) * DK ** (-0.5)))
        ks.append(k * lax.rsqrt(jnp.sum(k * k, axis=-1, keepdims=True) + epsilon))
        vs.append(v)
    lower_tri = jnp.where(iota((c, c), 0) >= iota((c, c), 1), 1.0, 0.0)
    n = rows // c
    probs = []
    for b in range(n):
        rs = slice(b * c, (b + 1) * c)
        g_all = dot_exact(lower_tri, ld_all[rs])
        g_t = g_all.T
        for h in range(heads):
            q, k, v = qs[h][rs], ks[h][rs], vs[h][rs]
            beta = beta_all[rs, 2 * h : 2 * h + 1]
            g_col = g_all[:, 2 * h + 1 : 2 * h + 2]
            g_row = g_t[2 * h + 1 : 2 * h + 2, :]
            decay, carry, tail, ii, jj = chunk_terms(base + b * c, ends, g_col, g_row, q, k, beta)
            qkk = DOT_QK(jnp.concatenate([q, k], axis=0), k, 1, 1)
            p = qkk[:c] * decay
            a = jnp.where(ii > jj, qkk[c:] * decay, 0.0) * beta
            probs.append(dict(b=b, h=h, q=q, k=k, v=v, beta=beta, carry=carry, tail=tail, p=p, a=a))
    inv = invert([x["a"] for x in probs], ii, jj, DOT_INV)
    for x, t in zip(probs, inv):
        x["t"] = t
        rhs = jnp.concatenate([(x["beta"] * x["carry"]) * x["k"], x["beta"] * x["v"]], axis=1)
        x["wv"] = DOT_WV(t, rhs)
    for x in probs:
        pwv = DOT_P(x["p"], x["wv"])
        x["qe"] = x["carry"] * x["q"] - pwv[:, :DK]
        x["pv"] = pwv[:, DK:]
        kwv = DOT_K(x["tail"] * x["k"], x["wv"], 0, 0)
        c_last = x["carry"][c - 1 :, :]
        x["m"] = jnp.where(ii == jj, c_last, 0.0) - kwv[:, :DK]
        x["bf"] = kwv[:, DK:]
    for x in probs:
        b, h = x["b"], x["h"]
        s = state[h]
        s_ref[b, h] = s
        t_ref[b, h] = x["t"]
        qe_ref[b, h] = x["qe"]
        m_ref[b, h] = x["m"]
        w = x["wv"][:, :DK]
        state[h] = x["bf"] + DOT_S(x["m"], s)
        wq = DOT_O(jnp.concatenate([w, x["qe"]], axis=0), s)
        u_ref[b * c : (b + 1) * c, h * DV : (h + 1) * DV] = x["wv"][:, DK:] - wq[:c]
        o_ref[b * c : (b + 1) * c, h * DV : (h + 1) * DV] = x["pv"] + wq[c:]
    live = jnp.where(segment_of(base + iota((rows, 1), 0), ends) < SEQS, 1.0, 0.0)
    for h in range(heads):
        o = o_ref[:, h * DV : (h + 1) * DV]
        z = proj_ref[:, h * full + wide : (h + 1) * full]
        r = lax.rsqrt(jnp.mean(o * o, axis=-1, keepdims=True) + epsilon)
        gated_ref[:, h * DV : (h + 1) * DV] = (o * (r * live) * gain_ref[...] * (z * sigmoid(z))).astype(bf16)


def backward_kernel(
    ends_ref, proj_ref, halo_ref, before_ref, taps_ref, rate_ref, shift_ref, gain_ref,
    dgated_ref, o_ref, u_ref, s_ref, t_ref, qe_ref, m_ref, leave_ref, later_ref,
    dproj_ref, dtaps_ref, dgain_ref, ddecay_ref, dstate, first_ref,
    xs, ds, *, heads, rows, taps, blocks, start,
):
    step = pl.program_id(0)
    i = blocks - 1 - step
    wide = 2 * DK + DV
    full = wide + DV
    ends = [ends_ref[k] for k in range(SEQS)]
    base = start + i * rows
    c = CHUNK

    @pl.when(step == 0)
    def _():
        ds[rows : rows + 8, :] = later_ref[...]
        dstate[...] = leave_ref[...]
        dtaps_ref[...] = jnp.zeros_like(dtaps_ref)
        dgain_ref[...] = jnp.zeros_like(dgain_ref)
        ddecay_ref[...] = jnp.zeros_like(ddecay_ref)

    @pl.when(step > 0)
    def _():
        ds[rows : rows + 8, :] = ds[0:8, :]

    for h in range(heads):
        cols = slice(h * full, h * full + wide)
        xs[0:8, h * wide : (h + 1) * wide] = jnp.where(i == 0, before_ref[:, cols], halo_ref[:, cols])
        xs[8:, h * wide : (h + 1) * wide] = proj_ref[:, h * full : h * full + wide]
    small = proj_ref[:, heads * full :]
    beta_all = sigmoid(small)
    shifted = small + shift_ref[...]
    rate = -jnp.exp(rate_ref[...])
    ld_all = rate * (jnp.maximum(shifted, 0.0) + jnp.log1p(jnp.exp(-jnp.abs(shifted))))
    masks = conv_masks(base, rows, ends, taps, 1)
    live = jnp.where(segment_of(base + iota((rows, 1), 0), ends) < SEQS, 1.0, 0.0)
    acts = []
    dos = []
    for h in range(heads):
        sl = slice(h * wide, (h + 1) * wide)
        run = xs[8:, sl] * taps_ref[0:1, sl]
        for j in range(1, taps):
            run = run + (xs[8 - j : 8 - j + rows, sl] * masks[j - 1]) * taps_ref[j : j + 1, sl]
        sg = sigmoid(run)
        act = run * sg
        dact = sg * (1.0 + run * (1.0 - sg))
        q, k, v = act[:, :DK], act[:, DK : 2 * DK], act[:, 2 * DK :]
        rq = lax.rsqrt(jnp.sum(q * q, axis=-1, keepdims=True) + epsilon)
        rk = lax.rsqrt(jnp.sum(k * k, axis=-1, keepdims=True) + epsilon)
        acts.append((q * rq, k * rk, v, dact, rq, rk))
        o = o_ref[:, h * DV : (h + 1) * DV]
        z = proj_ref[:, h * full + wide : (h + 1) * full]
        dg = dgated_ref[:, h * DV : (h + 1) * DV] * live
        r = lax.rsqrt(jnp.mean(o * o, axis=-1, keepdims=True) + epsilon)
        nrm = o * r
        sz = sigmoid(z)
        dz = dg * nrm * gain_ref[...] * (sz * (1.0 + z * (1.0 - sz)))
        dng = dg * (z * sz)
        dgain_ref[...] += jnp.sum((dng * nrm).reshape(rows // 8, 8, DV), axis=0)
        dn = dng * gain_ref[...]
        dos.append(r * (dn - nrm * jnp.mean(dn * nrm, axis=-1, keepdims=True)))
        dproj_ref[:, h * full + wide : (h + 1) * full] = dz.astype(bf16)
    low_i = iota((c, c), 0)
    low_j = iota((c, c), 1)
    lower_tri = jnp.where(low_i >= low_j, 1.0, 0.0)
    upper_tri = jnp.where(low_i <= low_j, 1.0, 0.0)
    strict_low = jnp.where(low_i > low_j, 1.0, 0.0)
    n = rows // c
    probs = []
    for b in reversed(range(n)):
        rs = slice(b * c, (b + 1) * c)
        g_all = dot_exact(lower_tri, ld_all[rs])
        g_t = g_all.T
        for h in range(heads):
            q, k, v = acts[h][0][rs] * DK ** (-0.5), acts[h][1][rs], acts[h][2][rs]
            beta = beta_all[rs, 2 * h : 2 * h + 1]
            g_col = g_all[:, 2 * h + 1 : 2 * h + 2]
            g_row = g_t[2 * h + 1 : 2 * h + 2, :]
            decay, carry, tail, ii, jj = chunk_terms(base + b * c, ends, g_col, g_row, q, k, beta)
            qkk = DOT_QK(jnp.concatenate([q, k], axis=0), k, 1, 1)
            p = qkk[:c] * decay
            dkk = jnp.where(ii > jj, qkk[c:] * decay, 0.0)
            do = dos[h][rs]
            u = u_ref[rs, h * DV : (h + 1) * DV]
            dp = DOT_B(do, u, 1, 1)
            pdo = DOT_B(p, do, 0, 0)
            qdo = DOT_B(qe_ref[b, h], do, 0, 0)
            f = DOT_B(do, s_ref[b, h], 1, 1)
            probs.append(dict(b=b, h=h, q=q, k=k, v=v, beta=beta, carry=carry, tail=tail, decay=decay, p=p, dkk=dkk,
                              do=do, u=u, dp=dp, pdo=pdo, qdo=qdo, f=f))
    for x in probs:
        b, h = x["b"], x["h"]
        dnext = dstate[h]
        x["dnext"] = dnext
        dstate[h] = DOT_S(m_ref[b, h], dnext, 0, 0) + x["qdo"]
    for x in probs:
        du = x["pdo"] + DOT_B(x["tail"] * x["k"], x["dnext"])
        x["dr"] = DOT_B(t_ref[x["b"], x["h"]], du, 0, 0)
        x["j"] = DOT_B(x["u"], x["dnext"], 1, 1)
    dq_all = [[None] * n for _ in range(heads)]
    dk_all = [[None] * n for _ in range(heads)]
    dv_all = [[None] * n for _ in range(heads)]
    dsmall = [[None] * heads for _ in range(n)]
    lane = iota((c, DK), 1)
    for x in probs:
        b, h, q, k, beta, carry = x["b"], x["h"], x["q"], x["k"], x["beta"], x["carry"]
        dr = x["dr"]
        s = s_ref[b, h]
        neg = DOT_B(dr, x["u"], 1, 1)
        hh = DOT_B(dr, s, 1, 1)
        neg = jnp.where(ii > jj, neg, 0.0)
        adk = neg * x["dkk"]
        dbeta = (
            jnp.sum(dr * x["v"], axis=-1, keepdims=True)
            - carry * jnp.sum(k * hh, axis=-1, keepdims=True)
            - jnp.sum(adk, axis=-1, keepdims=True)
        )
        dcarry = jnp.sum(q * x["f"], axis=-1, keepdims=True) - beta * jnp.sum(k * hh, axis=-1, keepdims=True)
        e = x["dp"] * x["p"] - beta * adk
        dqk = x["dp"] * x["decay"]
        dkk = -(neg * beta) * jnp.where(ii > jj, x["decay"], 0.0)
        dtail = x["tail"] * jnp.sum(k * x["j"], axis=-1, keepdims=True)
        dcl = carry[c - 1 :, :] * jnp.sum(x["dnext"] * s, keepdims=True)
        col = carry * dcarry + jnp.where(iota((c, 1), 0) == c - 1, dcl, 0.0)
        straddle = jnp.where(ii > jj, dot_exact(upper_tri, e), 0.0)
        both = dot_exact(upper_tri, jnp.where(lane == 0, col, 0.0)) + dot_exact(
            strict_low, jnp.where(lane == 0, dtail, 0.0)
        )
        dld = jnp.sum(straddle, axis=-1, keepdims=True) + both[:, 0:1]
        dq_all[h][b] = carry * x["f"] + DOT_G(dqk, k)
        dk_all[h][b] = (
            x["tail"] * x["j"] - (carry * beta) * hh + DOT_G(dqk, q, 0, 0) + DOT_G(dkk, k) + DOT_G(dkk, k, 0, 0)
        )
        dv_all[h][b] = beta * dr
        dsmall[b][h] = (dbeta, dld)
    for b in range(n):
        rs = slice(b * c, (b + 1) * c)
        tile = jnp.zeros((c, DK), f32)
        for h in range(heads):
            dbeta, dld = dsmall[b][h]
            tile = jnp.where(lane == 2 * h, dbeta, jnp.where(lane == 2 * h + 1, dld, tile))
        bet = beta_all[rs]
        dshift = rate * tile * sigmoid(shifted[rs])
        even = (lane & 1) == 0
        inside = lane < 2 * heads
        ddecay_ref[0:8, :] += jnp.sum(jnp.where(even, 0.0, tile * ld_all[rs]).reshape(c // 8, 8, DK), axis=0)
        ddecay_ref[8:16, :] += jnp.sum(jnp.where(even, 0.0, dshift).reshape(c // 8, 8, DK), axis=0)
        dproj_ref[rs, heads * full :] = jnp.where(
            inside, jnp.where(even, tile * (bet * (1.0 - bet)), dshift), 0.0
        ).astype(bf16)
    for h in range(heads):
        qn, kn, v, dact, rq, rk = acts[h]
        dq = jnp.concatenate(dq_all[h], axis=0) * DK ** (-0.5)
        dk = jnp.concatenate(dk_all[h], axis=0)
        dq = rq * (dq - qn * jnp.sum(dq * qn, axis=-1, keepdims=True))
        dk = rk * (dk - kn * jnp.sum(dk * kn, axis=-1, keepdims=True))
        dv = jnp.concatenate(dv_all[h], axis=0)
        o = h * wide
        ds[0:rows, o : o + DK] = dq * dact[:, :DK]
        ds[0:rows, o + DK : o + 2 * DK] = dk * dact[:, DK : 2 * DK]
        ds[0:rows, o + 2 * DK : o + wide] = dv * dact[:, 2 * DK :]
    ahead = conv_masks(base, rows, ends, taps, -1)
    for h in range(heads):
        sl = slice(h * wide, (h + 1) * wide)
        own = ds[0:rows, sl]
        total = own * taps_ref[0:1, sl]
        dtaps_ref[0:8, sl] += jnp.sum((own * xs[8:, sl]).reshape(rows // 8, 8, wide), axis=0)
        for j in range(1, taps):
            total = total + (ds[j : j + rows, sl] * ahead[j - 1]) * taps_ref[j : j + 1, sl]
            dtaps_ref[8 * j : 8 * j + 8, sl] += jnp.sum(
                (own * (xs[8 - j : 8 - j + rows, sl] * masks[j - 1])).reshape(rows // 8, 8, wide), axis=0
            )
        dproj_ref[:, h * full : h * full + wide] = total.astype(bf16)
    first_ref[...] = ds[0:8, :]


DOT_QK = dot3
DOT_INV = dot3
DOT_WV = dot3
DOT_P = dot3
DOT_K = dot3
DOT_S = dot3
DOT_O = dot3
DOT_B = dot3
DOT_G = dot1


def mixer_forward(ends, proj, before, before_at, taps, rate, shift, gain, enter, *, heads, rows, start):
    total, width = proj.shape
    blocks = total // rows
    n = rows // CHUNK
    row = lambda i, e: (i, 0)
    same = lambda i, e: (0, 0)
    quad = lambda i, e: (i, 0, 0, 0)
    wide = 2 * DK + DV
    chunks = total // CHUNK
    kernel = functools.partial(forward_kernel, heads=heads, rows=rows, taps=taps.shape[0], start=start)
    wide_rows = pl.BlockSpec((rows, heads * DV), row)
    return pl.pallas_call(
        kernel,
        grid_spec=pltpu.PrefetchScalarGridSpec(
            num_scalar_prefetch=1,
            grid=(blocks,),
            in_specs=[
                pl.BlockSpec((rows, width), row),
                pl.BlockSpec((8, width), lambda i, e: (before_at, 0)),
                pl.BlockSpec(taps.shape, same),
                pl.BlockSpec(rate.shape, same),
                pl.BlockSpec(shift.shape, same),
                pl.BlockSpec(gain.shape, same),
                pl.BlockSpec(enter.shape, lambda i, e: (0, 0, 0)),
            ],
            out_specs=[
                wide_rows,
                wide_rows,
                wide_rows,
                pl.BlockSpec((n, heads, DK, DV), quad),
                pl.BlockSpec((n, heads, CHUNK, CHUNK), quad),
                pl.BlockSpec((n, heads, CHUNK, DK), quad),
                pl.BlockSpec((n, heads, DK, DK), quad),
                pl.BlockSpec(enter.shape, lambda i, e: (0, 0, 0)),
            ],
            scratch_shapes=[pltpu.VMEM((rows + 8, heads * wide), f32)],
        ),
        out_shape=[
            jax.ShapeDtypeStruct((total, heads * DV), bf16),
            jax.ShapeDtypeStruct((total, heads * DV), f32),
            jax.ShapeDtypeStruct((total, heads * DV), f32),
            jax.ShapeDtypeStruct((chunks, heads, DK, DV), f32),
            jax.ShapeDtypeStruct((chunks, heads, CHUNK, CHUNK), f32),
            jax.ShapeDtypeStruct((chunks, heads, CHUNK, DK), f32),
            jax.ShapeDtypeStruct((chunks, heads, DK, DK), f32),
            jax.ShapeDtypeStruct(enter.shape, f32),
        ],
        compiler_params=pltpu.CompilerParams(
            dimension_semantics=("arbitrary",), vmem_limit_bytes=56 * 1024 * 1024
        ),
        cost_estimate=pl.CostEstimate(
            flops=total * heads * 1_000_000, bytes_accessed=total * heads * 9_000, transcendentals=total * heads * 2_000
        ),
        name="mixer_forward",
    )(ends, proj, before, taps, rate, shift, gain, enter)


def mixer_backward(
    ends, proj, before, before_at, taps, rate, shift, gain, dgated, saved, leave, later, *, heads, rows, start
):
    total, width = proj.shape
    blocks = total // rows
    n = rows // CHUNK
    row = lambda s, e: (blocks - 1 - s, 0)
    halo = lambda s, e: (jnp.maximum((blocks - 1 - s) * (rows // 8) - 1, 0), 0)
    same = lambda s, e: (0, 0)
    quad = lambda s, e: (blocks - 1 - s, 0, 0, 0)
    wide = 2 * DK + DV
    kernel = functools.partial(
        backward_kernel, heads=heads, rows=rows, taps=taps.shape[0], blocks=blocks, start=start
    )
    wide_rows = pl.BlockSpec((rows, heads * DV), row)
    return pl.pallas_call(
        kernel,
        grid_spec=pltpu.PrefetchScalarGridSpec(
            num_scalar_prefetch=1,
            grid=(blocks,),
            in_specs=[
                pl.BlockSpec((rows, width), row),
                pl.BlockSpec((8, width), halo),
                pl.BlockSpec((8, width), lambda s, e: (before_at, 0)),
                pl.BlockSpec(taps.shape, same),
                pl.BlockSpec(rate.shape, same),
                pl.BlockSpec(shift.shape, same),
                pl.BlockSpec(gain.shape, same),
                wide_rows,
                wide_rows,
                wide_rows,
                pl.BlockSpec((n, heads, DK, DV), quad),
                pl.BlockSpec((n, heads, CHUNK, CHUNK), quad),
                pl.BlockSpec((n, heads, CHUNK, DK), quad),
                pl.BlockSpec((n, heads, DK, DK), quad),
                pl.BlockSpec(leave.shape, lambda s, e: (0, 0, 0)),
                pl.BlockSpec(later.shape, same),
            ],
            out_specs=[
                pl.BlockSpec((rows, width), row),
                pl.BlockSpec((8 * taps.shape[0], heads * wide), same),
                pl.BlockSpec((8, DV), same),
                pl.BlockSpec((16, 128), same),
                pl.BlockSpec(leave.shape, lambda s, e: (0, 0, 0)),
                pl.BlockSpec(later.shape, same),
            ],
            scratch_shapes=[
                pltpu.VMEM((rows + 8, heads * wide), f32),
                pltpu.VMEM((rows + 8, heads * wide), f32),
            ],
        ),
        out_shape=[
            jax.ShapeDtypeStruct((total, width), bf16),
            jax.ShapeDtypeStruct((8 * taps.shape[0], heads * wide), f32),
            jax.ShapeDtypeStruct((8, DV), f32),
            jax.ShapeDtypeStruct((16, 128), f32),
            jax.ShapeDtypeStruct(leave.shape, f32),
            jax.ShapeDtypeStruct(later.shape, f32),
        ],
        compiler_params=pltpu.CompilerParams(
            dimension_semantics=("arbitrary",), vmem_limit_bytes=56 * 1024 * 1024
        ),
        cost_estimate=pl.CostEstimate(
            flops=total * heads * 1_000_000, bytes_accessed=total * heads * 9_000, transcendentals=total * heads * 2_000
        ),
        name="mixer_backward",
    )(ends, proj, proj, before, taps, rate, shift, gain, dgated, *saved, leave, later)


FORWARD_ROWS = 512
BACKWARD_ROWS = 256
RUNS = 2


def rms_scale(values):
    return lax.rsqrt(jnp.mean(values * values, axis=-1, keepdims=True) + epsilon)


def norm_back(values, scale, gain, grad):
    u = gain * grad
    back = scale * u - values * (scale * scale * scale) * jnp.mean(values * u, axis=-1, keepdims=True)
    return back, jnp.sum(grad * (values * scale), axis=0)


def swap(x, axis, bit):
    size = lax.axis_size(axis)
    return lax.ppermute(x, axis, [(i, i ^ bit) for i in range(size)])


def exchange_roles(x):
    n = lax.axis_size("lo")
    return lax.ppermute(x, ("lo", "tensor"), [(a * n + b, b * n + a) for a in range(n) for b in range(n)])


def bits(size):
    return [1 << k for k in range(size.bit_length() - 1)]


def reversed_bits(n):
    order = [0]
    for bit in reversed(bits(n)):
        order = order + [k ^ bit for k in order]
    return order


def gather_first(x):
    return jnp.concatenate([x, swap(x, "lo", bits(lax.axis_size("lo"))[-1])], axis=0)


def gather_last(x):
    for bit in reversed(bits(lax.axis_size("lo"))[:-1]):
        x = jnp.concatenate([x, swap(x, "lo", bit)], axis=0)
    return x


def gather_rows(x):
    return gather_last(gather_first(x))


def halve(x, bit, kind):
    half = x.shape[0] // 2
    return x[:half].astype(f32) + swap(x[half:].astype(kind), "lo", bit).astype(f32)


def scatter_first(x):
    kind = x.dtype
    for bit in bits(lax.axis_size("lo"))[:-1]:
        x = halve(x, bit, kind)
    half = x.shape[0] // 2
    return x[:half], x[half:].astype(kind)


def scatter_last(kept, sent):
    return kept + swap(sent, "lo", bits(lax.axis_size("lo"))[-1]).astype(f32)


def sum_everywhere(x):
    for axis in ("lo", "tensor", "hi"):
        for bit in bits(lax.axis_size(axis)):
            x = x + swap(x, axis, bit)
    return x


def rank_of(key):
    return jnp.sum((key[..., None, :] < key[..., :, None]).astype(jnp.int32), axis=-1)


def after(x, *first):
    return lax.optimization_barrier((x, first))[0]


def widen(columns):
    return lax.all_gather(columns, ("hi", "tensor"), axis=0, tiled=True)


def narrow(columns):
    return lax.psum_scatter(columns.astype(bf16), ("hi", "tensor"), scatter_dimension=0, tiled=True)


def product(a, b, ca=1, cb=0, dtype=f32):
    return lax.dot_general(a, b, (((ca,), (cb,)), ((), ())), preferred_element_type=f32).astype(dtype)


def body(
    tokens,
    cotangent,
    lengths,
    token_order,
    token_return,
    w_mix,
    w_ba,
    conv_w,
    w_out,
    w_gate_up,
    w_down,
    gain_attn,
    gain_ffn,
    gain_out,
    decay_log,
    decay_bias,
):
    splits = lax.axis_size("lo")
    groups = lax.axis_size("hi") * splits
    me = lax.axis_index("lo")
    local_rows, model_width = tokens.shape
    group_rows = local_rows * splits
    per_peer = local_rows // groups
    weight_rows, heads, head_width = w_mix.shape
    units = w_down.shape[1]
    taps = conv_w.shape[2]
    conv_width = head_width - DV
    proj_width = heads * head_width

    spread = ("hi", "tensor")
    width = lax.axis_size("hi")
    span = jnp.arange(local_rows, dtype=jnp.int32)
    part_rows = width * per_peer

    send_rank = rank_of(token_return // group_rows * local_rows + token_return % local_rows)
    send_hot = (span[:, None] == send_rank[None, :]).astype(bf16)

    def across(rows):
        return lax.all_to_all(rows, spread, split_axis=0, concat_axis=0, tiled=True)

    def pack(rows):
        return product(send_hot, rows, dtype=bf16).reshape(groups, per_peer, -1)

    def by_part(rows):
        rows = jnp.transpose(rows.reshape(width, splits, per_peer, -1), (1, 0, 2, 3))
        return rows.reshape(local_rows, -1)

    def from_part(rows):
        rows = jnp.transpose(rows.reshape(splits, width, per_peer, model_width), (1, 0, 2, 3))
        return rows.reshape(groups, per_peer, model_width)

    def unpack(rows):
        return product(send_hot, rows.reshape(local_rows, model_width), 0, 0, bf16)

    place = token_return % local_rows
    lane = jnp.arange(128, dtype=jnp.int32)[None, :]
    digits = jnp.where(lane == 0, (place // 16)[:, None], jnp.where(lane == 1, (place % 16)[:, None], 0))
    tagged = jnp.concatenate([tokens, digits.astype(bf16)], axis=1)
    arrived = across(pack(tagged))
    packed_grad = across(pack(after(cotangent, arrived)))
    run_parts = splits // RUNS
    run_rows = run_parts * local_rows

    def in_parts(rows):
        rows = rows.reshape(splits, run_parts, part_rows, -1)
        return jnp.transpose(rows, (1, 0, 2, 3)).reshape(run_parts, local_rows, -1)

    def order_of(tags):
        tags = in_parts(tags)[:, :, :2].astype(jnp.int32)
        at = tags[:, :, 0] * 16 + tags[:, :, 1]
        return (at[:, None, :] == span[None, :, None]).astype(bf16)

    def to_sequence(order, rows):
        return lax.dot_general(
            order, in_parts(rows), (((2,), (1,)), ((0,), (0,))), preferred_element_type=f32
        ).astype(bf16).reshape(run_rows, -1)

    def from_sequence(order, rows):
        rows = lax.dot_general(
            order, rows.reshape(run_parts, local_rows, -1), (((1,), (1,)), ((0,), (0,))),
            preferred_element_type=f32,
        ).astype(bf16).reshape(run_parts, splits, part_rows, -1)
        return jnp.transpose(rows, (1, 0, 2, 3)).reshape(run_rows, -1)

    head_start = me * heads
    lanes = jnp.zeros((1, 128), f32)
    rate_row = lanes.at[0, 1 : 2 * heads : 2].set(lax.dynamic_slice_in_dim(decay_log, head_start, heads))
    shift_row = lanes.at[0, 1 : 2 * heads : 2].set(lax.dynamic_slice_in_dim(decay_bias, head_start, heads))
    own_lengths = exchange_roles(lengths)
    ends = jnp.sum(jnp.where(jnp.tri(SEQS, dtype=bool), own_lengths, 0), axis=1).astype(jnp.int32)
    small_at = proj_width
    conv_at = small_at + heads * w_ba.shape[2]
    spare = 128 - heads * w_ba.shape[2] - taps
    mix_own = exchange_roles(
        jnp.concatenate(
            [
                w_mix.reshape(weight_rows, proj_width).astype(bf16),
                w_ba.reshape(weight_rows, -1).astype(bf16),
                conv_w.reshape(weight_rows, taps).astype(bf16),
                jnp.zeros((weight_rows, spare), bf16),
                w_out.reshape(weight_rows, heads * DV).astype(bf16),
            ],
            axis=1,
        )
    )
    mix_all = widen(mix_own)
    arrived = by_part(after(arrived, ends, rate_row, shift_row))
    packed_in, tags = arrived[:, :model_width], arrived[:, model_width:]
    runs = range(RUNS)
    own_rows = local_rows // RUNS

    def split(rows):
        return [rows[r * own_rows : (r + 1) * own_rows] for r in runs]

    input_f32 = packed_in.astype(f32)
    input_scale = rms_scale(input_f32)
    input_runs = split(input_f32)
    normed_runs = split(jnp.concatenate([(input_f32 * input_scale * gain_attn).astype(bf16), tags], axis=1))
    gathered_0 = gather_rows(normed_runs[0])
    ffn_sent = jnp.concatenate(
        [w_gate_up.reshape(weight_rows, 2 * units).astype(bf16), w_down.astype(bf16)], axis=1
    )
    out_all = mix_all[:, small_at + 128 :]
    mix_all = mix_all[:, : small_at + 128]

    conv_all = mix_all[:, conv_at : conv_at + taps].reshape(-1, heads, taps).astype(f32)
    tap_rows = jnp.transpose(conv_all, (2, 1, 0)).reshape(taps, heads * conv_width)
    gain_row = gain_out[None]
    constants = (tap_rows, rate_row, shift_row, gain_row)

    state = jnp.zeros((heads, DK, DV), f32)

    def ahead(r):
        return (projected[r - 1], run_rows // 8 - 1) if r else (projected[r], 0)

    def mix_forward(r, state):
        return mixer_forward(
            ends, projected[r], *ahead(r), *constants, state, heads=heads, rows=FORWARD_ROWS, start=r * run_rows
        )

    def feed_forward(r, normed_mid):
        place = (r * run_parts + jnp.arange(run_parts, dtype=jnp.int32))[:, None, None] * local_rows
        alive = (place + span[None, :, None] < ends[SEQS - 1]).astype(bf16)
        live = from_sequence(orders[r], jnp.broadcast_to(alive, (run_parts, local_rows, 128)))[:, :1].astype(f32)
        grad_hidden = product(grad_all[r], w_last) * live
        gate_up = product(normed_mid, w_pair)
        gate, up = gate_up[:, :units], gate_up[:, units:]
        s = sigmoid(gate)
        hidden = (gate * s * up * live).astype(bf16)
        grad_pair = jnp.concatenate(
            [grad_hidden * up * (s * (1.0 + gate * (1.0 - s))), grad_hidden * (gate * s)], axis=1
        ).astype(bf16)
        return hidden, grad_pair, product(grad_pair, w_pair, 1, 1, bf16)

    def normed_of(middle):
        scale = rms_scale(middle)
        return scale, (middle * scale * gain_ffn).astype(bf16)

    constants = (tap_rows, rate_row, shift_row, gain_row)
    orders = [order_of(gathered_0[:, model_width:])]
    seq_0 = to_sequence(orders[0], gathered_0[:, :model_width])
    projected = [product(seq_0, mix_all)]
    packed_grad = by_part(packed_grad)
    projected[0], normed_runs, ffn_sent, packed_grad = lax.optimization_barrier(
        (projected[0], normed_runs, ffn_sent, packed_grad)
    )
    *saved_0, state = mix_forward(0, state)
    crossed = swap(packed_grad, "lo", bits(splits)[-1])
    saved_0, first_1, ffn_own = lax.optimization_barrier(
        (saved_0, gather_first(normed_runs[1]), exchange_roles(ffn_sent))
    )
    ffn_all = widen(ffn_own)
    grad_runs = split(packed_grad)
    gathered_1 = gather_last(first_1)
    terms_0 = product(from_sequence(orders[0], saved_0[0]), out_all, 1, 1)
    gathered_1 = after(gathered_1, terms_0)
    orders.append(order_of(gathered_1[:, model_width:]))
    seq_1 = to_sequence(orders[1], gathered_1[:, :model_width])
    projected.append(product(seq_1, mix_all))
    kept_0, sent_0 = scatter_first(terms_0)
    projected[1], kept_0, sent_0, crossed = lax.optimization_barrier((projected[1], kept_0, sent_0, crossed))
    grad_all = [gather_last(jnp.concatenate(x, axis=0)) for x in zip(grad_runs, split(crossed))]
    *saved_1, state = mix_forward(1, state)
    middle_0 = input_runs[0] + after(scatter_last(kept_0, sent_0), saved_1[0])
    scale_0, normed_mid_0 = normed_of(middle_0)
    terms_1 = product(from_sequence(orders[1], saved_1[0]), out_all, 1, 1)
    first_0 = gather_first(normed_mid_0)
    kept_1, sent_1 = scatter_first(terms_1)
    kept_1, sent_1, first_0, ffn_all = lax.optimization_barrier((kept_1, sent_1, first_0, ffn_all))
    w_pair, w_last = ffn_all[:, : 2 * units], ffn_all[:, 2 * units :]
    normed_mid_0 = gather_last(first_0)

    hidden_0, pair_0, grad_terms_0 = feed_forward(0, normed_mid_0)
    middle_1 = input_runs[1] + after(scatter_last(kept_1, sent_1), grad_terms_0)
    scale_1, normed_mid_1 = normed_of(middle_1)
    first_1 = gather_first(normed_mid_1)
    grad_kept_0, grad_sent_0 = scatter_first(grad_terms_0)
    grad_kept_0, grad_sent_0, first_1 = lax.optimization_barrier((grad_kept_0, grad_sent_0, first_1))
    normed_mid_1 = gather_last(first_1)
    hidden_1, pair_1, grad_terms_1 = feed_forward(1, normed_mid_1)
    grad_kept_1, grad_sent_1 = scatter_first(grad_terms_1)
    grad_kept_1, grad_sent_1, grad_terms_0_sum = lax.optimization_barrier(
        (grad_kept_1, grad_sent_1, scatter_last(grad_kept_0, grad_sent_0))
    )
    hidden_0, pair_0, hidden_1, pair_1 = after((hidden_0, pair_0, hidden_1, pair_1), grad_sent_1)
    grad_pairs = product(normed_mid_0, pair_0, 0, 0) + product(normed_mid_1, pair_1, 0, 0)
    grad_terms_1_sum = after(scatter_last(grad_kept_1, grad_sent_1), grad_pairs)
    back_1, gain_1 = norm_back(middle_1, scale_1, gain_ffn, grad_terms_1_sum)
    grad_middle_1 = grad_runs[1].astype(f32) + back_1
    first_1 = gather_first(grad_middle_1.astype(bf16))
    hidden_0, hidden_1 = after((hidden_0, hidden_1), grad_middle_1)
    grad_last = product(grad_all[0], hidden_0, 0, 0) + product(grad_all[1], hidden_1, 0, 0)
    layer_terms = [product(h, w_last, 1, 1, bf16) for h in (hidden_0, hidden_1)]
    back_0, gain_0 = norm_back(middle_0, scale_0, gain_ffn, after(grad_terms_0_sum, grad_middle_1))
    grad_gain_ffn = gain_0 + gain_1
    grad_middle_0 = grad_runs[0].astype(f32) + back_0
    first_1, grad_last, layer_terms, grad_low_0 = lax.optimization_barrier(
        (first_1, grad_last, layer_terms, grad_middle_0.astype(bf16))
    )
    grad_mid_seq_1 = to_sequence(orders[1], gather_last(first_1))
    grad_ffn = narrow(jnp.concatenate([grad_pairs.astype(bf16), grad_last.astype(bf16)], axis=1))

    def mix_backward(r, grad_gated, saved, leave, later):
        return mixer_backward(
            ends, projected[r], *ahead(r), *constants, grad_gated, saved[1:], leave, later,
            heads=heads, rows=BACKWARD_ROWS, start=r * run_rows,
        )

    leave = jnp.zeros((heads, DK, DV), f32)
    later = jnp.zeros((8, heads * conv_width), f32)
    layer_parts = [scatter_first(x) for x in layer_terms]
    grad_gated_1 = product(grad_mid_seq_1, out_all)
    grad_gated_1, grad_low_0, layer_parts = lax.optimization_barrier((grad_gated_1, grad_low_0, layer_parts))
    grad_proj_1, *sums_1, leave, later = mix_backward(1, grad_gated_1, saved_1, leave, later)
    layer_sums = [scatter_last(*x) for x in layer_parts]
    grad_proj_1, first_0, layer_sums = lax.optimization_barrier((grad_proj_1, gather_first(grad_low_0), layer_sums))
    grad_mid_seq_0 = to_sequence(orders[0], gather_last(first_0))
    grad_gated_0 = product(grad_mid_seq_0, out_all)
    layer_rows = jnp.concatenate([m + x for m, x in zip((middle_0, middle_1), layer_sums)], axis=0)
    layer_rows = from_part(layer_rows.astype(bf16))
    grad_gated_0, layer_rows = lax.optimization_barrier((grad_gated_0, layer_rows))
    grad_proj_0, *sums_0, leave, later = mix_backward(0, grad_gated_0, saved_0, leave, later)
    grad_proj_0, grad_ffn, layer_back = lax.optimization_barrier((grad_proj_0, grad_ffn, across(layer_rows)))
    grad_taps, grad_gain_out, grad_decay = [a + b for a, b in zip(sums_0, sums_1)]
    grad_conv = jnp.sum(grad_taps.reshape(taps, 8, heads, conv_width), axis=1)
    grad_conv = jnp.transpose(grad_conv, (2, 1, 0)).reshape(-1, taps)
    grad_mix = product(seq_0, grad_proj_0, 0, 0) + product(seq_1, grad_proj_1, 0, 0)
    grad_mix = (grad_mix + jnp.pad(grad_conv, ((0, 0), (conv_at, spare)))).astype(bf16)
    grad_out_w = product(grad_mid_seq_0, saved_0[0], 0, 0) + product(grad_mid_seq_1, saved_1[0], 0, 0)
    grad_mix = jnp.concatenate([grad_mix, grad_out_w.astype(bf16)], axis=1)
    grad_mix, *proj_parts = lax.optimization_barrier((grad_mix, grad_proj_0, grad_proj_1))
    normed_terms = [from_sequence(orders[r], product(proj_parts[r], mix_all, 1, 1, bf16)) for r in runs]
    grad_mix = exchange_roles(narrow(grad_mix)).astype(f32)
    normed_terms = [x.reshape(splits, own_rows, model_width) for x in normed_terms]
    normed_terms = jnp.concatenate(normed_terms, axis=1).reshape(group_rows, model_width)
    grad_normed = scatter_last(*scatter_first(normed_terms))
    grad_normed, grad_ffn = lax.optimization_barrier((grad_normed, exchange_roles(grad_ffn)))
    grad_ffn = grad_ffn.astype(f32)
    grad_input_norm, grad_gain_attn = norm_back(input_f32, input_scale, gain_attn, grad_normed)
    grad_middle = jnp.concatenate([grad_middle_0, grad_middle_1], axis=0)
    input_grad = unpack(across(from_part((grad_middle + grad_input_norm).astype(bf16))))
    layer_out = unpack(layer_back)

    head_total = decay_log.shape[0]
    decay_sums = jnp.sum(grad_decay.reshape(2, 8, 128), axis=1)[:, 1 : 2 * heads : 2]
    decay_full = lax.dynamic_update_slice(jnp.zeros((2, head_total), f32), decay_sums, (0, head_start))
    flat = jnp.concatenate(
        [grad_gain_attn, grad_gain_ffn, jnp.sum(grad_gain_out, axis=0), decay_full.reshape(-1)]
    )
    flat = sum_everywhere(jnp.pad(flat, (0, -flat.shape[0] % 1024)).reshape(8, -1)).reshape(-1)
    at = 0
    sums = []
    for size in (model_width, model_width, gain_out.shape[0], head_total, head_total):
        sums.append(flat[at : at + size])
        at += size
    return (
        layer_out,
        input_grad,
        grad_mix[:, :small_at].reshape(w_mix.shape),
        grad_mix[:, small_at:conv_at].reshape(w_ba.shape),
        grad_mix[:, conv_at : conv_at + taps].reshape(conv_w.shape),
        grad_mix[:, small_at + 128 :].reshape(w_out.shape),
        grad_ffn[:, : 2 * units].reshape(w_gate_up.shape),
        grad_ffn[:, 2 * units :],
        *sums,
    )


def solution(mesh):
    dp, splits = mesh.shape["dp"], mesh.shape["tensor"]
    roles = Mesh(mesh.devices.reshape(dp // splits, splits, splits), ("hi", "lo", "tensor"))
    group = ("hi", "lo")
    rows = P((*group, "tensor"))
    by_head = P(group, "tensor", None)
    by_unit = (P(group, None, "tensor"), P(group, "tensor"))
    return jax.shard_map(
        body,
        mesh=roles,
        in_specs=(rows, rows, P(group), rows, rows, by_head, by_head, by_head, by_head, *by_unit)
        + (P(),) * 5,
        out_specs=(rows, rows, by_head, by_head, by_head, by_head, *by_unit) + (P(),) * 5,
        check_vma=False,
    )
```

```python
import functools
import jax
import jax.numpy as jnp
from jax import lax
from jax.experimental import pallas as pl
from jax.experimental.pallas import tpu as pltpu
from jax.sharding import Mesh
from jax.sharding import PartitionSpec as P

DK = 128
DV = 256
SEQS = 3
CHUNK = 128
epsilon = 1e-06
f32 = jnp.float32
bf16 = jnp.bfloat16


def dot(a, b, ca=1, cb=0):
    return lax.dot_general(a, b, (((ca,), (cb,)), ((), ())), preferred_element_type=f32)


def halves(x):
    high = x.astype(bf16)
    return high, (x - high.astype(f32)).astype(bf16)


def dot1(a, b, ca=1, cb=0):
    return dot(a.astype(bf16), b.astype(bf16), ca, cb)


def dot3(a, b, ca=1, cb=0):
    ah, al = halves(a)
    bh, bl = halves(b)
    return dot(jnp.concatenate([ah, al, ah], axis=ca), jnp.concatenate([bh, bh, bl], axis=cb), ca, cb)


def dot_exact(a, b, ca=1, cb=0):
    ah = a.astype(bf16)
    bh, bl = halves(b)
    bt = (b - bh.astype(f32) - bl.astype(f32)).astype(bf16)
    return dot(ah, bh, ca, cb) + (dot(ah, bl, ca, cb) + dot(ah, bt, ca, cb))


def sigmoid(x):
    return 1.0 / (1.0 + jnp.exp(-x))


def segment_of(position, ends):
    return sum((position >= e).astype(jnp.int32) for e in ends)


def iota(shape, axis):
    return lax.broadcasted_iota(jnp.int32, shape, axis)


def conv_masks(base, rows, ends, taps, sign):
    t = base + iota((rows, 1), 0)
    own = segment_of(t, ends)
    masks = []
    for j in range(1, taps):
        other = t - sign * j
        same = segment_of(other, ends) == own
        masks.append(jnp.where(same & (other >= 0), 1.0, 0.0))
    return masks


def chunk_terms(base, ends, g_col, g_row, q, k, beta):
    c = CHUNK
    ti = base + iota((c, 1), 0)
    tj = base + iota((1, c), 1)
    si = segment_of(ti, ends)
    sj = segment_of(tj, ends)
    ii = iota((c, c), 0)
    jj = iota((c, c), 1)
    decay = jnp.where((si == sj) & (ii >= jj), jnp.exp(jnp.minimum(g_col - g_row, 0.0)), 0.0)
    before = jnp.where(base > 0, segment_of(base - 1, ends), -1)
    last = segment_of(base + c - 1, ends)
    carry = jnp.where(si == before, jnp.exp(g_col), 0.0)
    g_last = g_col[c - 1 :, :]
    tail = jnp.where(si == last, jnp.exp(jnp.minimum(g_last - g_col, 0.0)), 0.0)
    return decay, carry, tail, ii, jj


def invert(lower, ii, jj, mul):
    first = ((ii ^ jj) == 1) & (ii > jj)
    eye = jnp.where(ii == jj, 1.0, 0.0)
    inv = [eye - jnp.where(first, a, 0.0) for a in lower]
    size = 2
    while size < CHUNK:
        joins = ((ii // (2 * size)) == (jj // (2 * size))) & ((ii & size) != 0) & ((jj & size) == 0)
        half = [mul(jnp.where(joins, a, 0.0), t) for a, t in zip(lower, inv)]
        inv = [t - mul(t, x) for t, x in zip(inv, half)]
        size *= 2
    return inv


def silu_parts(u):
    s = sigmoid(u)
    return u * s, s


def forward_kernel(
    ends_ref, proj_ref, before_ref, taps_ref, rate_ref, shift_ref, gain_ref, enter_ref,
    gated_ref, o_ref, u_ref, s_ref, t_ref, qe_ref, m_ref, state,
    xs, *, heads, rows, taps, start,
):
    i = pl.program_id(0)
    wide = 2 * DK + DV
    full = wide + DV
    ends = [ends_ref[k] for k in range(SEQS)]
    base = start + i * rows
    c = CHUNK

    @pl.when(i == 0)
    def _():
        for h in range(heads):
            xs[0:8, h * wide : (h + 1) * wide] = before_ref[:, h * full : h * full + wide]
        state[...] = enter_ref[...]

    @pl.when(i > 0)
    def _():
        xs[0:8, :] = xs[rows : rows + 8, :]

    for h in range(heads):
        xs[8:, h * wide : (h + 1) * wide] = proj_ref[:, h * full : h * full + wide]
    small = proj_ref[:, heads * full :]
    beta_all = sigmoid(small)
    shifted = small + shift_ref[...]
    ld_all = -jnp.exp(rate_ref[...]) * (jnp.maximum(shifted, 0.0) + jnp.log1p(jnp.exp(-jnp.abs(shifted))))
    masks = conv_masks(base, rows, ends, taps, 1)
    qs, ks, vs = [], [], []
    for h in range(heads):
        sl = slice(h * wide, (h + 1) * wide)
        run = xs[8:, sl] * taps_ref[0:1, sl]
        for j in range(1, taps):
            run = run + (xs[8 - j : 8 - j + rows, sl] * masks[j - 1]) * taps_ref[j : j + 1, sl]
        act = run * sigmoid(run)
        q, k, v = act[:, :DK], act[:, DK : 2 * DK], act[:, 2 * DK :]
        qs.append(q * (lax.rsqrt(jnp.sum(q * q, axis=-1, keepdims=True) + epsilon) * DK ** (-0.5)))
        ks.append(k * lax.rsqrt(jnp.sum(k * k, axis=-1, keepdims=True) + epsilon))
        vs.append(v)
    lower_tri = jnp.where(iota((c, c), 0) >= iota((c, c), 1), 1.0, 0.0)
    n = rows // c
    probs = []
    for b in range(n):
        rs = slice(b * c, (b + 1) * c)
        g_all = dot_exact(lower_tri, ld_all[rs])
        g_t = g_all.T
        for h in range(heads):
            q, k, v = qs[h][rs], ks[h][rs], vs[h][rs]
            beta = beta_all[rs, 2 * h : 2 * h + 1]
            g_col = g_all[:, 2 * h + 1 : 2 * h + 2]
            g_row = g_t[2 * h + 1 : 2 * h + 2, :]
            decay, carry, tail, ii, jj = chunk_terms(base + b * c, ends, g_col, g_row, q, k, beta)
            qkk = DOT_QK(jnp.concatenate([q, k], axis=0), k, 1, 1)
            p = qkk[:c] * decay
            a = jnp.where(ii > jj, qkk[c:] * decay, 0.0) * beta
            probs.append(dict(b=b, h=h, q=q, k=k, v=v, beta=beta, carry=carry, tail=tail, p=p, a=a))
    inv = invert([x["a"] for x in probs], ii, jj, DOT_INV)
    for x, t in zip(probs, inv):
        x["t"] = t
        rhs = jnp.concatenate([(x["beta"] * x["carry"]) * x["k"], x["beta"] * x["v"]], axis=1)
        x["wv"] = DOT_WV(t, rhs)
    for x in probs:
        pwv = DOT_P(x["p"], x["wv"])
        x["qe"] = x["carry"] * x["q"] - pwv[:, :DK]
        x["pv"] = pwv[:, DK:]
        kwv = DOT_K(x["tail"] * x["k"], x["wv"], 0, 0)
        c_last = x["carry"][c - 1 :, :]
        x["m"] = jnp.where(ii == jj, c_last, 0.0) - kwv[:, :DK]
        x["bf"] = kwv[:, DK:]
    for x in probs:
        b, h = x["b"], x["h"]
        s = state[h]
        s_ref[b, h] = s
        t_ref[b, h] = x["t"]
        qe_ref[b, h] = x["qe"]
        m_ref[b, h] = x["m"]
        w = x["wv"][:, :DK]
        state[h] = x["bf"] + DOT_S(x["m"], s)
        wq = DOT_O(jnp.concatenate([w, x["qe"]], axis=0), s)
        u_ref[b * c : (b + 1) * c, h * DV : (h + 1) * DV] = x["wv"][:, DK:] - wq[:c]
        o_ref[b * c : (b + 1) * c, h * DV : (h + 1) * DV] = x["pv"] + wq[c:]
    live = jnp.where(segment_of(base + iota((rows, 1), 0), ends) < SEQS, 1.0, 0.0)
    for h in range(heads):
        o = o_ref[:, h * DV : (h + 1) * DV]
        z = proj_ref[:, h * full + wide : (h + 1) * full]
        r = lax.rsqrt(jnp.mean(o * o, axis=-1, keepdims=True) + epsilon)
        gated_ref[:, h * DV : (h + 1) * DV] = (o * (r * live) * gain_ref[...] * (z * sigmoid(z))).astype(bf16)


def backward_kernel(
    ends_ref, proj_ref, halo_ref, before_ref, taps_ref, rate_ref, shift_ref, gain_ref,
    dgated_ref, o_ref, u_ref, s_ref, t_ref, qe_ref, m_ref, leave_ref, later_ref,
    dproj_ref, dtaps_ref, dgain_ref, ddecay_ref, dstate, first_ref,
    xs, ds, *, heads, rows, taps, blocks, start,
):
    step = pl.program_id(0)
    i = blocks - 1 - step
    wide = 2 * DK + DV
    full = wide + DV
    ends = [ends_ref[k] for k in range(SEQS)]
    base = start + i * rows
    c = CHUNK

    @pl.when(step == 0)
    def _():
        ds[rows : rows + 8, :] = later_ref[...]
        dstate[...] = leave_ref[...]
        dtaps_ref[...] = jnp.zeros_like(dtaps_ref)
        dgain_ref[...] = jnp.zeros_like(dgain_ref)
        ddecay_ref[...] = jnp.zeros_like(ddecay_ref)

    @pl.when(step > 0)
    def _():
        ds[rows : rows + 8, :] = ds[0:8, :]

    for h in range(heads):
        cols = slice(h * full, h * full + wide)
        xs[0:8, h * wide : (h + 1) * wide] = jnp.where(i == 0, before_ref[:, cols], halo_ref[:, cols])
        xs[8:, h * wide : (h + 1) * wide] = proj_ref[:, h * full : h * full + wide]
    small = proj_ref[:, heads * full :]
    beta_all = sigmoid(small)
    shifted = small + shift_ref[...]
    rate = -jnp.exp(rate_ref[...])
    ld_all = rate * (jnp.maximum(shifted, 0.0) + jnp.log1p(jnp.exp(-jnp.abs(shifted))))
    masks = conv_masks(base, rows, ends, taps, 1)
    live = jnp.where(segment_of(base + iota((rows, 1), 0), ends) < SEQS, 1.0, 0.0)
    acts = []
    dos = []
    for h in range(heads):
        sl = slice(h * wide, (h + 1) * wide)
        run = xs[8:, sl] * taps_ref[0:1, sl]
        for j in range(1, taps):
            run = run + (xs[8 - j : 8 - j + rows, sl] * masks[j - 1]) * taps_ref[j : j + 1, sl]
        sg = sigmoid(run)
        act = run * sg
        dact = sg * (1.0 + run * (1.0 - sg))
        q, k, v = act[:, :DK], act[:, DK : 2 * DK], act[:, 2 * DK :]
        rq = lax.rsqrt(jnp.sum(q * q, axis=-1, keepdims=True) + epsilon)
        rk = lax.rsqrt(jnp.sum(k * k, axis=-1, keepdims=True) + epsilon)
        acts.append((q * rq, k * rk, v, dact, rq, rk))
        o = o_ref[:, h * DV : (h + 1) * DV]
        z = proj_ref[:, h * full + wide : (h + 1) * full]
        dg = dgated_ref[:, h * DV : (h + 1) * DV] * live
        r = lax.rsqrt(jnp.mean(o * o, axis=-1, keepdims=True) + epsilon)
        nrm = o * r
        sz = sigmoid(z)
        dz = dg * nrm * gain_ref[...] * (sz * (1.0 + z * (1.0 - sz)))
        dng = dg * (z * sz)
        dgain_ref[...] += jnp.sum((dng * nrm).reshape(rows // 8, 8, DV), axis=0)
        dn = dng * gain_ref[...]
        dos.append(r * (dn - nrm * jnp.mean(dn * nrm, axis=-1, keepdims=True)))
        dproj_ref[:, h * full + wide : (h + 1) * full] = dz.astype(bf16)
    low_i = iota((c, c), 0)
    low_j = iota((c, c), 1)
    lower_tri = jnp.where(low_i >= low_j, 1.0, 0.0)
    upper_tri = jnp.where(low_i <= low_j, 1.0, 0.0)
    strict_low = jnp.where(low_i > low_j, 1.0, 0.0)
    n = rows // c
    probs = []
    for b in reversed(range(n)):
        rs = slice(b * c, (b + 1) * c)
        g_all = dot_exact(lower_tri, ld_all[rs])
        g_t = g_all.T
        for h in range(heads):
            q, k, v = acts[h][0][rs] * DK ** (-0.5), acts[h][1][rs], acts[h][2][rs]
            beta = beta_all[rs, 2 * h : 2 * h + 1]
            g_col = g_all[:, 2 * h + 1 : 2 * h + 2]
            g_row = g_t[2 * h + 1 : 2 * h + 2, :]
            decay, carry, tail, ii, jj = chunk_terms(base + b * c, ends, g_col, g_row, q, k, beta)
            qkk = DOT_QK(jnp.concatenate([q, k], axis=0), k, 1, 1)
            p = qkk[:c] * decay
            dkk = jnp.where(ii > jj, qkk[c:] * decay, 0.0)
            do = dos[h][rs]
            u = u_ref[rs, h * DV : (h + 1) * DV]
            dp = DOT_B(do, u, 1, 1)
            pdo = DOT_B(p, do, 0, 0)
            qdo = DOT_B(qe_ref[b, h], do, 0, 0)
            f = DOT_B(do, s_ref[b, h], 1, 1)
            probs.append(dict(b=b, h=h, q=q, k=k, v=v, beta=beta, carry=carry, tail=tail, decay=decay, p=p, dkk=dkk,
                              do=do, u=u, dp=dp, pdo=pdo, qdo=qdo, f=f))
    for x in probs:
        b, h = x["b"], x["h"]
        dnext = dstate[h]
        x["dnext"] = dnext
        dstate[h] = DOT_S(m_ref[b, h], dnext, 0, 0) + x["qdo"]
    for x in probs:
        du = x["pdo"] + DOT_B(x["tail"] * x["k"], x["dnext"])
        x["dr"] = DOT_B(t_ref[x["b"], x["h"]], du, 0, 0)
        x["j"] = DOT_B(x["u"], x["dnext"], 1, 1)
    dq_all = [[None] * n for _ in range(heads)]
    dk_all = [[None] * n for _ in range(heads)]
    dv_all = [[None] * n for _ in range(heads)]
    dsmall = [[None] * heads for _ in range(n)]
    lane = iota((c, DK), 1)
    for x in probs:
        b, h, q, k, beta, carry = x["b"], x["h"], x["q"], x["k"], x["beta"], x["carry"]
        dr = x["dr"]
        s = s_ref[b, h]
        neg = DOT_B(dr, x["u"], 1, 1)
        hh = DOT_B(dr, s, 1, 1)
        neg = jnp.where(ii > jj, neg, 0.0)
        adk = neg * x["dkk"]
        dbeta = (
            jnp.sum(dr * x["v"], axis=-1, keepdims=True)
            - carry * jnp.sum(k * hh, axis=-1, keepdims=True)
            - jnp.sum(adk, axis=-1, keepdims=True)
        )
        dcarry = jnp.sum(q * x["f"], axis=-1, keepdims=True) - beta * jnp.sum(k * hh, axis=-1, keepdims=True)
        e = x["dp"] * x["p"] - beta * adk
        dqk = x["dp"] * x["decay"]
        dkk = -(neg * beta) * jnp.where(ii > jj, x["decay"], 0.0)
        dtail = x["tail"] * jnp.sum(k * x["j"], axis=-1, keepdims=True)
        dcl = carry[c - 1 :, :] * jnp.sum(x["dnext"] * s, keepdims=True)
        col = carry * dcarry + jnp.where(iota((c, 1), 0) == c - 1, dcl, 0.0)
        straddle = jnp.where(ii > jj, dot_exact(upper_tri, e), 0.0)
        both = dot_exact(upper_tri, jnp.where(lane == 0, col, 0.0)) + dot_exact(
            strict_low, jnp.where(lane == 0, dtail, 0.0)
        )
        dld = jnp.sum(straddle, axis=-1, keepdims=True) + both[:, 0:1]
        dq_all[h][b] = carry * x["f"] + DOT_G(dqk, k)
        dk_all[h][b] = (
            x["tail"] * x["j"] - (carry * beta) * hh + DOT_G(dqk, q, 0, 0) + DOT_G(dkk, k) + DOT_G(dkk, k, 0, 0)
        )
        dv_all[h][b] = beta * dr
        dsmall[b][h] = (dbeta, dld)
    for b in range(n):
        rs = slice(b * c, (b + 1) * c)
        tile = jnp.zeros((c, DK), f32)
        for h in range(heads):
            dbeta, dld = dsmall[b][h]
            tile = jnp.where(lane == 2 * h, dbeta, jnp.where(lane == 2 * h + 1, dld, tile))
        bet = beta_all[rs]
        dshift = rate * tile * sigmoid(shifted[rs])
        even = (lane & 1) == 0
        inside = lane < 2 * heads
        ddecay_ref[0:8, :] += jnp.sum(jnp.where(even, 0.0, tile * ld_all[rs]).reshape(c // 8, 8, DK), axis=0)
        ddecay_ref[8:16, :] += jnp.sum(jnp.where(even, 0.0, dshift).reshape(c // 8, 8, DK), axis=0)
        dproj_ref[rs, heads * full :] = jnp.where(
            inside, jnp.where(even, tile * (bet * (1.0 - bet)), dshift), 0.0
        ).astype(bf16)
    for h in range(heads):
        qn, kn, v, dact, rq, rk = acts[h]
        dq = jnp.concatenate(dq_all[h], axis=0) * DK ** (-0.5)
        dk = jnp.concatenate(dk_all[h], axis=0)
        dq = rq * (dq - qn * jnp.sum(dq * qn, axis=-1, keepdims=True))
        dk = rk * (dk - kn * jnp.sum(dk * kn, axis=-1, keepdims=True))
        dv = jnp.concatenate(dv_all[h], axis=0)
        o = h * wide
        ds[0:rows, o : o + DK] = dq * dact[:, :DK]
        ds[0:rows, o + DK : o + 2 * DK] = dk * dact[:, DK : 2 * DK]
        ds[0:rows, o + 2 * DK : o + wide] = dv * dact[:, 2 * DK :]
    ahead = conv_masks(base, rows, ends, taps, -1)
    for h in range(heads):
        sl = slice(h * wide, (h + 1) * wide)
        own = ds[0:rows, sl]
        total = own * taps_ref[0:1, sl]
        dtaps_ref[0:8, sl] += jnp.sum((own * xs[8:, sl]).reshape(rows // 8, 8, wide), axis=0)
        for j in range(1, taps):
            total = total + (ds[j : j + rows, sl] * ahead[j - 1]) * taps_ref[j : j + 1, sl]
            dtaps_ref[8 * j : 8 * j + 8, sl] += jnp.sum(
                (own * (xs[8 - j : 8 - j + rows, sl] * masks[j - 1])).reshape(rows // 8, 8, wide), axis=0
            )
        dproj_ref[:, h * full : h * full + wide] = total.astype(bf16)
    first_ref[...] = ds[0:8, :]


DOT_QK = dot3
DOT_INV = dot3
DOT_WV = dot3
DOT_P = dot3
DOT_K = dot3
DOT_S = dot3
DOT_O = dot3
DOT_B = dot3
DOT_G = dot1


def mixer_forward(ends, proj, before, before_at, taps, rate, shift, gain, enter, *, heads, rows, start):
    total, width = proj.shape
    blocks = total // rows
    n = rows // CHUNK
    row = lambda i, e: (i, 0)
    same = lambda i, e: (0, 0)
    quad = lambda i, e: (i, 0, 0, 0)
    wide = 2 * DK + DV
    chunks = total // CHUNK
    kernel = functools.partial(forward_kernel, heads=heads, rows=rows, taps=taps.shape[0], start=start)
    wide_rows = pl.BlockSpec((rows, heads * DV), row)
    return pl.pallas_call(
        kernel,
        grid_spec=pltpu.PrefetchScalarGridSpec(
            num_scalar_prefetch=1,
            grid=(blocks,),
            in_specs=[
                pl.BlockSpec((rows, width), row),
                pl.BlockSpec((8, width), lambda i, e: (before_at, 0)),
                pl.BlockSpec(taps.shape, same),
                pl.BlockSpec(rate.shape, same),
                pl.BlockSpec(shift.shape, same),
                pl.BlockSpec(gain.shape, same),
                pl.BlockSpec(enter.shape, lambda i, e: (0, 0, 0)),
            ],
            out_specs=[
                wide_rows,
                wide_rows,
                wide_rows,
                pl.BlockSpec((n, heads, DK, DV), quad),
                pl.BlockSpec((n, heads, CHUNK, CHUNK), quad),
                pl.BlockSpec((n, heads, CHUNK, DK), quad),
                pl.BlockSpec((n, heads, DK, DK), quad),
                pl.BlockSpec(enter.shape, lambda i, e: (0, 0, 0)),
            ],
            scratch_shapes=[pltpu.VMEM((rows + 8, heads * wide), f32)],
        ),
        out_shape=[
            jax.ShapeDtypeStruct((total, heads * DV), bf16),
            jax.ShapeDtypeStruct((total, heads * DV), f32),
            jax.ShapeDtypeStruct((total, heads * DV), f32),
            jax.ShapeDtypeStruct((chunks, heads, DK, DV), f32),
            jax.ShapeDtypeStruct((chunks, heads, CHUNK, CHUNK), f32),
            jax.ShapeDtypeStruct((chunks, heads, CHUNK, DK), f32),
            jax.ShapeDtypeStruct((chunks, heads, DK, DK), f32),
            jax.ShapeDtypeStruct(enter.shape, f32),
        ],
        compiler_params=pltpu.CompilerParams(
            dimension_semantics=("arbitrary",), vmem_limit_bytes=56 * 1024 * 1024
        ),
        cost_estimate=pl.CostEstimate(
            flops=total * heads * 1_000_000, bytes_accessed=total * heads * 9_000, transcendentals=total * heads * 2_000
        ),
        name="mixer_forward",
    )(ends, proj, before, taps, rate, shift, gain, enter)


def mixer_backward(
    ends, proj, before, before_at, taps, rate, shift, gain, dgated, saved, leave, later, *, heads, rows, start
):
    total, width = proj.shape
    blocks = total // rows
    n = rows // CHUNK
    row = lambda s, e: (blocks - 1 - s, 0)
    halo = lambda s, e: (jnp.maximum((blocks - 1 - s) * (rows // 8) - 1, 0), 0)
    same = lambda s, e: (0, 0)
    quad = lambda s, e: (blocks - 1 - s, 0, 0, 0)
    wide = 2 * DK + DV
    kernel = functools.partial(
        backward_kernel, heads=heads, rows=rows, taps=taps.shape[0], blocks=blocks, start=start
    )
    wide_rows = pl.BlockSpec((rows, heads * DV), row)
    return pl.pallas_call(
        kernel,
        grid_spec=pltpu.PrefetchScalarGridSpec(
            num_scalar_prefetch=1,
            grid=(blocks,),
            in_specs=[
                pl.BlockSpec((rows, width), row),
                pl.BlockSpec((8, width), halo),
                pl.BlockSpec((8, width), lambda s, e: (before_at, 0)),
                pl.BlockSpec(taps.shape, same),
                pl.BlockSpec(rate.shape, same),
                pl.BlockSpec(shift.shape, same),
                pl.BlockSpec(gain.shape, same),
                wide_rows,
                wide_rows,
                wide_rows,
                pl.BlockSpec((n, heads, DK, DV), quad),
                pl.BlockSpec((n, heads, CHUNK, CHUNK), quad),
                pl.BlockSpec((n, heads, CHUNK, DK), quad),
                pl.BlockSpec((n, heads, DK, DK), quad),
                pl.BlockSpec(leave.shape, lambda s, e: (0, 0, 0)),
                pl.BlockSpec(later.shape, same),
            ],
            out_specs=[
                pl.BlockSpec((rows, width), row),
                pl.BlockSpec((8 * taps.shape[0], heads * wide), same),
                pl.BlockSpec((8, DV), same),
                pl.BlockSpec((16, 128), same),
                pl.BlockSpec(leave.shape, lambda s, e: (0, 0, 0)),
                pl.BlockSpec(later.shape, same),
            ],
            scratch_shapes=[
                pltpu.VMEM((rows + 8, heads * wide), f32),
                pltpu.VMEM((rows + 8, heads * wide), f32),
            ],
        ),
        out_shape=[
            jax.ShapeDtypeStruct((total, width), bf16),
            jax.ShapeDtypeStruct((8 * taps.shape[0], heads * wide), f32),
            jax.ShapeDtypeStruct((8, DV), f32),
            jax.ShapeDtypeStruct((16, 128), f32),
            jax.ShapeDtypeStruct(leave.shape, f32),
            jax.ShapeDtypeStruct(later.shape, f32),
        ],
        compiler_params=pltpu.CompilerParams(
            dimension_semantics=("arbitrary",), vmem_limit_bytes=56 * 1024 * 1024
        ),
        cost_estimate=pl.CostEstimate(
            flops=total * heads * 1_000_000, bytes_accessed=total * heads * 9_000, transcendentals=total * heads * 2_000
        ),
        name="mixer_backward",
    )(ends, proj, proj, before, taps, rate, shift, gain, dgated, *saved, leave, later)


FORWARD_ROWS = 512
BACKWARD_ROWS = 256
RUNS = 2


def rms_scale(values):
    return lax.rsqrt(jnp.mean(values * values, axis=-1, keepdims=True) + epsilon)


def norm_back(values, scale, gain, grad):
    u = gain * grad
    back = scale * u - values * (scale * scale * scale) * jnp.mean(values * u, axis=-1, keepdims=True)
    return back, jnp.sum(grad * (values * scale), axis=0)


def swap(x, axis, bit):
    size = lax.axis_size(axis)
    return lax.ppermute(x, axis, [(i, i ^ bit) for i in range(size)])


def exchange_roles(x):
    n = lax.axis_size("lo")
    return lax.ppermute(x, ("lo", "tensor"), [(a * n + b, b * n + a) for a in range(n) for b in range(n)])


def bits(size):
    return [1 << k for k in range(size.bit_length() - 1)]


def reversed_bits(n):
    order = [0]
    for bit in reversed(bits(n)):
        order = order + [k ^ bit for k in order]
    return order


def gather_first(x):
    return jnp.concatenate([x, swap(x, "lo", bits(lax.axis_size("lo"))[-1])], axis=0)


def gather_last(x):
    for bit in reversed(bits(lax.axis_size("lo"))[:-1]):
        x = jnp.concatenate([x, swap(x, "lo", bit)], axis=0)
    return x


def gather_rows(x):
    return gather_last(gather_first(x))


def halve(x, bit, kind):
    half = x.shape[0] // 2
    return x[:half].astype(f32) + swap(x[half:].astype(kind), "lo", bit).astype(f32)


def scatter_first(x):
    kind = x.dtype
    for bit in bits(lax.axis_size("lo"))[:-1]:
        x = halve(x, bit, kind)
    half = x.shape[0] // 2
    return x[:half], x[half:].astype(kind)


def scatter_last(kept, sent):
    return kept + swap(sent, "lo", bits(lax.axis_size("lo"))[-1]).astype(f32)


def sum_everywhere(x):
    for axis in ("lo", "tensor", "hi"):
        for bit in bits(lax.axis_size(axis)):
            x = x + swap(x, axis, bit)
    return x


def rank_of(key):
    return jnp.sum((key[..., None, :] < key[..., :, None]).astype(jnp.int32), axis=-1)


def after(x, *first):
    return lax.optimization_barrier((x, first))[0]


def widen(columns):
    return lax.all_gather(columns, ("hi", "tensor"), axis=0, tiled=True)


def narrow(columns):
    return lax.psum_scatter(columns.astype(bf16), ("hi", "tensor"), scatter_dimension=0, tiled=True)


def product(a, b, ca=1, cb=0, dtype=f32):
    return lax.dot_general(a, b, (((ca,), (cb,)), ((), ())), preferred_element_type=f32).astype(dtype)


def body(
    tokens,
    cotangent,
    lengths,
    token_order,
    token_return,
    w_mix,
    w_ba,
    conv_w,
    w_out,
    w_gate_up,
    w_down,
    gain_attn,
    gain_ffn,
    gain_out,
    decay_log,
    decay_bias,
):
    splits = lax.axis_size("lo")
    groups = lax.axis_size("hi") * splits
    me = lax.axis_index("lo")
    local_rows, model_width = tokens.shape
    group_rows = local_rows * splits
    per_peer = local_rows // groups
    weight_rows, heads, head_width = w_mix.shape
    units = w_down.shape[1]
    taps = conv_w.shape[2]
    conv_width = head_width - DV
    proj_width = heads * head_width

    spread = ("hi", "tensor")
    width = lax.axis_size("hi")
    span = jnp.arange(local_rows, dtype=jnp.int32)
    part_rows = width * per_peer

    send_rank = rank_of(token_return // group_rows * local_rows + token_return % local_rows)
    send_hot = (span[:, None] == send_rank[None, :]).astype(bf16)

    def across(rows):
        return lax.all_to_all(rows, spread, split_axis=0, concat_axis=0, tiled=True)

    def pack(rows):
        return product(send_hot, rows, dtype=bf16).reshape(groups, per_peer, -1)

    def by_part(rows):
        rows = jnp.transpose(rows.reshape(width, splits, per_peer, -1), (1, 0, 2, 3))
        return rows.reshape(local_rows, -1)

    def from_part(rows):
        rows = jnp.transpose(rows.reshape(splits, width, per_peer, model_width), (1, 0, 2, 3))
        return rows.reshape(groups, per_peer, model_width)

    def unpack(rows):
        return product(send_hot, rows.reshape(local_rows, model_width), 0, 0, bf16)

    place = token_return % local_rows
    lane = jnp.arange(128, dtype=jnp.int32)[None, :]
    digits = jnp.where(lane == 0, (place // 16)[:, None], jnp.where(lane == 1, (place % 16)[:, None], 0))
    tagged = jnp.concatenate([tokens, digits.astype(bf16)], axis=1)
    arrived = across(pack(tagged))
    packed_grad = across(pack(after(cotangent, arrived)))
    run_parts = splits // RUNS
    run_rows = run_parts * local_rows

    def in_parts(rows):
        rows = rows.reshape(splits, run_parts, part_rows, -1)
        return jnp.transpose(rows, (1, 0, 2, 3)).reshape(run_parts, local_rows, -1)

    def order_of(tags):
        tags = in_parts(tags)[:, :, :2].astype(jnp.int32)
        at = tags[:, :, 0] * 16 + tags[:, :, 1]
        return (at[:, None, :] == span[None, :, None]).astype(bf16)

    def to_sequence(order, rows):
        return lax.dot_general(
            order, in_parts(rows), (((2,), (1,)), ((0,), (0,))), preferred_element_type=f32
        ).astype(bf16).reshape(run_rows, -1)

    def from_sequence(order, rows):
        rows = lax.dot_general(
            order, rows.reshape(run_parts, local_rows, -1), (((1,), (1,)), ((0,), (0,))),
            preferred_element_type=f32,
        ).astype(bf16).reshape(run_parts, splits, part_rows, -1)
        return jnp.transpose(rows, (1, 0, 2, 3)).reshape(run_rows, -1)

    head_start = me * heads
    lanes = jnp.zeros((1, 128), f32)
    rate_row = lanes.at[0, 1 : 2 * heads : 2].set(lax.dynamic_slice_in_dim(decay_log, head_start, heads))
    shift_row = lanes.at[0, 1 : 2 * heads : 2].set(lax.dynamic_slice_in_dim(decay_bias, head_start, heads))
    own_lengths = exchange_roles(lengths)
    ends = jnp.sum(jnp.where(jnp.tri(SEQS, dtype=bool), own_lengths, 0), axis=1).astype(jnp.int32)
    small_at = proj_width
    conv_at = small_at + heads * w_ba.shape[2]
    spare = 128 - heads * w_ba.shape[2] - taps
    mix_own = exchange_roles(
        jnp.concatenate(
            [
                w_mix.reshape(weight_rows, proj_width).astype(bf16),
                w_ba.reshape(weight_rows, -1).astype(bf16),
                conv_w.reshape(weight_rows, taps).astype(bf16),
                jnp.zeros((weight_rows, spare), bf16),
                w_out.reshape(weight_rows, heads * DV).astype(bf16),
            ],
            axis=1,
        )
    )
    mix_all = widen(mix_own)
    arrived = by_part(after(arrived, ends, rate_row, shift_row))
    packed_in, tags = arrived[:, :model_width], arrived[:, model_width:]
    runs = range(RUNS)
    own_rows = local_rows // RUNS

    def split(rows):
        return [rows[r * own_rows : (r + 1) * own_rows] for r in runs]

    input_f32 = packed_in.astype(f32)
    input_scale = rms_scale(input_f32)
    input_runs = split(input_f32)
    normed_runs = split(jnp.concatenate([(input_f32 * input_scale * gain_attn).astype(bf16), tags], axis=1))
    gathered_0 = gather_rows(normed_runs[0])
    ffn_sent = jnp.concatenate(
        [w_gate_up.reshape(weight_rows, 2 * units).astype(bf16), w_down.astype(bf16)], axis=1
    )
    out_all = mix_all[:, small_at + 128 :]
    mix_all = mix_all[:, : small_at + 128]

    conv_all = mix_all[:, conv_at : conv_at + taps].reshape(-1, heads, taps).astype(f32)
    tap_rows = jnp.transpose(conv_all, (2, 1, 0)).reshape(taps, heads * conv_width)
    gain_row = gain_out[None]
    constants = (tap_rows, rate_row, shift_row, gain_row)

    state = jnp.zeros((heads, DK, DV), f32)

    def ahead(r):
        return (projected[r - 1], run_rows // 8 - 1) if r else (projected[r], 0)

    def mix_forward(r, state):
        return mixer_forward(
            ends, projected[r], *ahead(r), *constants, state, heads=heads, rows=FORWARD_ROWS, start=r * run_rows
        )

    def feed_forward(r, normed_mid):
        place = (r * run_parts + jnp.arange(run_parts, dtype=jnp.int32))[:, None, None] * local_rows
        alive = (place + span[None, :, None] < ends[SEQS - 1]).astype(bf16)
        live = from_sequence(orders[r], jnp.broadcast_to(alive, (run_parts, local_rows, 128)))[:, :1].astype(f32)
        grad_hidden = product(grad_all[r], w_last) * live
        gate_up = product(normed_mid, w_pair)
        gate, up = gate_up[:, :units], gate_up[:, units:]
        s = sigmoid(gate)
        hidden = (gate * s * up * live).astype(bf16)
        grad_pair = jnp.concatenate(
            [grad_hidden * up * (s * (1.0 + gate * (1.0 - s))), grad_hidden * (gate * s)], axis=1
        ).astype(bf16)
        return hidden, grad_pair, product(grad_pair, w_pair, 1, 1, bf16)

    def normed_of(middle):
        scale = rms_scale(middle)
        return scale, (middle * scale * gain_ffn).astype(bf16)

    constants = (tap_rows, rate_row, shift_row, gain_row)
    orders = [order_of(gathered_0[:, model_width:])]
    seq_0 = to_sequence(orders[0], gathered_0[:, :model_width])
    projected = [product(seq_0, mix_all)]
    gathered_1 = gather_rows(normed_runs[1])
    orders.append(order_of(gathered_1[:, model_width:]))
    seq_1 = to_sequence(orders[1], gathered_1[:, :model_width])
    ffn_own = exchange_roles(after(ffn_sent, gathered_1))
    projected[0], seq_1, ffn_own, packed_grad = lax.optimization_barrier(
        (projected[0], seq_1, ffn_own, by_part(packed_grad))
    )
    ffn_all = widen(ffn_own)
    *saved_0, state = mix_forward(0, state)
    crossed = swap(packed_grad, "lo", bits(splits)[-1])
    saved_0, crossed = lax.optimization_barrier((saved_0, crossed))
    grad_runs = split(packed_grad)
    terms_0 = product(from_sequence(orders[0], saved_0[0]), out_all, 1, 1)
    projected.append(product(after(seq_1, terms_0), mix_all))
    kept_0, sent_0 = scatter_first(terms_0)
    projected[1], kept_0, sent_0 = lax.optimization_barrier((projected[1], kept_0, sent_0))
    grad_all = [gather_last(jnp.concatenate(x, axis=0)) for x in zip(grad_runs, split(crossed))]
    *saved_1, state = mix_forward(1, state)
    middle_0 = input_runs[0] + after(scatter_last(kept_0, sent_0), saved_1[0])
    scale_0, normed_mid_0 = normed_of(middle_0)
    terms_1 = product(from_sequence(orders[1], saved_1[0]), out_all, 1, 1)
    first_0 = gather_first(normed_mid_0)
    kept_1, sent_1 = scatter_first(terms_1)
    kept_1, sent_1, first_0, ffn_all = lax.optimization_barrier((kept_1, sent_1, first_0, ffn_all))
    w_pair, w_last = ffn_all[:, : 2 * units], ffn_all[:, 2 * units :]
    normed_mid_0 = gather_last(first_0)

    hidden_0, pair_0, grad_terms_0 = feed_forward(0, normed_mid_0)
    middle_1 = input_runs[1] + after(scatter_last(kept_1, sent_1), grad_terms_0)
    scale_1, normed_mid_1 = normed_of(middle_1)
    first_1 = gather_first(normed_mid_1)
    grad_kept_0, grad_sent_0 = scatter_first(grad_terms_0)
    grad_kept_0, grad_sent_0, first_1 = lax.optimization_barrier((grad_kept_0, grad_sent_0, first_1))
    normed_mid_1 = gather_last(first_1)
    hidden_1, pair_1, grad_terms_1 = feed_forward(1, normed_mid_1)
    grad_kept_1, grad_sent_1 = scatter_first(grad_terms_1)
    grad_kept_1, grad_sent_1, grad_terms_0_sum = lax.optimization_barrier(
        (grad_kept_1, grad_sent_1, scatter_last(grad_kept_0, grad_sent_0))
    )
    hidden_0, pair_0, hidden_1, pair_1 = after((hidden_0, pair_0, hidden_1, pair_1), grad_sent_1)
    grad_pairs = product(normed_mid_0, pair_0, 0, 0) + product(normed_mid_1, pair_1, 0, 0)
    grad_terms_1_sum = after(scatter_last(grad_kept_1, grad_sent_1), grad_pairs)
    back_1, gain_1 = norm_back(middle_1, scale_1, gain_ffn, grad_terms_1_sum)
    grad_middle_1 = grad_runs[1].astype(f32) + back_1
    first_1 = gather_first(grad_middle_1.astype(bf16))
    hidden_0, hidden_1 = after((hidden_0, hidden_1), grad_middle_1)
    grad_last = product(grad_all[0], hidden_0, 0, 0) + product(grad_all[1], hidden_1, 0, 0)
    layer_terms = [product(h, w_last, 1, 1, bf16) for h in (hidden_0, hidden_1)]
    back_0, gain_0 = norm_back(middle_0, scale_0, gain_ffn, after(grad_terms_0_sum, grad_middle_1))
    grad_gain_ffn = gain_0 + gain_1
    grad_middle_0 = grad_runs[0].astype(f32) + back_0
    first_1, grad_last, layer_terms, grad_low_0 = lax.optimization_barrier(
        (first_1, grad_last, layer_terms, grad_middle_0.astype(bf16))
    )
    grad_mid_seq_1 = to_sequence(orders[1], gather_last(first_1))
    grad_ffn = narrow(jnp.concatenate([grad_pairs.astype(bf16), grad_last.astype(bf16)], axis=1))

    def mix_backward(r, grad_gated, saved, leave, later):
        return mixer_backward(
            ends, projected[r], *ahead(r), *constants, grad_gated, saved[1:], leave, later,
            heads=heads, rows=BACKWARD_ROWS, start=r * run_rows,
        )

    leave = jnp.zeros((heads, DK, DV), f32)
    later = jnp.zeros((8, heads * conv_width), f32)
    layer_parts = [scatter_first(x) for x in layer_terms]
    grad_gated_1 = product(grad_mid_seq_1, out_all)
    grad_gated_1, grad_low_0, layer_parts = lax.optimization_barrier((grad_gated_1, grad_low_0, layer_parts))
    grad_proj_1, *sums_1, leave, later = mix_backward(1, grad_gated_1, saved_1, leave, later)
    layer_sums = [scatter_last(*x) for x in layer_parts]
    grad_proj_1, first_0, layer_sums = lax.optimization_barrier((grad_proj_1, gather_first(grad_low_0), layer_sums))
    grad_mid_seq_0 = to_sequence(orders[0], gather_last(first_0))
    grad_gated_0 = product(grad_mid_seq_0, out_all)
    layer_rows = jnp.concatenate([m + x for m, x in zip((middle_0, middle_1), layer_sums)], axis=0)
    layer_rows = from_part(layer_rows.astype(bf16))
    grad_gated_0, layer_rows = lax.optimization_barrier((grad_gated_0, layer_rows))
    grad_proj_0, *sums_0, leave, later = mix_backward(0, grad_gated_0, saved_0, leave, later)
    grad_proj_0, grad_ffn, layer_back = lax.optimization_barrier((grad_proj_0, grad_ffn, across(layer_rows)))
    grad_taps, grad_gain_out, grad_decay = [a + b for a, b in zip(sums_0, sums_1)]
    grad_conv = jnp.sum(grad_taps.reshape(taps, 8, heads, conv_width), axis=1)
    grad_conv = jnp.transpose(grad_conv, (2, 1, 0)).reshape(-1, taps)
    grad_mix = product(seq_0, grad_proj_0, 0, 0) + product(seq_1, grad_proj_1, 0, 0)
    grad_mix = (grad_mix + jnp.pad(grad_conv, ((0, 0), (conv_at, spare)))).astype(bf16)
    grad_out_w = product(grad_mid_seq_0, saved_0[0], 0, 0) + product(grad_mid_seq_1, saved_1[0], 0, 0)
    grad_mix = jnp.concatenate([grad_mix, grad_out_w.astype(bf16)], axis=1)
    grad_mix, *proj_parts = lax.optimization_barrier((grad_mix, grad_proj_0, grad_proj_1))
    normed_terms = [from_sequence(orders[r], product(proj_parts[r], mix_all, 1, 1, bf16)) for r in runs]
    grad_mix = exchange_roles(narrow(grad_mix)).astype(f32)
    normed_terms = [x.reshape(splits, own_rows, model_width) for x in normed_terms]
    normed_terms = jnp.concatenate(normed_terms, axis=1).reshape(group_rows, model_width)
    grad_normed = scatter_last(*scatter_first(normed_terms))
    grad_normed, grad_ffn = lax.optimization_barrier((grad_normed, exchange_roles(grad_ffn)))
    grad_ffn = grad_ffn.astype(f32)
    grad_input_norm, grad_gain_attn = norm_back(input_f32, input_scale, gain_attn, grad_normed)
    grad_middle = jnp.concatenate([grad_middle_0, grad_middle_1], axis=0)
    input_grad = unpack(across(from_part((grad_middle + grad_input_norm).astype(bf16))))
    layer_out = unpack(layer_back)

    head_total = decay_log.shape[0]
    decay_sums = jnp.sum(grad_decay.reshape(2, 8, 128), axis=1)[:, 1 : 2 * heads : 2]
    decay_full = lax.dynamic_update_slice(jnp.zeros((2, head_total), f32), decay_sums, (0, head_start))
    flat = jnp.concatenate(
        [grad_gain_attn, grad_gain_ffn, jnp.sum(grad_gain_out, axis=0), decay_full.reshape(-1)]
    )
    flat = sum_everywhere(jnp.pad(flat, (0, -flat.shape[0] % 1024)).reshape(8, -1)).reshape(-1)
    at = 0
    sums = []
    for size in (model_width, model_width, gain_out.shape[0], head_total, head_total):
        sums.append(flat[at : at + size])
        at += size
    return (
        layer_out,
        input_grad,
        grad_mix[:, :small_at].reshape(w_mix.shape),
        grad_mix[:, small_at:conv_at].reshape(w_ba.shape),
        grad_mix[:, conv_at : conv_at + taps].reshape(conv_w.shape),
        grad_mix[:, small_at + 128 :].reshape(w_out.shape),
        grad_ffn[:, : 2 * units].reshape(w_gate_up.shape),
        grad_ffn[:, 2 * units :],
        *sums,
    )


def solution(mesh):
    dp, splits = mesh.shape["dp"], mesh.shape["tensor"]
    roles = Mesh(mesh.devices.reshape(dp // splits, splits, splits), ("hi", "lo", "tensor"))
    group = ("hi", "lo")
    rows = P((*group, "tensor"))
    by_head = P(group, "tensor", None)
    by_unit = (P(group, None, "tensor"), P(group, "tensor"))
    return jax.shard_map(
        body,
        mesh=roles,
        in_specs=(rows, rows, P(group), rows, rows, by_head, by_head, by_head, by_head, *by_unit)
        + (P(),) * 5,
        out_specs=(rows, rows, by_head, by_head, by_head, by_head, *by_unit) + (P(),) * 5,
        check_vma=False,
    )
```

```python
import functools
import jax
import jax.numpy as jnp
from jax import lax
from jax.experimental import pallas as pl
from jax.experimental.pallas import tpu as pltpu
from jax.sharding import Mesh
from jax.sharding import PartitionSpec as P

DK = 128
DV = 256
SEQS = 3
CHUNK = 128
epsilon = 1e-06
f32 = jnp.float32
bf16 = jnp.bfloat16


def dot(a, b, ca=1, cb=0):
    return lax.dot_general(a, b, (((ca,), (cb,)), ((), ())), preferred_element_type=f32)


def halves(x):
    high = x.astype(bf16)
    return high, (x - high.astype(f32)).astype(bf16)


def dot1(a, b, ca=1, cb=0):
    return dot(a.astype(bf16), b.astype(bf16), ca, cb)


def dot3(a, b, ca=1, cb=0):
    ah, al = halves(a)
    bh, bl = halves(b)
    return dot(jnp.concatenate([ah, al, ah], axis=ca), jnp.concatenate([bh, bh, bl], axis=cb), ca, cb)


def dot_exact(a, b, ca=1, cb=0):
    ah = a.astype(bf16)
    bh, bl = halves(b)
    bt = (b - bh.astype(f32) - bl.astype(f32)).astype(bf16)
    return dot(ah, bh, ca, cb) + (dot(ah, bl, ca, cb) + dot(ah, bt, ca, cb))


def sigmoid(x):
    return 1.0 / (1.0 + jnp.exp(-x))


def segment_of(position, ends):
    return sum((position >= e).astype(jnp.int32) for e in ends)


def iota(shape, axis):
    return lax.broadcasted_iota(jnp.int32, shape, axis)


def conv_masks(base, rows, ends, taps, sign):
    t = base + iota((rows, 1), 0)
    own = segment_of(t, ends)
    masks = []
    for j in range(1, taps):
        other = t - sign * j
        same = segment_of(other, ends) == own
        masks.append(jnp.where(same & (other >= 0), 1.0, 0.0))
    return masks


def chunk_terms(base, ends, g_col, g_row, q, k, beta):
    c = CHUNK
    ti = base + iota((c, 1), 0)
    tj = base + iota((1, c), 1)
    si = segment_of(ti, ends)
    sj = segment_of(tj, ends)
    ii = iota((c, c), 0)
    jj = iota((c, c), 1)
    decay = jnp.where((si == sj) & (ii >= jj), jnp.exp(jnp.minimum(g_col - g_row, 0.0)), 0.0)
    before = jnp.where(base > 0, segment_of(base - 1, ends), -1)
    last = segment_of(base + c - 1, ends)
    carry = jnp.where(si == before, jnp.exp(g_col), 0.0)
    g_last = g_col[c - 1 :, :]
    tail = jnp.where(si == last, jnp.exp(jnp.minimum(g_last - g_col, 0.0)), 0.0)
    return decay, carry, tail, ii, jj


def invert(lower, ii, jj, mul):
    first = ((ii ^ jj) == 1) & (ii > jj)
    eye = jnp.where(ii == jj, 1.0, 0.0)
    inv = [eye - jnp.where(first, a, 0.0) for a in lower]
    size = 2
    while size < CHUNK:
        joins = ((ii // (2 * size)) == (jj // (2 * size))) & ((ii & size) != 0) & ((jj & size) == 0)
        half = [mul(jnp.where(joins, a, 0.0), t) for a, t in zip(lower, inv)]
        inv = [t - mul(t, x) for t, x in zip(inv, half)]
        size *= 2
    return inv


def silu_parts(u):
    s = sigmoid(u)
    return u * s, s


def forward_kernel(
    ends_ref, proj_ref, before_ref, taps_ref, rate_ref, shift_ref, gain_ref, enter_ref,
    gated_ref, o_ref, u_ref, s_ref, t_ref, qe_ref, m_ref, state,
    xs, *, heads, rows, taps, start,
):
    i = pl.program_id(0)
    wide = 2 * DK + DV
    full = wide + DV
    ends = [ends_ref[k] for k in range(SEQS)]
    base = start + i * rows
    c = CHUNK

    @pl.when(i == 0)
    def _():
        for h in range(heads):
            xs[0:8, h * wide : (h + 1) * wide] = before_ref[:, h * full : h * full + wide]
        state[...] = enter_ref[...]

    @pl.when(i > 0)
    def _():
        xs[0:8, :] = xs[rows : rows + 8, :]

    for h in range(heads):
        xs[8:, h * wide : (h + 1) * wide] = proj_ref[:, h * full : h * full + wide]
    small = proj_ref[:, heads * full :]
    beta_all = sigmoid(small)
    shifted = small + shift_ref[...]
    ld_all = -jnp.exp(rate_ref[...]) * (jnp.maximum(shifted, 0.0) + jnp.log1p(jnp.exp(-jnp.abs(shifted))))
    masks = conv_masks(base, rows, ends, taps, 1)
    qs, ks, vs = [], [], []
    for h in range(heads):
        sl = slice(h * wide, (h + 1) * wide)
        run = xs[8:, sl] * taps_ref[0:1, sl]
        for j in range(1, taps):
            run = run + (xs[8 - j : 8 - j + rows, sl] * masks[j - 1]) * taps_ref[j : j + 1, sl]
        act = run * sigmoid(run)
        q, k, v = act[:, :DK], act[:, DK : 2 * DK], act[:, 2 * DK :]
        qs.append(q * (lax.rsqrt(jnp.sum(q * q, axis=-1, keepdims=True) + epsilon) * DK ** (-0.5)))
        ks.append(k * lax.rsqrt(jnp.sum(k * k, axis=-1, keepdims=True) + epsilon))
        vs.append(v)
    lower_tri = jnp.where(iota((c, c), 0) >= iota((c, c), 1), 1.0, 0.0)
    n = rows // c
    probs = []
    for b in range(n):
        rs = slice(b * c, (b + 1) * c)
        g_all = dot_exact(lower_tri, ld_all[rs])
        g_t = g_all.T
        for h in range(heads):
            q, k, v = qs[h][rs], ks[h][rs], vs[h][rs]
            beta = beta_all[rs, 2 * h : 2 * h + 1]
            g_col = g_all[:, 2 * h + 1 : 2 * h + 2]
            g_row = g_t[2 * h + 1 : 2 * h + 2, :]
            decay, carry, tail, ii, jj = chunk_terms(base + b * c, ends, g_col, g_row, q, k, beta)
            qkk = DOT_QK(jnp.concatenate([q, k], axis=0), k, 1, 1)
            p = qkk[:c] * decay
            a = jnp.where(ii > jj, qkk[c:] * decay, 0.0) * beta
            probs.append(dict(b=b, h=h, q=q, k=k, v=v, beta=beta, carry=carry, tail=tail, p=p, a=a))
    inv = invert([x["a"] for x in probs], ii, jj, DOT_INV)
    for x, t in zip(probs, inv):
        x["t"] = t
        rhs = jnp.concatenate([(x["beta"] * x["carry"]) * x["k"], x["beta"] * x["v"]], axis=1)
        x["wv"] = DOT_WV(t, rhs)
    for x in probs:
        pwv = DOT_P(x["p"], x["wv"])
        x["qe"] = x["carry"] * x["q"] - pwv[:, :DK]
        x["pv"] = pwv[:, DK:]
        kwv = DOT_K(x["tail"] * x["k"], x["wv"], 0, 0)
        c_last = x["carry"][c - 1 :, :]
        x["m"] = jnp.where(ii == jj, c_last, 0.0) - kwv[:, :DK]
        x["bf"] = kwv[:, DK:]
    for x in probs:
        b, h = x["b"], x["h"]
        s = state[h]
        s_ref[b, h] = s
        t_ref[b, h] = x["t"]
        qe_ref[b, h] = x["qe"]
        m_ref[b, h] = x["m"]
        w = x["wv"][:, :DK]
        state[h] = x["bf"] + DOT_S(x["m"], s)
        wq = DOT_O(jnp.concatenate([w, x["qe"]], axis=0), s)
        u_ref[b * c : (b + 1) * c, h * DV : (h + 1) * DV] = x["wv"][:, DK:] - wq[:c]
        o_ref[b * c : (b + 1) * c, h * DV : (h + 1) * DV] = x["pv"] + wq[c:]
    live = jnp.where(segment_of(base + iota((rows, 1), 0), ends) < SEQS, 1.0, 0.0)
    for h in range(heads):
        o = o_ref[:, h * DV : (h + 1) * DV]
        z = proj_ref[:, h * full + wide : (h + 1) * full]
        r = lax.rsqrt(jnp.mean(o * o, axis=-1, keepdims=True) + epsilon)
        gated_ref[:, h * DV : (h + 1) * DV] = (o * (r * live) * gain_ref[...] * (z * sigmoid(z))).astype(bf16)


def backward_kernel(
    ends_ref, proj_ref, halo_ref, before_ref, taps_ref, rate_ref, shift_ref, gain_ref,
    dgated_ref, o_ref, u_ref, s_ref, t_ref, qe_ref, m_ref, leave_ref, later_ref,
    dproj_ref, dtaps_ref, dgain_ref, ddecay_ref, dstate, first_ref,
    xs, ds, *, heads, rows, taps, blocks, start,
):
    step = pl.program_id(0)
    i = blocks - 1 - step
    wide = 2 * DK + DV
    full = wide + DV
    ends = [ends_ref[k] for k in range(SEQS)]
    base = start + i * rows
    c = CHUNK

    @pl.when(step == 0)
    def _():
        ds[rows : rows + 8, :] = later_ref[...]
        dstate[...] = leave_ref[...]
        dtaps_ref[...] = jnp.zeros_like(dtaps_ref)
        dgain_ref[...] = jnp.zeros_like(dgain_ref)
        ddecay_ref[...] = jnp.zeros_like(ddecay_ref)

    @pl.when(step > 0)
    def _():
        ds[rows : rows + 8, :] = ds[0:8, :]

    for h in range(heads):
        cols = slice(h * full, h * full + wide)
        xs[0:8, h * wide : (h + 1) * wide] = jnp.where(i == 0, before_ref[:, cols], halo_ref[:, cols])
        xs[8:, h * wide : (h + 1) * wide] = proj_ref[:, h * full : h * full + wide]
    small = proj_ref[:, heads * full :]
    beta_all = sigmoid(small)
    shifted = small + shift_ref[...]
    rate = -jnp.exp(rate_ref[...])
    ld_all = rate * (jnp.maximum(shifted, 0.0) + jnp.log1p(jnp.exp(-jnp.abs(shifted))))
    masks = conv_masks(base, rows, ends, taps, 1)
    live = jnp.where(segment_of(base + iota((rows, 1), 0), ends) < SEQS, 1.0, 0.0)
    acts = []
    dos = []
    for h in range(heads):
        sl = slice(h * wide, (h + 1) * wide)
        run = xs[8:, sl] * taps_ref[0:1, sl]
        for j in range(1, taps):
            run = run + (xs[8 - j : 8 - j + rows, sl] * masks[j - 1]) * taps_ref[j : j + 1, sl]
        sg = sigmoid(run)
        act = run * sg
        dact = sg * (1.0 + run * (1.0 - sg))
        q, k, v = act[:, :DK], act[:, DK : 2 * DK], act[:, 2 * DK :]
        rq = lax.rsqrt(jnp.sum(q * q, axis=-1, keepdims=True) + epsilon)
        rk = lax.rsqrt(jnp.sum(k * k, axis=-1, keepdims=True) + epsilon)
        acts.append((q * rq, k * rk, v, dact, rq, rk))
        o = o_ref[:, h * DV : (h + 1) * DV]
        z = proj_ref[:, h * full + wide : (h + 1) * full]
        dg = dgated_ref[:, h * DV : (h + 1) * DV] * live
        r = lax.rsqrt(jnp.mean(o * o, axis=-1, keepdims=True) + epsilon)
        nrm = o * r
        sz = sigmoid(z)
        dz = dg * nrm * gain_ref[...] * (sz * (1.0 + z * (1.0 - sz)))
        dng = dg * (z * sz)
        dgain_ref[...] += jnp.sum((dng * nrm).reshape(rows // 8, 8, DV), axis=0)
        dn = dng * gain_ref[...]
        dos.append(r * (dn - nrm * jnp.mean(dn * nrm, axis=-1, keepdims=True)))
        dproj_ref[:, h * full + wide : (h + 1) * full] = dz.astype(bf16)
    low_i = iota((c, c), 0)
    low_j = iota((c, c), 1)
    lower_tri = jnp.where(low_i >= low_j, 1.0, 0.0)
    upper_tri = jnp.where(low_i <= low_j, 1.0, 0.0)
    strict_low = jnp.where(low_i > low_j, 1.0, 0.0)
    n = rows // c
    probs = []
    for b in reversed(range(n)):
        rs = slice(b * c, (b + 1) * c)
        g_all = dot_exact(lower_tri, ld_all[rs])
        g_t = g_all.T
        for h in range(heads):
            q, k, v = acts[h][0][rs] * DK ** (-0.5), acts[h][1][rs], acts[h][2][rs]
            beta = beta_all[rs, 2 * h : 2 * h + 1]
            g_col = g_all[:, 2 * h + 1 : 2 * h + 2]
            g_row = g_t[2 * h + 1 : 2 * h + 2, :]
            decay, carry, tail, ii, jj = chunk_terms(base + b * c, ends, g_col, g_row, q, k, beta)
            qkk = DOT_QK(jnp.concatenate([q, k], axis=0), k, 1, 1)
            p = qkk[:c] * decay
            dkk = jnp.where(ii > jj, qkk[c:] * decay, 0.0)
            do = dos[h][rs]
            u = u_ref[rs, h * DV : (h + 1) * DV]
            dp = DOT_B(do, u, 1, 1)
            pdo = DOT_B(p, do, 0, 0)
            qdo = DOT_B(qe_ref[b, h], do, 0, 0)
            f = DOT_B(do, s_ref[b, h], 1, 1)
            probs.append(dict(b=b, h=h, q=q, k=k, v=v, beta=beta, carry=carry, tail=tail, decay=decay, p=p, dkk=dkk,
                              do=do, u=u, dp=dp, pdo=pdo, qdo=qdo, f=f))
    for x in probs:
        b, h = x["b"], x["h"]
        dnext = dstate[h]
        x["dnext"] = dnext
        dstate[h] = DOT_S(m_ref[b, h], dnext, 0, 0) + x["qdo"]
    for x in probs:
        du = x["pdo"] + DOT_B(x["tail"] * x["k"], x["dnext"])
        x["dr"] = DOT_B(t_ref[x["b"], x["h"]], du, 0, 0)
        x["j"] = DOT_B(x["u"], x["dnext"], 1, 1)
    dq_all = [[None] * n for _ in range(heads)]
    dk_all = [[None] * n for _ in range(heads)]
    dv_all = [[None] * n for _ in range(heads)]
    dsmall = [[None] * heads for _ in range(n)]
    lane = iota((c, DK), 1)
    for x in probs:
        b, h, q, k, beta, carry = x["b"], x["h"], x["q"], x["k"], x["beta"], x["carry"]
        dr = x["dr"]
        s = s_ref[b, h]
        neg = DOT_B(dr, x["u"], 1, 1)
        hh = DOT_B(dr, s, 1, 1)
        neg = jnp.where(ii > jj, neg, 0.0)
        adk = neg * x["dkk"]
        dbeta = (
            jnp.sum(dr * x["v"], axis=-1, keepdims=True)
            - carry * jnp.sum(k * hh, axis=-1, keepdims=True)
            - jnp.sum(adk, axis=-1, keepdims=True)
        )
        dcarry = jnp.sum(q * x["f"], axis=-1, keepdims=True) - beta * jnp.sum(k * hh, axis=-1, keepdims=True)
        e = x["dp"] * x["p"] - beta * adk
        dqk = x["dp"] * x["decay"]
        dkk = -(neg * beta) * jnp.where(ii > jj, x["decay"], 0.0)
        dtail = x["tail"] * jnp.sum(k * x["j"], axis=-1, keepdims=True)
        dcl = carry[c - 1 :, :] * jnp.sum(x["dnext"] * s, keepdims=True)
        col = carry * dcarry + jnp.where(iota((c, 1), 0) == c - 1, dcl, 0.0)
        straddle = jnp.where(ii > jj, dot_exact(upper_tri, e), 0.0)
        both = dot_exact(upper_tri, jnp.where(lane == 0, col, 0.0)) + dot_exact(
            strict_low, jnp.where(lane == 0, dtail, 0.0)
        )
        dld = jnp.sum(straddle, axis=-1, keepdims=True) + both[:, 0:1]
        dq_all[h][b] = carry * x["f"] + DOT_G(dqk, k)
        dk_all[h][b] = (
            x["tail"] * x["j"] - (carry * beta) * hh + DOT_G(dqk, q, 0, 0) + DOT_G(dkk, k) + DOT_G(dkk, k, 0, 0)
        )
        dv_all[h][b] = beta * dr
        dsmall[b][h] = (dbeta, dld)
    for b in range(n):
        rs = slice(b * c, (b + 1) * c)
        tile = jnp.zeros((c, DK), f32)
        for h in range(heads):
            dbeta, dld = dsmall[b][h]
            tile = jnp.where(lane == 2 * h, dbeta, jnp.where(lane == 2 * h + 1, dld, tile))
        bet = beta_all[rs]
        dshift = rate * tile * sigmoid(shifted[rs])
        even = (lane & 1) == 0
        inside = lane < 2 * heads
        ddecay_ref[0:8, :] += jnp.sum(jnp.where(even, 0.0, tile * ld_all[rs]).reshape(c // 8, 8, DK), axis=0)
        ddecay_ref[8:16, :] += jnp.sum(jnp.where(even, 0.0, dshift).reshape(c // 8, 8, DK), axis=0)
        dproj_ref[rs, heads * full :] = jnp.where(
            inside, jnp.where(even, tile * (bet * (1.0 - bet)), dshift), 0.0
        ).astype(bf16)
    for h in range(heads):
        qn, kn, v, dact, rq, rk = acts[h]
        dq = jnp.concatenate(dq_all[h], axis=0) * DK ** (-0.5)
        dk = jnp.concatenate(dk_all[h], axis=0)
        dq = rq * (dq - qn * jnp.sum(dq * qn, axis=-1, keepdims=True))
        dk = rk * (dk - kn * jnp.sum(dk * kn, axis=-1, keepdims=True))
        dv = jnp.concatenate(dv_all[h], axis=0)
        o = h * wide
        ds[0:rows, o : o + DK] = dq * dact[:, :DK]
        ds[0:rows, o + DK : o + 2 * DK] = dk * dact[:, DK : 2 * DK]
        ds[0:rows, o + 2 * DK : o + wide] = dv * dact[:, 2 * DK :]
    ahead = conv_masks(base, rows, ends, taps, -1)
    for h in range(heads):
        sl = slice(h * wide, (h + 1) * wide)
        own = ds[0:rows, sl]
        total = own * taps_ref[0:1, sl]
        dtaps_ref[0:8, sl] += jnp.sum((own * xs[8:, sl]).reshape(rows // 8, 8, wide), axis=0)
        for j in range(1, taps):
            total = total + (ds[j : j + rows, sl] * ahead[j - 1]) * taps_ref[j : j + 1, sl]
            dtaps_ref[8 * j : 8 * j + 8, sl] += jnp.sum(
                (own * (xs[8 - j : 8 - j + rows, sl] * masks[j - 1])).reshape(rows // 8, 8, wide), axis=0
            )
        dproj_ref[:, h * full : h * full + wide] = total.astype(bf16)
    first_ref[...] = ds[0:8, :]


DOT_QK = dot3
DOT_INV = dot3
DOT_WV = dot3
DOT_P = dot3
DOT_K = dot3
DOT_S = dot3
DOT_O = dot3
DOT_B = dot3
DOT_G = dot1


def mixer_forward(ends, proj, before, before_at, taps, rate, shift, gain, enter, *, heads, rows, start):
    total, width = proj.shape
    blocks = total // rows
    n = rows // CHUNK
    row = lambda i, e: (i, 0)
    same = lambda i, e: (0, 0)
    quad = lambda i, e: (i, 0, 0, 0)
    wide = 2 * DK + DV
    chunks = total // CHUNK
    kernel = functools.partial(forward_kernel, heads=heads, rows=rows, taps=taps.shape[0], start=start)
    wide_rows = pl.BlockSpec((rows, heads * DV), row)
    return pl.pallas_call(
        kernel,
        grid_spec=pltpu.PrefetchScalarGridSpec(
            num_scalar_prefetch=1,
            grid=(blocks,),
            in_specs=[
                pl.BlockSpec((rows, width), row),
                pl.BlockSpec((8, width), lambda i, e: (before_at, 0)),
                pl.BlockSpec(taps.shape, same),
                pl.BlockSpec(rate.shape, same),
                pl.BlockSpec(shift.shape, same),
                pl.BlockSpec(gain.shape, same),
                pl.BlockSpec(enter.shape, lambda i, e: (0, 0, 0)),
            ],
            out_specs=[
                wide_rows,
                wide_rows,
                wide_rows,
                pl.BlockSpec((n, heads, DK, DV), quad),
                pl.BlockSpec((n, heads, CHUNK, CHUNK), quad),
                pl.BlockSpec((n, heads, CHUNK, DK), quad),
                pl.BlockSpec((n, heads, DK, DK), quad),
                pl.BlockSpec(enter.shape, lambda i, e: (0, 0, 0)),
            ],
            scratch_shapes=[pltpu.VMEM((rows + 8, heads * wide), f32)],
        ),
        out_shape=[
            jax.ShapeDtypeStruct((total, heads * DV), bf16),
            jax.ShapeDtypeStruct((total, heads * DV), f32),
            jax.ShapeDtypeStruct((total, heads * DV), f32),
            jax.ShapeDtypeStruct((chunks, heads, DK, DV), f32),
            jax.ShapeDtypeStruct((chunks, heads, CHUNK, CHUNK), f32),
            jax.ShapeDtypeStruct((chunks, heads, CHUNK, DK), f32),
            jax.ShapeDtypeStruct((chunks, heads, DK, DK), f32),
            jax.ShapeDtypeStruct(enter.shape, f32),
        ],
        compiler_params=pltpu.CompilerParams(
            dimension_semantics=("arbitrary",), vmem_limit_bytes=56 * 1024 * 1024
        ),
        cost_estimate=pl.CostEstimate(
            flops=total * heads * 1_000_000, bytes_accessed=total * heads * 9_000, transcendentals=total * heads * 2_000
        ),
        name="mixer_forward",
    )(ends, proj, before, taps, rate, shift, gain, enter)


def mixer_backward(
    ends, proj, before, before_at, taps, rate, shift, gain, dgated, saved, leave, later, *, heads, rows, start
):
    total, width = proj.shape
    blocks = total // rows
    n = rows // CHUNK
    row = lambda s, e: (blocks - 1 - s, 0)
    halo = lambda s, e: (jnp.maximum((blocks - 1 - s) * (rows // 8) - 1, 0), 0)
    same = lambda s, e: (0, 0)
    quad = lambda s, e: (blocks - 1 - s, 0, 0, 0)
    wide = 2 * DK + DV
    kernel = functools.partial(
        backward_kernel, heads=heads, rows=rows, taps=taps.shape[0], blocks=blocks, start=start
    )
    wide_rows = pl.BlockSpec((rows, heads * DV), row)
    return pl.pallas_call(
        kernel,
        grid_spec=pltpu.PrefetchScalarGridSpec(
            num_scalar_prefetch=1,
            grid=(blocks,),
            in_specs=[
                pl.BlockSpec((rows, width), row),
                pl.BlockSpec((8, width), halo),
                pl.BlockSpec((8, width), lambda s, e: (before_at, 0)),
                pl.BlockSpec(taps.shape, same),
                pl.BlockSpec(rate.shape, same),
                pl.BlockSpec(shift.shape, same),
                pl.BlockSpec(gain.shape, same),
                wide_rows,
                wide_rows,
                wide_rows,
                pl.BlockSpec((n, heads, DK, DV), quad),
                pl.BlockSpec((n, heads, CHUNK, CHUNK), quad),
                pl.BlockSpec((n, heads, CHUNK, DK), quad),
                pl.BlockSpec((n, heads, DK, DK), quad),
                pl.BlockSpec(leave.shape, lambda s, e: (0, 0, 0)),
                pl.BlockSpec(later.shape, same),
            ],
            out_specs=[
                pl.BlockSpec((rows, width), row),
                pl.BlockSpec((8 * taps.shape[0], heads * wide), same),
                pl.BlockSpec((8, DV), same),
                pl.BlockSpec((16, 128), same),
                pl.BlockSpec(leave.shape, lambda s, e: (0, 0, 0)),
                pl.BlockSpec(later.shape, same),
            ],
            scratch_shapes=[
                pltpu.VMEM((rows + 8, heads * wide), f32),
                pltpu.VMEM((rows + 8, heads * wide), f32),
            ],
        ),
        out_shape=[
            jax.ShapeDtypeStruct((total, width), bf16),
            jax.ShapeDtypeStruct((8 * taps.shape[0], heads * wide), f32),
            jax.ShapeDtypeStruct((8, DV), f32),
            jax.ShapeDtypeStruct((16, 128), f32),
            jax.ShapeDtypeStruct(leave.shape, f32),
            jax.ShapeDtypeStruct(later.shape, f32),
        ],
        compiler_params=pltpu.CompilerParams(
            dimension_semantics=("arbitrary",), vmem_limit_bytes=56 * 1024 * 1024
        ),
        cost_estimate=pl.CostEstimate(
            flops=total * heads * 1_000_000, bytes_accessed=total * heads * 9_000, transcendentals=total * heads * 2_000
        ),
        name="mixer_backward",
    )(ends, proj, proj, before, taps, rate, shift, gain, dgated, *saved, leave, later)


FORWARD_ROWS = 512
BACKWARD_ROWS = 256
RUNS = 2


def rms_scale(values):
    return lax.rsqrt(jnp.mean(values * values, axis=-1, keepdims=True) + epsilon)


def norm_back(values, scale, gain, grad):
    u = gain * grad
    back = scale * u - values * (scale * scale * scale) * jnp.mean(values * u, axis=-1, keepdims=True)
    return back, jnp.sum(grad * (values * scale), axis=0)


def swap(x, axis, bit):
    size = lax.axis_size(axis)
    return lax.ppermute(x, axis, [(i, i ^ bit) for i in range(size)])


def exchange_roles(x):
    n = lax.axis_size("lo")
    return lax.ppermute(x, ("lo", "tensor"), [(a * n + b, b * n + a) for a in range(n) for b in range(n)])


def bits(size):
    return [1 << k for k in range(size.bit_length() - 1)]


def reversed_bits(n):
    order = [0]
    for bit in reversed(bits(n)):
        order = order + [k ^ bit for k in order]
    return order


def gather_first(x):
    return jnp.concatenate([x, swap(x, "lo", bits(lax.axis_size("lo"))[-1])], axis=0)


def gather_last(x):
    for bit in reversed(bits(lax.axis_size("lo"))[:-1]):
        x = jnp.concatenate([x, swap(x, "lo", bit)], axis=0)
    return x


def gather_rows(x):
    return gather_last(gather_first(x))


def halve(x, bit, kind):
    half = x.shape[0] // 2
    return x[:half].astype(f32) + swap(x[half:].astype(kind), "lo", bit).astype(f32)


def scatter_first(x):
    kind = x.dtype
    for bit in bits(lax.axis_size("lo"))[:-1]:
        x = halve(x, bit, kind)
    half = x.shape[0] // 2
    return x[:half], x[half:].astype(kind)


def scatter_last(kept, sent):
    return kept + swap(sent, "lo", bits(lax.axis_size("lo"))[-1]).astype(f32)


def sum_everywhere(x):
    for axis in ("lo", "tensor", "hi"):
        for bit in bits(lax.axis_size(axis)):
            x = x + swap(x, axis, bit)
    return x


def rank_of(key):
    return jnp.sum((key[..., None, :] < key[..., :, None]).astype(jnp.int32), axis=-1)


def after(x, *first):
    return lax.optimization_barrier((x, first))[0]


def widen(columns):
    return lax.all_gather(columns, ("hi", "tensor"), axis=0, tiled=True)


def narrow(columns):
    return lax.psum_scatter(columns.astype(bf16), ("hi", "tensor"), scatter_dimension=0, tiled=True)


def product(a, b, ca=1, cb=0, dtype=f32):
    return lax.dot_general(a, b, (((ca,), (cb,)), ((), ())), preferred_element_type=f32).astype(dtype)


def body(
    tokens,
    cotangent,
    lengths,
    token_order,
    token_return,
    w_mix,
    w_ba,
    conv_w,
    w_out,
    w_gate_up,
    w_down,
    gain_attn,
    gain_ffn,
    gain_out,
    decay_log,
    decay_bias,
):
    splits = lax.axis_size("lo")
    groups = lax.axis_size("hi") * splits
    me = lax.axis_index("lo")
    local_rows, model_width = tokens.shape
    group_rows = local_rows * splits
    per_peer = local_rows // groups
    weight_rows, heads, head_width = w_mix.shape
    units = w_down.shape[1]
    taps = conv_w.shape[2]
    conv_width = head_width - DV
    proj_width = heads * head_width

    spread = ("hi", "tensor")
    width = lax.axis_size("hi")
    span = jnp.arange(local_rows, dtype=jnp.int32)
    part_rows = width * per_peer

    send_rank = rank_of(token_return // group_rows * local_rows + token_return % local_rows)
    send_hot = (span[:, None] == send_rank[None, :]).astype(bf16)

    def across(rows):
        return lax.all_to_all(rows, spread, split_axis=0, concat_axis=0, tiled=True)

    def pack(rows):
        return product(send_hot, rows, dtype=bf16).reshape(groups, per_peer, -1)

    def by_part(rows):
        rows = jnp.transpose(rows.reshape(width, splits, per_peer, -1), (1, 0, 2, 3))
        return rows.reshape(local_rows, -1)

    def from_part(rows):
        rows = jnp.transpose(rows.reshape(splits, width, per_peer, model_width), (1, 0, 2, 3))
        return rows.reshape(groups, per_peer, model_width)

    def unpack(rows):
        return product(send_hot, rows.reshape(local_rows, model_width), 0, 0, bf16)

    place = token_return % local_rows
    lane = jnp.arange(128, dtype=jnp.int32)[None, :]
    digits = jnp.where(lane == 0, (place // 16)[:, None], jnp.where(lane == 1, (place % 16)[:, None], 0))
    tagged = jnp.concatenate([tokens, digits.astype(bf16)], axis=1)
    arrived = across(pack(tagged))
    run_parts = splits // RUNS
    run_rows = run_parts * local_rows

    def in_parts(rows):
        rows = rows.reshape(splits, run_parts, part_rows, -1)
        return jnp.transpose(rows, (1, 0, 2, 3)).reshape(run_parts, local_rows, -1)

    def order_of(tags):
        tags = in_parts(tags)[:, :, :2].astype(jnp.int32)
        at = tags[:, :, 0] * 16 + tags[:, :, 1]
        return (at[:, None, :] == span[None, :, None]).astype(bf16)

    def to_sequence(order, rows):
        return lax.dot_general(
            order, in_parts(rows), (((2,), (1,)), ((0,), (0,))), preferred_element_type=f32
        ).astype(bf16).reshape(run_rows, -1)

    def from_sequence(order, rows):
        rows = lax.dot_general(
            order, rows.reshape(run_parts, local_rows, -1), (((1,), (1,)), ((0,), (0,))),
            preferred_element_type=f32,
        ).astype(bf16).reshape(run_parts, splits, part_rows, -1)
        return jnp.transpose(rows, (1, 0, 2, 3)).reshape(run_rows, -1)

    head_start = me * heads
    lanes = jnp.zeros((1, 128), f32)
    rate_row = lanes.at[0, 1 : 2 * heads : 2].set(lax.dynamic_slice_in_dim(decay_log, head_start, heads))
    shift_row = lanes.at[0, 1 : 2 * heads : 2].set(lax.dynamic_slice_in_dim(decay_bias, head_start, heads))
    own_lengths = exchange_roles(lengths)
    ends = jnp.sum(jnp.where(jnp.tri(SEQS, dtype=bool), own_lengths, 0), axis=1).astype(jnp.int32)
    small_at = proj_width
    conv_at = small_at + heads * w_ba.shape[2]
    spare = 128 - heads * w_ba.shape[2] - taps
    mix_own = exchange_roles(
        jnp.concatenate(
            [
                w_mix.reshape(weight_rows, proj_width).astype(bf16),
                w_ba.reshape(weight_rows, -1).astype(bf16),
                conv_w.reshape(weight_rows, taps).astype(bf16),
                jnp.zeros((weight_rows, spare), bf16),
                w_out.reshape(weight_rows, heads * DV).astype(bf16),
            ],
            axis=1,
        )
    )
    mix_all = widen(mix_own)
    arrived = by_part(after(arrived, ends, rate_row, shift_row))
    packed_in, tags = arrived[:, :model_width], arrived[:, model_width:]
    runs = range(RUNS)
    own_rows = local_rows // RUNS

    def split(rows):
        return [rows[r * own_rows : (r + 1) * own_rows] for r in runs]

    input_f32 = packed_in.astype(f32)
    input_scale = rms_scale(input_f32)
    input_runs = split(input_f32)
    normed_runs = split(jnp.concatenate([(input_f32 * input_scale * gain_attn).astype(bf16), tags], axis=1))
    gathered_0 = gather_rows(normed_runs[0])
    ffn_sent = jnp.concatenate(
        [w_gate_up.reshape(weight_rows, 2 * units).astype(bf16), w_down.astype(bf16)], axis=1
    )
    out_all = mix_all[:, small_at + 128 :]
    mix_all = mix_all[:, : small_at + 128]

    conv_all = mix_all[:, conv_at : conv_at + taps].reshape(-1, heads, taps).astype(f32)
    tap_rows = jnp.transpose(conv_all, (2, 1, 0)).reshape(taps, heads * conv_width)
    gain_row = gain_out[None]
    constants = (tap_rows, rate_row, shift_row, gain_row)

    state = jnp.zeros((heads, DK, DV), f32)

    def ahead(r):
        return (projected[r - 1], run_rows // 8 - 1) if r else (projected[r], 0)

    def mix_forward(r, state):
        return mixer_forward(
            ends, projected[r], *ahead(r), *constants, state, heads=heads, rows=FORWARD_ROWS, start=r * run_rows
        )

    def feed_forward(r, normed_mid):
        place = (r * run_parts + jnp.arange(run_parts, dtype=jnp.int32))[:, None, None] * local_rows
        alive = (place + span[None, :, None] < ends[SEQS - 1]).astype(bf16)
        live = from_sequence(orders[r], jnp.broadcast_to(alive, (run_parts, local_rows, 128)))[:, :1].astype(f32)
        grad_hidden = product(grad_all[r], w_last) * live
        gate_up = product(normed_mid, w_pair)
        gate, up = gate_up[:, :units], gate_up[:, units:]
        s = sigmoid(gate)
        hidden = (gate * s * up * live).astype(bf16)
        grad_pair = jnp.concatenate(
            [grad_hidden * up * (s * (1.0 + gate * (1.0 - s))), grad_hidden * (gate * s)], axis=1
        ).astype(bf16)
        return hidden, grad_pair, product(grad_pair, w_pair, 1, 1, bf16)

    def normed_of(middle):
        scale = rms_scale(middle)
        return scale, (middle * scale * gain_ffn).astype(bf16)

    constants = (tap_rows, rate_row, shift_row, gain_row)
    orders = [order_of(gathered_0[:, model_width:])]
    seq_0 = to_sequence(orders[0], gathered_0[:, :model_width])
    cotangent, mix_all = lax.optimization_barrier((cotangent, mix_all))
    packed_grad = across(pack(cotangent))
    projected = [product(seq_0, mix_all)]
    gathered_1 = gather_rows(normed_runs[1])
    orders.append(order_of(gathered_1[:, model_width:]))
    seq_1 = to_sequence(orders[1], gathered_1[:, :model_width])
    ffn_own = exchange_roles(after(ffn_sent, gathered_1))
    projected[0], seq_1, ffn_own, packed_grad = lax.optimization_barrier(
        (projected[0], seq_1, ffn_own, by_part(packed_grad))
    )
    ffn_all = widen(ffn_own)
    *saved_0, state = mix_forward(0, state)
    crossed = swap(packed_grad, "lo", bits(splits)[-1])
    saved_0, crossed = lax.optimization_barrier((saved_0, crossed))
    grad_runs = split(packed_grad)
    terms_0 = product(from_sequence(orders[0], saved_0[0]), out_all, 1, 1)
    projected.append(product(after(seq_1, terms_0), mix_all))
    kept_0, sent_0 = scatter_first(terms_0)
    projected[1], kept_0, sent_0 = lax.optimization_barrier((projected[1], kept_0, sent_0))
    grad_all = [gather_last(jnp.concatenate(x, axis=0)) for x in zip(grad_runs, split(crossed))]
    *saved_1, state = mix_forward(1, state)
    middle_0 = input_runs[0] + after(scatter_last(kept_0, sent_0), saved_1[0])
    scale_0, normed_mid_0 = normed_of(middle_0)
    terms_1 = product(from_sequence(orders[1], saved_1[0]), out_all, 1, 1)
    first_0 = gather_first(normed_mid_0)
    kept_1, sent_1 = scatter_first(terms_1)
    kept_1, sent_1, first_0, ffn_all = lax.optimization_barrier((kept_1, sent_1, first_0, ffn_all))
    w_pair, w_last = ffn_all[:, : 2 * units], ffn_all[:, 2 * units :]
    normed_mid_0 = gather_last(first_0)

    hidden_0, pair_0, grad_terms_0 = feed_forward(0, normed_mid_0)
    middle_1 = input_runs[1] + after(scatter_last(kept_1, sent_1), grad_terms_0)
    scale_1, normed_mid_1 = normed_of(middle_1)
    first_1 = gather_first(normed_mid_1)
    grad_kept_0, grad_sent_0 = scatter_first(grad_terms_0)
    grad_kept_0, grad_sent_0, first_1 = lax.optimization_barrier((grad_kept_0, grad_sent_0, first_1))
    normed_mid_1 = gather_last(first_1)
    hidden_1, pair_1, grad_terms_1 = feed_forward(1, normed_mid_1)
    grad_kept_1, grad_sent_1 = scatter_first(grad_terms_1)
    grad_kept_1, grad_sent_1, grad_terms_0_sum = lax.optimization_barrier(
        (grad_kept_1, grad_sent_1, scatter_last(grad_kept_0, grad_sent_0))
    )
    hidden_0, pair_0, hidden_1, pair_1 = after((hidden_0, pair_0, hidden_1, pair_1), grad_sent_1)
    grad_pairs = product(normed_mid_0, pair_0, 0, 0) + product(normed_mid_1, pair_1, 0, 0)
    grad_terms_1_sum = after(scatter_last(grad_kept_1, grad_sent_1), grad_pairs)
    back_1, gain_1 = norm_back(middle_1, scale_1, gain_ffn, grad_terms_1_sum)
    grad_middle_1 = grad_runs[1].astype(f32) + back_1
    first_1 = gather_first(grad_middle_1.astype(bf16))
    hidden_0, hidden_1 = after((hidden_0, hidden_1), grad_middle_1)
    grad_last = product(grad_all[0], hidden_0, 0, 0) + product(grad_all[1], hidden_1, 0, 0)
    layer_terms = [product(h, w_last, 1, 1, bf16) for h in (hidden_0, hidden_1)]
    back_0, gain_0 = norm_back(middle_0, scale_0, gain_ffn, after(grad_terms_0_sum, grad_middle_1))
    grad_gain_ffn = gain_0 + gain_1
    grad_middle_0 = grad_runs[0].astype(f32) + back_0
    first_1, grad_last, layer_terms, grad_low_0 = lax.optimization_barrier(
        (first_1, grad_last, layer_terms, grad_middle_0.astype(bf16))
    )
    grad_mid_seq_1 = to_sequence(orders[1], gather_last(first_1))
    grad_ffn = narrow(jnp.concatenate([grad_pairs.astype(bf16), grad_last.astype(bf16)], axis=1))

    def mix_backward(r, grad_gated, saved, leave, later):
        return mixer_backward(
            ends, projected[r], *ahead(r), *constants, grad_gated, saved[1:], leave, later,
            heads=heads, rows=BACKWARD_ROWS, start=r * run_rows,
        )

    leave = jnp.zeros((heads, DK, DV), f32)
    later = jnp.zeros((8, heads * conv_width), f32)
    layer_parts = [scatter_first(x) for x in layer_terms]
    grad_gated_1 = product(grad_mid_seq_1, out_all)
    grad_gated_1, grad_low_0, layer_parts = lax.optimization_barrier((grad_gated_1, grad_low_0, layer_parts))
    grad_proj_1, *sums_1, leave, later = mix_backward(1, grad_gated_1, saved_1, leave, later)
    layer_sums = [scatter_last(*x) for x in layer_parts]
    grad_proj_1, first_0, layer_sums = lax.optimization_barrier((grad_proj_1, gather_first(grad_low_0), layer_sums))
    grad_mid_seq_0 = to_sequence(orders[0], gather_last(first_0))
    grad_gated_0 = product(grad_mid_seq_0, out_all)
    layer_rows = jnp.concatenate([m + x for m, x in zip((middle_0, middle_1), layer_sums)], axis=0)
    layer_rows = from_part(layer_rows.astype(bf16))
    grad_gated_0, layer_rows = lax.optimization_barrier((grad_gated_0, layer_rows))
    grad_proj_0, *sums_0, leave, later = mix_backward(0, grad_gated_0, saved_0, leave, later)
    grad_proj_0, grad_ffn, layer_back = lax.optimization_barrier((grad_proj_0, grad_ffn, across(layer_rows)))
    grad_taps, grad_gain_out, grad_decay = [a + b for a, b in zip(sums_0, sums_1)]
    grad_conv = jnp.sum(grad_taps.reshape(taps, 8, heads, conv_width), axis=1)
    grad_conv = jnp.transpose(grad_conv, (2, 1, 0)).reshape(-1, taps)
    grad_mix = product(seq_0, grad_proj_0, 0, 0) + product(seq_1, grad_proj_1, 0, 0)
    grad_mix = (grad_mix + jnp.pad(grad_conv, ((0, 0), (conv_at, spare)))).astype(bf16)
    grad_out_w = product(grad_mid_seq_0, saved_0[0], 0, 0) + product(grad_mid_seq_1, saved_1[0], 0, 0)
    grad_mix = jnp.concatenate([grad_mix, grad_out_w.astype(bf16)], axis=1)
    grad_mix, *proj_parts = lax.optimization_barrier((grad_mix, grad_proj_0, grad_proj_1))
    normed_terms = [from_sequence(orders[r], product(proj_parts[r], mix_all, 1, 1, bf16)) for r in runs]
    grad_mix = exchange_roles(narrow(grad_mix)).astype(f32)
    normed_terms = [x.reshape(splits, own_rows, model_width) for x in normed_terms]
    normed_terms = jnp.concatenate(normed_terms, axis=1).reshape(group_rows, model_width)
    grad_normed = scatter_last(*scatter_first(normed_terms))
    grad_normed, grad_ffn = lax.optimization_barrier((grad_normed, exchange_roles(grad_ffn)))
    grad_ffn = grad_ffn.astype(f32)
    grad_input_norm, grad_gain_attn = norm_back(input_f32, input_scale, gain_attn, grad_normed)
    grad_middle = jnp.concatenate([grad_middle_0, grad_middle_1], axis=0)
    input_grad = unpack(across(from_part((grad_middle + grad_input_norm).astype(bf16))))
    layer_out = unpack(layer_back)

    head_total = decay_log.shape[0]
    decay_sums = jnp.sum(grad_decay.reshape(2, 8, 128), axis=1)[:, 1 : 2 * heads : 2]
    decay_full = lax.dynamic_update_slice(jnp.zeros((2, head_total), f32), decay_sums, (0, head_start))
    flat = jnp.concatenate(
        [grad_gain_attn, grad_gain_ffn, jnp.sum(grad_gain_out, axis=0), decay_full.reshape(-1)]
    )
    flat = sum_everywhere(jnp.pad(flat, (0, -flat.shape[0] % 1024)).reshape(8, -1)).reshape(-1)
    at = 0
    sums = []
    for size in (model_width, model_width, gain_out.shape[0], head_total, head_total):
        sums.append(flat[at : at + size])
        at += size
    return (
        layer_out,
        input_grad,
        grad_mix[:, :small_at].reshape(w_mix.shape),
        grad_mix[:, small_at:conv_at].reshape(w_ba.shape),
        grad_mix[:, conv_at : conv_at + taps].reshape(conv_w.shape),
        grad_mix[:, small_at + 128 :].reshape(w_out.shape),
        grad_ffn[:, : 2 * units].reshape(w_gate_up.shape),
        grad_ffn[:, 2 * units :],
        *sums,
    )


def solution(mesh):
    dp, splits = mesh.shape["dp"], mesh.shape["tensor"]
    roles = Mesh(mesh.devices.reshape(dp // splits, splits, splits), ("hi", "lo", "tensor"))
    group = ("hi", "lo")
    rows = P((*group, "tensor"))
    by_head = P(group, "tensor", None)
    by_unit = (P(group, None, "tensor"), P(group, "tensor"))
    return jax.shard_map(
        body,
        mesh=roles,
        in_specs=(rows, rows, P(group), rows, rows, by_head, by_head, by_head, by_head, *by_unit)
        + (P(),) * 5,
        out_specs=(rows, rows, by_head, by_head, by_head, by_head, *by_unit) + (P(),) * 5,
        check_vma=False,
    )
```
